32 devices in a mesh: req: 4 (over z), tok: 8 (over y, x, core).
Axes of the slice: x: 2, y: 2, z: 4, core: 2. Of those that a mesh axis runs over, the one named last changes fastest.
Arguments:
- hidden_in: bfloat16 [4096, 2048], P(('req', 'tok')), may hold values from -1.5 to 1.5
- suffix_len: int32 [4, 4], P('req'), may hold values from 1 to 512, 1024 in all within a row
- prefix_of: int32 [4, 4], P('req'), may hold values from 0 to 3
- prefix_slot: int32 [4], replicated, may hold values from 0 to 3, each once
- prefix_cache: bfloat16 [4, 4, 2048, 128], P('req', None, 'tok'), may hold values from -160 to 160
- attn_gain: bfloat16 [2048], replicated, may hold values from 0.099609375 to 1.8984375
- query_weight: bfloat16 [2048, 2048], P(None, 'tok'), may hold values from -0.125 to 0.125
- keyval_weight: bfloat16 [4, 2048, 128], replicated, may hold values from -0.125 to 0.125
- out_weight: bfloat16 [2048, 2048], P('tok'), may hold values from -0.125 to 0.125
- mlp_gain: bfloat16 [2048], replicated, may hold values from 0.099609375 to 1.8984375
- gate_weight: bfloat16 [2048, 4096], P(None, 'req'), may hold values from -0.125 to 0.125
- up_weight: bfloat16 [2048, 4096], P(None, 'req'), may hold values from -0.125 to 0.125
- down_weight: bfloat16 [4096, 2048], P('req'), may hold values from -0.09375 to 0.09375
- final_gain: bfloat16 [2048], replicated, may hold values from 0.099609375 to 1.8984375
- head_weight: bfloat16 [32000, 2048], P('tok'), may hold values from -7 to 7
Outputs:
- hidden_out: bfloat16 [4096, 2048], P(('req', 'tok'))
- suffix_cache: bfloat16 [4096, 512], P('req', 'tok')
- last_rms: float32 [4, 4], P('req')
- top_logit: float32 [4, 4], P('req')
- log_total: float32 [4, 4], P('req')
The draws below stay inside these ranges and needn't reach their ends.
Inputs may be any that keep to these rules, and one draw needn't show every extreme that they name: `suffix_len`: each owner's 4 lengths sum to 1024, and the largest of each owner is 512.
All inputs are finite; a program needn't handle non-finite values.
Results may differ from the reference program's by a relative error of at most 0.02.
Values may be sent and summed in bfloat16 or wider, within the bound.
A program may use at most 128 MiB of HBM per device.

```python
import math
import jax
import jax.numpy as jnp
import numpy as np
from jax import lax

D = 2048
HEADS = 32
KVH = 4
HD = 64
FF = 4096
VOCAB = 32000
WINDOW = 2048
PRE_LEN = 16384
REQ_DEV = 4
OWNERS = 4
PREFIXES = 4
OWN_TOK = 1024
TOKENS = 4096
MOST = 512


def draw_prefix_cache(key, part):
    entry_key = jax.random.fold_in(key, 0)
    shape_all = (PREFIXES, KVH, WINDOW, 2 * HD)
    drawn = jnp.clip(jax.random.normal(entry_key, shape_all, jnp.float32), -4.0, 4.0)
    return drawn.astype(jnp.bfloat16)


def draw_head_weight(key, part):
    row_key, entry_key = jax.random.split(key)
    vocab_rows = jnp.arange(VOCAB)
    trend = 3.0 - 2.0 * vocab_rows.astype(jnp.float32) / VOCAB
    rough = jnp.exp(jax.random.uniform(row_key, (VOCAB, 1), jnp.float32, -1.15, 1.15))
    row_scale = 1.0 / math.sqrt(D) * trend[:, None] * rough
    drawn = jnp.clip(jax.random.normal(entry_key, (VOCAB, D), jnp.float32), -4.0, 4.0) * row_scale
    return jnp.clip(drawn, -7.0, 7.0).astype(jnp.bfloat16)


def set_ends(result, stream_key, smallest, top_value):
    spot = [jax.random.randint(jax.random.fold_in(stream_key, axis), (), 0, length) for axis, length in enumerate(result.shape)]
    main_axis = result.shape.index(max(result.shape))
    neighbour = spot[:main_axis] + [(spot[main_axis] + 1) % result.shape[main_axis]] + spot[main_axis + 1:]
    return result.at[tuple(spot)].set(smallest).at[tuple(neighbour)].set(top_value)


def level_of(rng, shape, shards, least, top_value):
    gain = 1.0
    for dim, parts in shards:
        steps = jax.random.uniform(jax.random.fold_in(jax.random.fold_in(rng, 6), dim), (parts,), jnp.float32, least / len(shards), top_value / len(shards))
        gain = gain * jnp.repeat(jnp.exp(steps), shape[dim] // parts).reshape((-1,) + (1,) * (len(shape) - 1 - dim))
    return gain


def rank_bounds(number_of, slope):
    weights = [(1 << 20) // math.isqrt(grade ** slope) + 1 for grade in range(1, number_of + 1)]
    scale = 1 + sum(weights) // (1 << 30)
    return np.cumsum(np.array([max(1, weight // scale) for weight in weights]))


def ranked_ids(own_key, extent, count, lean):
    table = rank_bounds(count, lean)
    ticket = jax.random.randint(jax.random.fold_in(own_key, 1), extent, 0, int(table[count - 1]))
    rank = jnp.searchsorted(jnp.asarray(table, jnp.int32), ticket, side="right")
    return jax.random.permutation(jax.random.fold_in(own_key, 2), count)[rank].astype(jnp.int32)


def profile(amount, total, limit, lean):
    loads = [(1 << 20) // math.isqrt(standing ** lean) + 1 for standing in range(2, amount + 1)]
    spare, holding = total - limit - (amount - 1), [1] * (amount - 1)
    while spare > 0:
        movable = [i for i in range(amount - 1) if holding[i] < limit]
        mass, left = sum([loads[i] for i in movable]), spare
        for i in movable:
            addition = min(limit - holding[i], max(1, left * loads[i] // mass), spare)
            holding[i] = holding[i] + addition
            spare = spare - addition
    return np.array([limit] + holding)


def ragged(stream_key, count, total, limit, slope):
    if count == 2:
        one = jax.random.randint(stream_key, (), max(1, total - limit), min(limit, total - 1) + 1)
        return jnp.stack([one, total - one])
    tallies = jnp.asarray(profile(count, total, limit, slope), jnp.int32)
    couples = (count - 1) // 2
    source_of, receiver = tallies[1:1 + 2 * couples:2], tallies[2:2 + 2 * couples:2]
    margin = jnp.minimum(source_of - 1, limit - receiver)
    moved = jax.random.randint(jax.random.fold_in(stream_key, 1), (couples,), 0, 1 << 20) % (margin + 1)
    tallies = tallies.at[1:1 + 2 * couples:2].set(source_of - moved).at[2:2 + 2 * couples:2].set(receiver + moved)
    return tallies[jax.random.permutation(jax.random.fold_in(stream_key, 2), count)]


def centred(rng, shape, scale, limit, shards=(), kind=jnp.bfloat16):
    level = level_of(rng, shape, shards, -0.22, 0.18) if shards else 1.0
    values = jax.random.normal(rng, shape, jnp.float32) * scale * level
    return jnp.minimum(jnp.maximum(values, -limit), limit).astype(kind)


def setup_inputs(seed: int = 0) -> dict:
    keys = jax.random.split(jax.random.key(seed), 16)
    hidden_in = centred(keys[0], (TOKENS, D), 0.25, 1.5, ((0, 32),))
    suffix_len = jax.vmap(lambda own: ragged(own, REQ_DEV, OWN_TOK, MOST, 2))(jax.random.split(keys[1], OWNERS)).reshape((OWNERS, REQ_DEV)).astype(jnp.int32)
    prefix_of = set_ends(ranked_ids(keys[2], (OWNERS, REQ_DEV), PREFIXES, 2), jax.random.fold_in(keys[2], 3), 0, PREFIXES - 1).astype(jnp.int32)
    prefix_slot = jax.random.permutation(keys[3], PREFIXES).astype(jnp.int32)
    prefix_cache = draw_prefix_cache(jax.random.fold_in(keys[15], 71), 0)
    attn_gain = jnp.clip(1.0 + 0.18 * jax.random.normal(keys[5], (D,), jnp.float32), 0.099609375, 1.8984375).astype(jnp.bfloat16)
    query_weight = centred(keys[6], (D, HEADS * HD), D ** -0.5, 0.125, ((1, 8),))
    keyval_weight = centred(keys[7], (KVH, D, 2 * HD), D ** -0.5, 0.125)
    out_weight = centred(keys[8], (HEADS * HD, D), (HEADS * HD) ** -0.5, 0.125, ((0, 8),))
    mlp_gain = jnp.clip(1.0 + 0.18 * jax.random.normal(keys[9], (D,), jnp.float32), 0.099609375, 1.8984375).astype(jnp.bfloat16)
    gate_weight = centred(keys[10], (D, FF), D ** -0.5, 0.125, ((1, 4),))
    up_weight = centred(keys[11], (D, FF), D ** -0.5, 0.125, ((1, 4),))
    down_weight = centred(keys[12], (FF, D), FF ** -0.5, 0.09375, ((0, 4),))
    final_gain = jnp.clip(1.0 + 0.18 * jax.random.normal(keys[13], (D,), jnp.float32), 0.099609375, 1.8984375).astype(jnp.bfloat16)
    head_weight = draw_head_weight(jax.random.fold_in(keys[15], 71), 0)
    return dict(hidden_in=hidden_in, suffix_len=suffix_len, prefix_of=prefix_of, prefix_slot=prefix_slot, prefix_cache=prefix_cache, attn_gain=attn_gain, query_weight=query_weight, keyval_weight=keyval_weight, out_weight=out_weight, mlp_gain=mlp_gain, gate_weight=gate_weight, up_weight=up_weight, down_weight=down_weight, final_gain=final_gain, head_weight=head_weight)


epsilon = 1e-05
neg_large = -1e+30

def rms_scale(values, gain_vec):
    widened = values.astype(jnp.float32)
    mean_square = lax.optimization_barrier(jnp.mean(widened * widened, axis=-1, keepdims=True))
    return widened * lax.rsqrt(mean_square + epsilon) * gain_vec.astype(jnp.float32)

def rotate(vectors, positions):
    half_width = vectors.shape[-1] // 2
    levels = jnp.arange(half_width).astype(jnp.float32)
    inverse = jnp.exp(levels * (-2.0 * math.log(10000.0) / vectors.shape[-1]))
    angles = positions.astype(jnp.float32)[:, None] * inverse[None, :]
    cosine = jnp.cos(angles)[:, None, :]
    sine_part = jnp.sin(angles)[:, None, :]
    first_half = vectors[..., :half_width]
    second_half = vectors[..., half_width:]
    return jnp.concatenate([first_half * cosine - second_half * sine_part, second_half * cosine + first_half * sine_part], axis=-1)

def owner_layout(lengths, row_count):
    lengths = lengths.astype(jnp.int32)
    end_rows = jnp.cumsum(lengths).astype(jnp.int32)
    starts = (end_rows - lengths).astype(jnp.int32)
    row_index = jnp.arange(row_count).astype(jnp.int32)
    member = (row_index[:, None] >= starts[None, :]) & (row_index[:, None] < end_rows[None, :])
    offsets = (row_index - lax.optimization_barrier(jnp.sum(jnp.where(member, starts[None, :], 0), axis=1))).astype(jnp.int32)
    return (starts, end_rows, offsets)

def slot_lookup(chosen, prefix_slot):
    table_index = jnp.arange(prefix_slot.shape[0]).astype(jnp.int32)
    hits = chosen.astype(jnp.int32)[:, None] == table_index[None, :]
    return lax.optimization_barrier(jnp.sum(jnp.where(hits, prefix_slot.astype(jnp.int32)[None, :], 0), axis=1)).astype(jnp.int32)

def request_attention(query_block, suffix_block, window, live_len):
    row_count = query_block.shape[0]
    head_width = query_block.shape[-1]
    window_len = window.shape[1]
    suffix_major = jnp.transpose(suffix_block, (1, 0, 2))
    key_rows = jnp.concatenate([window[:, :, :head_width], suffix_major[:, :, :head_width]], axis=1)
    value_rows = jnp.concatenate([window[:, :, head_width:], suffix_major[:, :, head_width:]], axis=1)
    scores = jnp.einsum('rgke,gse->gkrs', query_block.astype(jnp.float32), key_rows.astype(jnp.float32)) * head_width ** (-0.5)
    row_index = jnp.arange(row_count).astype(jnp.int32)
    prefix_seen = jnp.arange(window_len).astype(jnp.int32)[None, :] > row_index[:, None]
    suffix_seen = (row_index[None, :] <= row_index[:, None]) & (row_index[:, None] - row_index[None, :] < window_len) & (row_index[None, :] < live_len)
    visible = jnp.concatenate([prefix_seen, suffix_seen], axis=1)
    masked = jnp.where(visible, scores, neg_large)
    highest = lax.optimization_barrier(jnp.max(masked, axis=-1, keepdims=True))
    weights = jnp.where(visible, jnp.exp(masked - highest), 0.0)
    totals = lax.optimization_barrier(jnp.sum(weights, axis=-1, keepdims=True))
    totals = jnp.where(row_index[:, None] < live_len, totals, 1.0)
    rounded = lax.optimization_barrier(weights.astype(jnp.bfloat16))
    mixed_rows = jnp.einsum('gkrs,gse->rgke', rounded.astype(jnp.float32), value_rows.astype(jnp.float32))
    mixed_rows = mixed_rows / jnp.transpose(totals, (2, 0, 1, 3))
    return mixed_rows.reshape(row_count, -1).astype(jnp.bfloat16)

def reference(hidden_in, suffix_len, prefix_of, prefix_slot, prefix_cache, attn_gain, query_weight, keyval_weight, out_weight, mlp_gain, gate_weight, up_weight, down_weight, final_gain, head_weight):
    owners = suffix_len.shape[0]
    own_rows = hidden_in.shape[0] // owners
    most_rows = own_rows // 2
    heads_per_kv = HEADS // KVH

    def one_owner(packed):
        inputs, lengths, chosen = packed
        lengths = lengths.astype(jnp.int32)
        starts, end_rows, offsets = owner_layout(lengths, own_rows)
        positions = offsets + PRE_LEN
        normed = rms_scale(inputs, attn_gain).astype(jnp.bfloat16)
        queries = jnp.dot(normed, query_weight, preferred_element_type=jnp.float32).reshape(own_rows, HEADS, HD)
        queries = rotate(queries, positions).astype(jnp.bfloat16)
        keyvals = jnp.einsum('td,gde->tge', normed.astype(jnp.float32), keyval_weight.astype(jnp.float32))
        rotated = rotate(keyvals[:, :, :HD], positions)
        keyvals = jnp.concatenate([rotated, keyvals[:, :, HD:]], axis=-1).astype(jnp.bfloat16)
        padded_queries = jnp.concatenate([queries, jnp.zeros((most_rows, HEADS, HD), jnp.bfloat16)], axis=0)
        padded_keyvals = jnp.concatenate([keyvals, jnp.zeros((most_rows, KVH, 2 * HD), jnp.bfloat16)], axis=0)
        cache_rows = slot_lookup(chosen, prefix_slot)

        def one_request(buffer, request):
            first_row, live_len, cache_row = request
            query_block = lax.dynamic_slice_in_dim(padded_queries, first_row, most_rows, 0).reshape(most_rows, KVH, heads_per_kv, HD)
            suffix_block = lax.dynamic_slice_in_dim(padded_keyvals, first_row, most_rows, 0)
            window = lax.dynamic_index_in_dim(prefix_cache, cache_row, 0, keepdims=False)
            mixed_rows = request_attention(query_block, suffix_block, window, live_len)
            current = lax.dynamic_slice_in_dim(buffer, first_row, most_rows, 0)
            keep_rows = jnp.arange(most_rows).astype(jnp.int32)[:, None] < live_len
            return (lax.dynamic_update_slice_in_dim(buffer, jnp.where(keep_rows, mixed_rows, current), first_row, 0), None)
        buffer = jnp.zeros((own_rows + most_rows, HEADS * HD), jnp.bfloat16)
        buffer, unused = lax.scan(one_request, buffer, (starts, lengths, cache_rows))
        attended = buffer[:own_rows]
        middle = (inputs.astype(jnp.float32) + jnp.dot(attended, out_weight, preferred_element_type=jnp.float32)).astype(jnp.bfloat16)
        mlp_in = rms_scale(middle, mlp_gain).astype(jnp.bfloat16)
        gate_proj = jnp.dot(mlp_in, gate_weight, preferred_element_type=jnp.float32)
        lifted = jnp.dot(mlp_in, up_weight, preferred_element_type=jnp.float32)
        hidden_act = (jax.nn.silu(gate_proj) * lifted).astype(jnp.bfloat16)
        final_state = (middle.astype(jnp.float32) + jnp.dot(hidden_act, down_weight, preferred_element_type=jnp.float32)).astype(jnp.bfloat16)
        last_rows = final_state[end_rows - 1].astype(jnp.float32)
        mean_square = lax.optimization_barrier(jnp.mean(last_rows * last_rows, axis=-1, keepdims=True))
        spread = jnp.sqrt(mean_square + epsilon)
        final_normed = (last_rows * lax.rsqrt(mean_square + epsilon) * final_gain.astype(jnp.float32)).astype(jnp.bfloat16)
        logits = lax.dot_general(final_normed, head_weight, (((1,), (1,)), ((), ())), preferred_element_type=jnp.float32)
        highest = lax.optimization_barrier(jnp.max(logits, axis=-1))
        log_total = highest + jnp.log(lax.optimization_barrier(jnp.sum(jnp.exp(logits - highest[:, None]), axis=-1)))
        return (final_state, keyvals.reshape(own_rows, KVH * 2 * HD), spread[:, 0], highest, log_total)
    results = lax.map(one_owner, (hidden_in.reshape(owners, own_rows, hidden_in.shape[1]), suffix_len, prefix_of))
    hidden_out = results[0].reshape(owners * own_rows, hidden_in.shape[1])
    suffix_cache = results[1].reshape(owners * own_rows, KVH * 2 * HD)
    return (hidden_out, suffix_cache, results[2], results[3], results[4])
```

```python
import math

import jax
import jax.numpy as jnp
from jax import lax
from jax.experimental import pallas as pl
from jax.experimental.pallas import tpu as pltpu
from jax.sharding import PartitionSpec as P

HD = 64
PRE_LEN = 16384


epsilon = 1e-05
neg_large = -1e30


def rms_scale(values, gain_vec):
    widened = values.astype(jnp.float32)
    mean_square = jnp.mean(widened * widened, axis=-1, keepdims=True)
    return widened * lax.rsqrt(mean_square + epsilon) * gain_vec.astype(jnp.float32)


def owner_layout(lengths, row_count):
    place = jnp.arange(lengths.shape[0])
    end_rows = jnp.sum(jnp.where(place[None, :] <= place[:, None], lengths[None, :], 0), axis=1)
    starts = end_rows - lengths
    row_index = jnp.arange(row_count)
    member = (row_index[:, None] >= starts[None, :]) & (row_index[:, None] < end_rows[None, :])
    offsets = row_index - jnp.sum(jnp.where(member, starts[None, :], 0), axis=1)
    return (starts, end_rows, offsets)


def slot_lookup(chosen, prefix_slot):
    table_index = jnp.arange(prefix_slot.shape[0])
    hits = chosen[:, None] == table_index[None, :]
    return jnp.sum(jnp.where(hits, prefix_slot[None, :], 0), axis=1)


def attention_kernel(
    member_count,
    heads,
    piece,
    most_rows,
    window_len,
    chunk,
    suffix_chunk,
    scalars,
    q_ref,
    cos_ref,
    sin_ref,
    *refs,
):
    windows = refs[:member_count]
    suffix_ref, out_ref, query_scr, high_scr, total_scr, acc_scr, result_scr = refs[member_count:]
    requests = 4
    rows = q_ref.shape[1]
    half = HD // 2
    width = heads * rows
    member = scalars[3 * requests]
    tile = pl.program_id(0)
    first_row = (tile * member_count + member) * rows
    cosine = cos_ref[...]
    sine = sin_ref[...]
    for head in range(heads):
        low = q_ref[head * HD : head * HD + half, :]
        high = q_ref[head * HD + half : (head + 1) * HD, :]
        cols = pl.ds(head * rows, rows)
        turned = jnp.concatenate(
            [
                low * cosine - high * sine,
                high * cosine + low * sine,
                jnp.zeros((HD, rows), jnp.float32),
            ],
            axis=0,
        )
        query_scr[:, cols] = (turned * (HD**-0.5 * math.log2(math.e))).astype(jnp.bfloat16)

    def absorb(keyvals, row_of_key, visible_fn):
        scores = jnp.dot(keyvals, query_scr[...], preferred_element_type=jnp.float32)
        if visible_fn is not None:
            scores = jnp.where(visible_fn(scores.shape), scores, neg_large)
        before = high_scr[...]
        after = jnp.maximum(before, jnp.max(scores, axis=0, keepdims=True))
        weights = jnp.exp2(scores - after)
        fade = jnp.exp2(before - after)
        total_scr[...] = total_scr[...] * fade + jnp.sum(weights, axis=0, keepdims=True)
        mixed = lax.dot_general(
            keyvals,
            weights.astype(jnp.bfloat16),
            (((0,), (0,)), ((), ())),
            preferred_element_type=jnp.float32,
        )
        acc_scr[...] = acc_scr[...] * fade + mixed[HD:, :]
        high_scr[...] = after

    lane_row = first_row + lax.broadcasted_iota(jnp.int32, (1, width), 1) % rows

    def one_request(request, carry):
        start = scalars[request]
        end = scalars[requests + request]
        slot = scalars[2 * requests + request]

        @pl.when((start < first_row + rows) & (end > first_row))
        def _():
            high_scr[...] = jnp.full(high_scr.shape, neg_large, jnp.float32)
            total_scr[...] = jnp.zeros(total_scr.shape, jnp.float32)
            acc_scr[...] = jnp.zeros(acc_scr.shape, jnp.float32)
            offset = lane_row - start
            local_len = windows[0].shape[1]
            for first in reversed(range(0, local_len, chunk)):
                for shift in range(member_count):
                    part = lax.rem(member + shift, member_count)

                    def prefix_seen(shape, first=first, part=part):
                        index = first + lax.broadcasted_iota(jnp.int32, (shape[0], 1), 0)
                        position = (index // piece * member_count + part) * piece + index % piece
                        return position > offset

                    masked = first // piece * member_count * piece < most_rows
                    absorb(
                        windows[shift][slot, first : first + chunk, :],
                        None,
                        prefix_seen if masked else None,
                    )

            def suffix_step(step, inner):
                base = pl.multiple_of(step * suffix_chunk, suffix_chunk)

                def suffix_seen(shape):
                    key_row = base + lax.broadcasted_iota(jnp.int32, (shape[0], 1), 0)
                    return (
                        (key_row >= start)
                        & (key_row <= lane_row)
                        & (lane_row - key_row < window_len)
                    )

                absorb(suffix_ref[pl.ds(base, suffix_chunk), :], None, suffix_seen)
                return inner

            lax.fori_loop(
                start // suffix_chunk,
                (jnp.minimum(first_row + rows, end) - 1) // suffix_chunk + 1,
                suffix_step,
                0,
            )
            mine = (lane_row >= start) & (lane_row < end)
            result_scr[...] = jnp.where(mine, acc_scr[...] / total_scr[...], result_scr[...])

        return carry

    lax.fori_loop(0, requests, one_request, 0)
    for head in range(0, heads, 2):
        both = jnp.concatenate(
            [
                result_scr[:, head * rows : (head + 1) * rows],
                result_scr[:, (head + 1) * rows : (head + 2) * rows],
            ],
            axis=0,
        )
        out_ref[:, head * HD : (head + 2) * HD] = both.T.astype(jnp.bfloat16)


def attention(scalars, queries, cosine, sine, windows, suffix, rows, piece, most_rows, window_len):
    width, own = queries.shape
    heads = width // HD
    member_count = len(windows)
    chunk = min(512, windows[0].shape[1])
    suffix_chunk = 256

    def whole(array):
        return pl.BlockSpec(array.shape, lambda t, s, n=array.ndim: (0,) * n)

    return pl.pallas_call(
        lambda *refs: attention_kernel(
            member_count, heads, piece, most_rows, window_len, chunk, suffix_chunk, *refs
        ),
        out_shape=jax.ShapeDtypeStruct((own, width), jnp.bfloat16),
        grid_spec=pltpu.PrefetchScalarGridSpec(
            num_scalar_prefetch=1,
            grid=(own // rows,),
            in_specs=[
                pl.BlockSpec((width, rows), lambda t, s: (0, t)),
                pl.BlockSpec((HD // 2, rows), lambda t, s: (0, t)),
                pl.BlockSpec((HD // 2, rows), lambda t, s: (0, t)),
                *[whole(window) for window in windows],
                whole(suffix),
            ],
            out_specs=pl.BlockSpec((rows, width), lambda t, s: (t, 0)),
            scratch_shapes=[
                pltpu.VMEM((2 * HD, heads * rows), jnp.bfloat16),
                pltpu.VMEM((1, heads * rows), jnp.float32),
                pltpu.VMEM((1, heads * rows), jnp.float32),
                pltpu.VMEM((HD, heads * rows), jnp.float32),
                pltpu.VMEM((HD, heads * rows), jnp.float32),
            ],
        ),
        compiler_params=pltpu.CompilerParams(vmem_limit_bytes=48 * 2**20),
        cost_estimate=pl.CostEstimate(
            flops=20_000_000_000, bytes_accessed=8_000_000, transcendentals=10_000_000
        ),
        name="attention",
    )(scalars, queries, cosine, sine, *windows, suffix)


MESH = pl.DeviceIdType.MESH


def enter(groups):
    barrier = pltpu.get_barrier_semaphore()
    signals = 0
    for axis, count, stride in groups:
        place = lax.axis_index(axis)
        for shift in range(1, count):
            peer = lax.rem(place // stride + shift, count) * stride + lax.rem(place, stride)
            pl.semaphore_signal(barrier, inc=1, device_id={axis: peer}, device_id_type=MESH)
            signals += 1
    pl.semaphore_wait(barrier, signals)


def start_exchange(item, source, target, send, recv, local, row):
    scatter, (axis, count, stride) = item
    place = lax.axis_index(axis)
    mine = place // stride
    own = pltpu.make_async_copy(
        source.at[mine] if scatter else source, target.at[mine], local.at[row]
    )
    own.start()
    copies = [own]
    for shift in range(1, count):
        peer = lax.rem(mine + shift, count)
        copy = pltpu.make_async_remote_copy(
            src_ref=source.at[peer] if scatter else source,
            dst_ref=target.at[mine],
            send_sem=send.at[row, shift],
            recv_sem=recv.at[row, shift],
            device_id={axis: peer * stride + lax.rem(place, stride)},
            device_id_type=MESH,
        )
        copy.start()
        copies.append(copy)
    return copies


def remote_call(body, inputs, outputs, rows, most, collective_id, name):
    return pl.pallas_call(
        body,
        out_shape=outputs,
        in_specs=[pl.BlockSpec(memory_space=pl.ANY)] * len(inputs),
        out_specs=jax.tree.map(lambda _: pl.BlockSpec(memory_space=pl.ANY), outputs),
        scratch_shapes=[
            pltpu.SemaphoreType.DMA((rows, most)),
            pltpu.SemaphoreType.DMA((rows, most)),
            pltpu.SemaphoreType.DMA((rows,)),
        ],
        compiler_params=pltpu.CompilerParams(collective_id=collective_id, has_side_effects=True),
        name=name,
    )(*inputs)


def front_exchange(normed, dealt, alike, everyone, owners):
    def body(rows_ref, dealt_ref, all_rows, taken, windows, send, recv, local):
        enter([everyone, owners])
        first = start_exchange((True, everyone), dealt_ref, taken, send, recv, local, 0)
        second = start_exchange((False, alike), rows_ref, all_rows, send, recv, local, 1)
        for copy in first:
            copy.wait()
        third = start_exchange((False, owners), taken, windows, send, recv, local, 2)
        for copy in second + third:
            copy.wait()

    outputs = [
        jax.ShapeDtypeStruct((alike[1],) + normed.shape, normed.dtype),
        jax.ShapeDtypeStruct(dealt.shape, dealt.dtype),
        jax.ShapeDtypeStruct((owners[1],) + dealt.shape, dealt.dtype),
    ]
    most = max(alike[1], everyone[1], owners[1])
    return remote_call(body, [normed, dealt], outputs, 3, most, 0, "front_exchange")


def back_kernel(owner_count, kv_count, tok_count, parts, rows, vocab_step, *refs):
    att_ref, hid_ref = refs[:2]
    outw = refs[2 : 2 + parts]
    (
        gain_ref,
        fgain_ref,
        pick_ref,
        gate_hbm,
        up_hbm,
        down_hbm,
        head_hbm,
        out_ref,
        rms_ref,
        stat_ref,
        w_in,
        w_down,
        w_head,
        part_send,
        part_recv,
        half_send,
        half_recv,
        total,
        tiles,
        acc,
        act,
        shares,
        from_left,
        from_right,
        picked,
        picked_all,
        logits,
        stats,
        stats_all,
        load_sem,
        part_ss,
        part_rs,
        half_ss,
        half_rs,
        tile_ss,
        tile_rs,
        share_ss,
        left_rs,
        right_rs,
        pick_ss,
        pick_rs,
        stat_ss,
        stat_rs,
    ) = refs[2 + parts :]
    n = owner_count
    width = hid_ref.shape[1]
    chunks = tiles.shape[1]
    cw = width // chunks
    units = w_down.shape[0]
    tok = lax.axis_index("tok")
    z = lax.axis_index("req")
    members = tok_count // kv_count
    mine, member = tok // members, lax.rem(tok, members)
    across = mine + 1 - 2 * lax.rem(mine, 2)
    along = lax.rem(mine + 2, 4)
    diagonal = 3 - mine
    has_left, has_right = z > 0, z < n - 1
    left, right = lax.rem(z - 1 + n, n), lax.rem(z + 1, n)

    loads = [
        pltpu.make_async_copy(gate_hbm, w_in.at[:, :units], load_sem.at[0]),
        pltpu.make_async_copy(up_hbm, w_in.at[:, units:], load_sem.at[1]),
        pltpu.make_async_copy(down_hbm, w_down, load_sem.at[2]),
        pltpu.make_async_copy(head_hbm, w_head, load_sem.at[3]),
    ]
    for load in loads:
        load.start()

    barrier = pltpu.get_barrier_semaphore()

    def greet(shift, carry):
        pl.semaphore_signal(
            barrier,
            inc=1,
            device_id={"tok": lax.rem(tok + shift, tok_count)},
            device_id_type=MESH,
        )
        return carry

    lax.fori_loop(1, tok_count, greet, 0)

    @pl.when(has_left)
    def _():
        pl.semaphore_signal(barrier, inc=1, device_id={"req": left}, device_id_type=MESH)

    @pl.when(has_right)
    def _():
        pl.semaphore_signal(barrier, inc=1, device_id={"req": right}, device_id_type=MESH)

    def product(tile, c):
        at = pl.ds(pl.multiple_of(tile * rows, rows), rows)
        depth = att_ref.shape[1] // parts
        result = None
        for i in range(parts):
            term = jnp.dot(
                att_ref[at, i * depth : (i + 1) * depth],
                outw[i][:, c * cw : (c + 1) * cw],
                preferred_element_type=jnp.float32,
            )
            result = term if result is None else result + term
        return result

    def part_copy(kind, c):
        peer = across if c < chunks // 2 else along
        return pltpu.make_async_remote_copy(
            src_ref=part_send.at[kind, c],
            dst_ref=part_recv.at[kind, c],
            send_sem=part_ss.at[kind, c],
            recv_sem=part_rs.at[kind, c],
            device_id={"tok": peer * members + member},
            device_id_type=MESH,
        )

    def half_copy(c):
        peer = along if c < chunks // 2 else across
        return pltpu.make_async_remote_copy(
            src_ref=half_send.at[c],
            dst_ref=half_recv.at[c],
            send_sem=half_ss.at[c],
            recv_sem=half_rs.at[c],
            device_id={"tok": peer * members + member},
            device_id_type=MESH,
        )

    order = [c for pair in zip(range(chunks // 2), range(chunks // 2, chunks)) for c in pair]
    for c in order:
        part_send[0, c] = product(diagonal, c).astype(jnp.bfloat16)
    pl.semaphore_wait(
        barrier, tok_count - 1 + has_left.astype(jnp.int32) + has_right.astype(jnp.int32)
    )

    for c in order:
        part_copy(0, c).start()
    for c in order:
        near = across if c < chunks // 2 else along
        part_send[1, c] = product(near, c).astype(jnp.bfloat16)
        part_copy(1, c).start()
    for c in order:
        far = along if c < chunks // 2 else across
        here = product(far, c)
        part_copy(0, c).wait_recv()
        half_send[c] = (here + part_recv[0, c].astype(jnp.float32)).astype(jnp.bfloat16)
        half_copy(c).start()
    for c in order:
        cols = slice(c * cw, (c + 1) * cw)
        total[:, cols] = hid_ref[:, cols].astype(jnp.float32) + product(mine, c)
    squares = jnp.zeros((rows, 1), jnp.float32)
    for c in order:
        cols = slice(c * cw, (c + 1) * cw)
        part_copy(1, c).wait_recv()
        half_copy(c).wait_recv()
        summed = (
            total[:, cols]
            + part_recv[1, c].astype(jnp.float32)
            + half_recv[c].astype(jnp.float32)
        )
        middle = summed.astype(jnp.bfloat16).astype(jnp.float32)
        total[:, cols] = middle
        squares = squares + jnp.sum(middle * middle, axis=1, keepdims=True)
    scale = lax.rsqrt(squares / width + epsilon)

    def tile_copy(side, tile, c):
        return pltpu.make_async_remote_copy(
            src_ref=tiles.at[tile, c],
            dst_ref=tiles.at[tile, c],
            send_sem=tile_ss.at[side, tile, c],
            recv_sem=tile_rs.at[tile, c],
            device_id={"req": right if side == 0 else left},
            device_id_type=MESH,
        )

    def share_copy(side, tile, c):
        return pltpu.make_async_remote_copy(
            src_ref=shares.at[tile, c],
            dst_ref=(from_left if side == 0 else from_right).at[tile, c],
            send_sem=share_ss.at[tile, c],
            recv_sem=(left_rs if side == 0 else right_rs).at[tile, c],
            device_id={"req": right if side == 0 else left},
            device_id_type=MESH,
        )

    onward = (has_right, has_left)
    for c in range(chunks):
        cols = slice(c * cw, (c + 1) * cw)
        tiles[z, c] = (
            total[:, cols] * scale * gain_ref[:, cols].astype(jnp.float32)
        ).astype(jnp.bfloat16)
        for side in range(2):

            @pl.when(onward[side])
            def _(side=side, c=c):
                tile_copy(side, z, c).start()

    for load in loads[:3]:
        load.wait()

    def step(s, carry):
        sources = (z - s, z + s)
        valid = (sources[0] >= 0, (sources[1] < n) & (s > 0))
        for c in range(chunks):
            for side in range(2):

                @pl.when(valid[side] & (s > 0))
                def _(side=side, c=c):
                    tile_copy(side, sources[side], c).wait_recv()

                    @pl.when(onward[side])
                    def _():
                        tile_copy(side, sources[side], c).start()

            for side in range(2):

                @pl.when(valid[side])
                def _(side=side, c=c):
                    term = jnp.dot(
                        tiles[sources[side], c],
                        w_in[c * cw : (c + 1) * cw, :],
                        preferred_element_type=jnp.float32,
                    )
                    if c == 0:
                        acc[side] = term
                    else:
                        acc[side] += term

        for side in range(2):

            @pl.when(valid[side])
            def _(side=side):
                gate_proj = acc[side, :, :units]
                lifted = acc[side, :, units:]
                act[...] = (gate_proj / (1.0 + jnp.exp(-gate_proj)) * lifted).astype(
                    jnp.bfloat16
                )
                starts_sum = (s > 0) & jnp.logical_not(onward[side])
                for c in range(chunks):
                    shares[sources[side], c] = jnp.dot(
                        act[...],
                        w_down[:, c * cw : (c + 1) * cw],
                        preferred_element_type=jnp.float32,
                    ).astype(jnp.bfloat16)

                    @pl.when(starts_sum)
                    def _(c=c):
                        share_copy(1 - side, sources[side], c).start()

        targets = (s - z, 2 * (n - 1) - s - z)
        coming = (
            has_left & (targets[0] >= z) & (targets[0] < n),
            has_right & (targets[1] <= z) & (targets[1] >= 0),
        )
        for side in range(2):

            @pl.when(coming[side])
            def _(side=side):
                target = targets[side]
                arrived = from_left if side == 0 else from_right
                for c in range(chunks):
                    share_copy(side, target, c).wait_recv()

                    @pl.when(target != z)
                    def _(c=c):
                        shares[target, c] = (
                            shares[target, c].astype(jnp.float32)
                            + arrived[target, c].astype(jnp.float32)
                        ).astype(jnp.bfloat16)
                        share_copy(side, target, c).start()

        return carry

    lax.fori_loop(0, 2 * n - 1, step, 0)

    lane = lax.broadcasted_iota(jnp.int32, pick_ref.shape, 0) // 8
    chosen = jnp.zeros((pick_ref.shape[0], cw), jnp.float32)
    for c in range(chunks):
        cols = slice(c * cw, (c + 1) * cw)
        total[:, cols] += shares[z, c].astype(jnp.float32)

        @pl.when(has_left)
        def _(c=c, cols=cols):
            total[:, cols] += from_left[z, c].astype(jnp.float32)

        @pl.when(has_right)
        def _(c=c, cols=cols):
            total[:, cols] += from_right[z, c].astype(jnp.float32)

        final = total[:, cols].astype(jnp.bfloat16)
        out_ref[:, cols] = final
        picker = jnp.where(lane == c, pick_ref[...], 0.0).astype(jnp.bfloat16)
        chosen = chosen + jnp.dot(picker, final, preferred_element_type=jnp.float32)
    picked[...] = chosen.astype(jnp.bfloat16)

    def spread(source, target, ss, rs):
        def peer_copy(shift):
            return pltpu.make_async_remote_copy(
                src_ref=source,
                dst_ref=target.at[tok],
                send_sem=ss.at[shift],
                recv_sem=rs.at[shift],
                device_id={"tok": lax.rem(tok + shift, tok_count)},
                device_id_type=MESH,
            )

        def begin(shift, carry):
            peer_copy(shift).start()
            return carry

        def end(shift, carry):
            peer_copy(shift).wait()
            return carry

        lax.fori_loop(1, tok_count, begin, 0)
        target[tok] = source[...]
        lax.fori_loop(1, tok_count, end, 0)

    spread(picked, picked_all, pick_ss, pick_rs)
    gathered = picked_all[0].astype(jnp.float32)
    for i in range(1, tok_count):
        gathered = gathered + picked_all[i].astype(jnp.float32)
    last = jnp.concatenate([gathered[8 * c : 8 * c + 8] for c in range(chunks)], axis=1)
    mean_square = jnp.mean(last * last, axis=1, keepdims=True)
    rms_ref[...] = jnp.broadcast_to(jnp.sqrt(mean_square + epsilon), rms_ref.shape)
    final_normed = (
        last * lax.rsqrt(mean_square + epsilon) * fgain_ref[...].astype(jnp.float32)
    ).astype(jnp.bfloat16)
    final_normed = jnp.concatenate(
        [final_normed, jnp.zeros((128 - 8, width), jnp.bfloat16)], axis=0
    )
    loads[3].wait()

    def vocab(block, highest):
        at = pl.ds(pl.multiple_of(block * vocab_step, vocab_step), vocab_step)
        values = lax.dot_general(
            w_head[at, :],
            final_normed,
            (((1,), (1,)), ((), ())),
            preferred_element_type=jnp.float32,
        )
        logits[at, :] = values
        return jnp.maximum(highest, jnp.max(values, axis=0, keepdims=True))

    blocks = w_head.shape[0] // vocab_step
    top = lax.fori_loop(0, blocks, vocab, jnp.full((1, 128), -jnp.inf, jnp.float32))

    def exponents(block, amount):
        at = pl.ds(pl.multiple_of(block * vocab_step, vocab_step), vocab_step)
        return amount + jnp.sum(jnp.exp(logits[at, :] - top), axis=0, keepdims=True)

    amount = lax.fori_loop(0, blocks, exponents, jnp.zeros((1, 128), jnp.float32))
    stats[...] = jnp.concatenate([top, amount, jnp.zeros((6, 128), jnp.float32)], axis=0)
    spread(stats, stats_all, stat_ss, stat_rs)
    highest = stats_all[0, 0:1]
    for i in range(1, tok_count):
        highest = jnp.maximum(highest, stats_all[i, 0:1])
    amount = jnp.zeros((1, 128), jnp.float32)
    for i in range(tok_count):
        amount = amount + stats_all[i, 1:2] * jnp.exp(stats_all[i, 0:1] - highest)
    stat_ref[...] = jnp.concatenate(
        [highest, highest + jnp.log(amount), jnp.zeros((6, 128), jnp.float32)], axis=0
    )

    for c in order:
        part_copy(0, c).wait_send()
        part_copy(1, c).wait_send()
        half_copy(c).wait_send()

    def settle(tile, carry):
        for c in range(chunks):

            @pl.when(has_right & (tile <= z))
            def _(c=c):
                tile_copy(0, tile, c).wait_send()

            @pl.when(has_left & (tile >= z))
            def _(c=c):
                tile_copy(1, tile, c).wait_send()

            @pl.when(tile > z)
            def _(c=c):
                share_copy(0, tile, c).wait_send()

            @pl.when(tile < z)
            def _(c=c):
                share_copy(1, tile, c).wait_send()

        return carry

    lax.fori_loop(0, n, settle, 0)


def back(
    attended,
    hidden,
    out_parts,
    mlp_gain,
    final_gain,
    picker,
    gate_weight,
    up_weight,
    down_weight,
    head_weight,
    owner_count,
    kv_count,
    tok_count,
):
    rows, width = hidden.shape
    units = down_weight.shape[0]
    vocab_rows = head_weight.shape[0]
    vocab_step = max(b for b in range(16, 513, 16) if vocab_rows % b == 0)
    n, chunks = owner_count, 4
    cw = width // chunks
    bf16, f32 = jnp.bfloat16, jnp.float32
    dma = pltpu.SemaphoreType.DMA
    vmem = pl.BlockSpec(memory_space=pltpu.VMEM)
    hbm = pl.BlockSpec(memory_space=pltpu.HBM)
    parts = len(out_parts)
    return pl.pallas_call(
        lambda *refs: back_kernel(n, kv_count, tok_count, parts, rows, vocab_step, *refs),
        out_shape=[
            jax.ShapeDtypeStruct((rows, width), bf16),
            jax.ShapeDtypeStruct((8, 128), f32),
            jax.ShapeDtypeStruct((8, 128), f32),
        ],
        in_specs=[vmem] * (5 + parts) + [hbm] * 4,
        out_specs=[vmem] * 3,
        scratch_shapes=[
            pltpu.VMEM((width, 2 * units), bf16),
            pltpu.VMEM((units, width), bf16),
            pltpu.VMEM((vocab_rows, width), bf16),
            pltpu.VMEM((2, chunks, rows, cw), bf16),
            pltpu.VMEM((2, chunks, rows, cw), bf16),
            pltpu.VMEM((chunks, rows, cw), bf16),
            pltpu.VMEM((chunks, rows, cw), bf16),
            pltpu.VMEM((rows, width), f32),
            pltpu.VMEM((n, chunks, rows, cw), bf16),
            pltpu.VMEM((2, rows, 2 * units), f32),
            pltpu.VMEM((rows, units), bf16),
            pltpu.VMEM((n, chunks, rows, cw), bf16),
            pltpu.VMEM((n, chunks, rows, cw), bf16),
            pltpu.VMEM((n, chunks, rows, cw), bf16),
            pltpu.VMEM((8 * chunks, cw), bf16),
            pltpu.VMEM((tok_count, 8 * chunks, cw), bf16),
            pltpu.VMEM((vocab_rows, 128), f32),
            pltpu.VMEM((8, 128), f32),
            pltpu.VMEM((tok_count, 8, 128), f32),
            dma((4,)),
            dma((2, chunks)),
            dma((2, chunks)),
            dma((chunks,)),
            dma((chunks,)),
            dma((2, n, chunks)),
            dma((n, chunks)),
            dma((n, chunks)),
            dma((n, chunks)),
            dma((n, chunks)),
            dma((tok_count,)),
            dma((tok_count,)),
            dma((tok_count,)),
            dma((tok_count,)),
        ],
        compiler_params=pltpu.CompilerParams(
            collective_id=1, has_side_effects=True, vmem_limit_bytes=56 * 2**20
        ),
        name="back",
    )(
        attended,
        hidden,
        *out_parts,
        mlp_gain[None, :],
        final_gain[None, :],
        picker,
        gate_weight,
        up_weight,
        down_weight,
        head_weight,
    )


def shards(
    hidden_in,
    suffix_len,
    prefix_of,
    prefix_slot,
    prefix_cache,
    attn_gain,
    query_weight,
    keyval_weight,
    out_weight,
    mlp_gain,
    gate_weight,
    up_weight,
    down_weight,
    final_gain,
    head_weight,
):
    tok_count = lax.axis_size("tok")
    tok_place = lax.axis_index("tok")
    tok_rows = hidden_in.shape[0]
    own_rows = tok_rows * tok_count
    most_rows = own_rows // 2
    kv_count = keyval_weight.shape[0]
    members = tok_count // kv_count
    kv_head = tok_place // members
    member = tok_place % members
    owner_count = lax.axis_size("req")
    alike = ("tok", kv_count, members)
    everyone = ("tok", tok_count, 1)
    owners = ("req", owner_count, 1)

    def shifted(array, shift):
        pairs = [
            (h * members + (g + shift) % members, h * members + g)
            for h in range(kv_count)
            for g in range(members)
        ]
        return lax.ppermute(array, "tok", pairs)

    lengths = suffix_len[0]
    starts, end_rows, offsets = owner_layout(lengths, own_rows)
    query_parts = [query_weight] + [shifted(query_weight, s) for s in range(1, members)]
    out_parts = [out_weight] + [shifted(out_weight, s) for s in range(1, members)]
    normed = rms_scale(hidden_in, attn_gain).astype(jnp.bfloat16)
    window_block = prefix_cache.shape[2]
    piece = window_block // members
    dealt = prefix_cache.reshape(tok_count, piece, 2 * HD)
    rows_here, unused, windows = front_exchange(normed, dealt, alike, everyone, owners)
    rows_here = rows_here.reshape(kv_count * tok_rows, -1)
    windows = [windows.reshape(owner_count, tok_count * piece, 2 * HD)]
    windows += [shifted(windows[0], s) for s in range(1, members)]
    positions = lax.dynamic_index_in_dim(
        offsets.reshape(kv_count, members, tok_rows), member, 1, keepdims=False
    ).reshape(-1)
    positions = positions + PRE_LEN
    half = HD // 2
    levels = jnp.arange(half).astype(jnp.float32)
    inverse = jnp.exp(levels * (-2.0 * math.log(10000.0) / HD))
    angles = inverse[:, None] * positions.astype(jnp.float32)[None, :]
    cosine, sine = jnp.cos(angles), jnp.sin(angles)
    kv_weight = lax.dynamic_index_in_dim(keyval_weight, kv_head, 0, keepdims=False)
    keyvals = jnp.dot(rows_here, kv_weight, preferred_element_type=jnp.float32)
    low, high = keyvals[:, :half], keyvals[:, half:HD]
    cos_rows, sin_rows = cosine.T, sine.T
    keyvals = jnp.concatenate(
        [
            low * cos_rows - high * sin_rows,
            high * cos_rows + low * sin_rows,
            keyvals[:, HD:],
        ],
        axis=-1,
    ).astype(jnp.bfloat16)
    suffix = jnp.zeros((members, kv_count, tok_rows, 2 * HD), jnp.bfloat16)
    for s in range(members):
        part = keyvals if s == 0 else shifted(keyvals, s)
        suffix = lax.dynamic_update_index_in_dim(
            suffix, part.reshape(kv_count, tok_rows, 2 * HD), (member + s) % members, 0
        )
    suffix = jnp.transpose(suffix, (1, 0, 2, 3)).reshape(own_rows, 2 * HD)
    cache_width = kv_count * 2 * HD // tok_count
    cache_offset = tok_place * cache_width % (2 * HD)
    suffix_cache = lax.dynamic_slice_in_dim(suffix, cache_offset, cache_width, 1)
    queries = lax.dot_general(
        jnp.concatenate(query_parts, axis=1),
        rows_here,
        (((0,), (1,)), ((), ())),
        preferred_element_type=jnp.float32,
    )
    cache_rows = slot_lookup(prefix_of[0], prefix_slot)
    scalars = jnp.concatenate([starts, end_rows, cache_rows, member[None]]).astype(jnp.int32)
    attended = attention(
        scalars,
        queries,
        cosine,
        sine,
        windows,
        suffix,
        tok_rows,
        piece,
        most_rows,
        window_block * tok_count,
    )
    request_count = starts.shape[0]
    local_index = jnp.arange(tok_rows) + tok_place * tok_rows
    slots = jnp.pad(end_rows - 1, (0, 8 - request_count), constant_values=-1)
    picker = (local_index[None, :] == jnp.tile(slots, 4)[:, None]).astype(jnp.float32)
    final_state, spread, tail = back(
        attended,
        hidden_in,
        out_parts,
        mlp_gain,
        final_gain,
        picker,
        gate_weight,
        up_weight,
        down_weight,
        head_weight,
        owner_count,
        kv_count,
        tok_count,
    )
    return (
        final_state,
        suffix_cache,
        spread[:request_count, 0][None, :],
        tail[0:1, :request_count],
        tail[1:2, :request_count],
    )


def solution(mesh):
    placed = (
        P(("req", "tok"), None),
        P("req", None),
        P("req", None),
        P(),
        P("req", None, "tok", None),
        P(),
        P(None, "tok"),
        P(),
        P("tok", None),
        P(),
        P(None, "req"),
        P(None, "req"),
        P("req", None),
        P(),
        P("tok", None),
    )
    return jax.shard_map(
        shards,
        mesh=mesh,
        in_specs=placed,
        out_specs=(
            P(("req", "tok"), None),
            P("req", "tok"),
            P("req", None),
            P("req", None),
            P("req", None),
        ),
        check_vma=False,
    )
```

```python
import math

import jax
import jax.numpy as jnp
from jax import lax
from jax.experimental import pallas as pl
from jax.experimental.pallas import tpu as pltpu
from jax.sharding import PartitionSpec as P

HD = 64
PRE_LEN = 16384


epsilon = 1e-05
neg_large = -1e30


def attention_kernel(
    heads,
    most_rows,
    window_len,
    chunk,
    suffix_chunk,
    tok_count,
    kv_count,
    lengths_ref,
    chosen_ref,
    slot_ref,
    query_ref,
    windows,
    suffix_ref,
    out_ref,
    cache_ref,
    high_scr,
    total_scr,
    acc_scr,
    result_scr,
):
    requests = lengths_ref.shape[1]
    width = query_ref.shape[2]
    rows = width // heads
    members = tok_count // kv_count
    tok = lax.axis_index("tok")
    member = lax.rem(tok, members)
    tile = pl.program_id(0)
    first_row = (tile * members + member) * rows

    @pl.when(tile == 0)
    def _():
        cache_width = cache_ref.shape[1]
        for place in range(2 * HD // cache_width):

            @pl.when(lax.rem(tok, 2 * HD // cache_width) == place)
            def _(place=place):
                cache_ref[...] = suffix_ref[:, place * cache_width : (place + 1) * cache_width]

    def absorb(keyvals, visible_fn):
        scores = jnp.dot(keyvals, query_ref[0], preferred_element_type=jnp.float32)
        if visible_fn is not None:
            scores = jnp.where(visible_fn(scores.shape), scores, neg_large)
        before = high_scr[...]
        after = jnp.maximum(before, jnp.max(scores, axis=0, keepdims=True))
        weights = jnp.exp2(scores - after)
        fade = jnp.exp2(before - after)
        total_scr[...] = total_scr[...] * fade + jnp.sum(weights, axis=0, keepdims=True)
        mixed = lax.dot_general(
            keyvals,
            weights.astype(jnp.bfloat16),
            (((0,), (0,)), ((), ())),
            preferred_element_type=jnp.float32,
        )
        acc_scr[...] = acc_scr[...] * fade + mixed[HD:, :]
        high_scr[...] = after

    lane_row = first_row + lax.broadcasted_iota(jnp.int32, (1, width), 1) % rows

    def one_request(request, start):
        end = start + lengths_ref[0, request]
        slot = slot_ref[chosen_ref[0, request]]

        @pl.when((start < first_row + rows) & (end > first_row))
        def _():
            high_scr[...] = jnp.full(high_scr.shape, neg_large, jnp.float32)
            total_scr[...] = jnp.zeros(total_scr.shape, jnp.float32)
            acc_scr[...] = jnp.zeros(acc_scr.shape, jnp.float32)
            offset = lane_row - start
            for first in reversed(range(0, window_len, chunk)):

                def prefix_seen(shape, first=first):
                    position = first + lax.broadcasted_iota(jnp.int32, (shape[0], 1), 0)
                    return position > offset

                absorb(
                    windows[slot, first : first + chunk, :],
                    prefix_seen if first < most_rows else None,
                )

            def suffix_step(step, inner):
                base = pl.multiple_of(step * suffix_chunk, suffix_chunk)

                def suffix_seen(shape):
                    key_row = base + lax.broadcasted_iota(jnp.int32, (shape[0], 1), 0)
                    return (
                        (key_row >= start)
                        & (key_row <= lane_row)
                        & (lane_row - key_row < window_len)
                    )

                absorb(suffix_ref[pl.ds(base, suffix_chunk), :], suffix_seen)
                return inner

            lax.fori_loop(
                start // suffix_chunk,
                (jnp.minimum(first_row + rows, end) - 1) // suffix_chunk + 1,
                suffix_step,
                0,
            )
            mine = (lane_row >= start) & (lane_row < end)
            result_scr[...] = jnp.where(mine, acc_scr[...] / total_scr[...], result_scr[...])

        return end

    lax.fori_loop(0, requests, one_request, 0)
    for head in range(0, heads, 2):
        both = jnp.concatenate(
            [
                result_scr[:, head * rows : (head + 1) * rows],
                result_scr[:, (head + 1) * rows : (head + 2) * rows],
            ],
            axis=0,
        )
        out_ref[:, head * HD : (head + 2) * HD] = both.T.astype(jnp.bfloat16)


def attention(lengths, chosen, prefix_slot, queries, windows, suffix, rows, tok_count):
    kv_count, unused, lanes = queries.shape
    heads = lanes // rows
    own_rows = suffix.shape[0]
    window_len = windows.shape[1]
    chunk = min(512, window_len)
    suffix_chunk = 256
    cache_width = kv_count * 2 * HD // tok_count

    def whole(array):
        return pl.BlockSpec(array.shape, lambda t, *s, n=array.ndim: (0,) * n)

    return pl.pallas_call(
        lambda *refs: attention_kernel(
            heads, own_rows // 2, window_len, chunk, suffix_chunk, tok_count, kv_count, *refs
        ),
        out_shape=[
            jax.ShapeDtypeStruct((kv_count * rows, heads * HD), jnp.bfloat16),
            jax.ShapeDtypeStruct((own_rows, cache_width), jnp.bfloat16),
        ],
        grid_spec=pltpu.PrefetchScalarGridSpec(
            num_scalar_prefetch=3,
            grid=(kv_count,),
            in_specs=[
                pl.BlockSpec((1, 2 * HD, lanes), lambda t, *s: (t, 0, 0)),
                whole(windows),
                whole(suffix),
            ],
            out_specs=[
                pl.BlockSpec((rows, heads * HD), lambda t, *s: (t, 0)),
                pl.BlockSpec((own_rows, cache_width), lambda t, *s: (0, 0)),
            ],
            scratch_shapes=[
                pltpu.VMEM((1, lanes), jnp.float32),
                pltpu.VMEM((1, lanes), jnp.float32),
                pltpu.VMEM((HD, lanes), jnp.float32),
                pltpu.VMEM((HD, lanes), jnp.float32),
            ],
        ),
        compiler_params=pltpu.CompilerParams(vmem_limit_bytes=48 * 2**20),
        cost_estimate=pl.CostEstimate(
            flops=20_000_000_000, bytes_accessed=8_000_000, transcendentals=10_000_000
        ),
        name="attention",
    )(lengths, chosen, prefix_slot, queries, windows, suffix)


MESH = pl.DeviceIdType.MESH


def request_ends(lengths_ref, count):
    ends, end = [], 0
    for request in range(count):
        end = end + lengths_ref[0, request]
        ends.append(end)
    return ends


def front_kernel(
    owner_count,
    kv_count,
    tok_count,
    lengths_ref,
    hid_ref,
    gain_ref,
    query_hbm,
    keyval_hbm,
    prefix_hbm,
    query_ref,
    suffix_ref,
    windows,
    weights,
    tiles,
    suffix,
    local_sem,
    weight_ss,
    weight_rs,
    deal_ss,
    deal_rs,
    tile_ss,
    tile_rs,
    hop_ss,
    hop_rs,
    core_ss,
    core_rs,
    suffix_ss,
    suffix_rs,
):
    n = owner_count
    rows, width = hid_ref.shape
    chunks = tiles.shape[1]
    cw = width // chunks
    columns = query_hbm.shape[1]
    tok = lax.axis_index("tok")
    z = lax.axis_index("req")
    members = tok_count // kv_count
    mine, member = tok // members, lax.rem(tok, members)
    across = mine + 1 - 2 * lax.rem(mine, 2)
    along = lax.rem(mine + 2, 4)
    diagonal = 3 - mine
    has_left, has_right = z > 0, z < n - 1
    left, right = lax.rem(z - 1 + n, n), lax.rem(z + 1, n)
    onward = (has_right, has_left)
    half = HD // 2
    heads = members * columns // HD

    own_query = pltpu.make_async_copy(query_hbm, weights.at[:, :columns], local_sem.at[0])
    own_keyval = pltpu.make_async_copy(
        keyval_hbm.at[mine], weights.at[:, members * columns :], local_sem.at[1]
    )
    own_window = pltpu.make_async_copy(
        prefix_hbm.at[mine, member], windows.at[z, tok, member], local_sem.at[2]
    )
    own_query.start()
    own_keyval.start()
    own_window.start()

    barrier = pltpu.get_barrier_semaphore()

    def greet(shift, carry):
        pl.semaphore_signal(
            barrier,
            inc=1,
            device_id={"tok": lax.rem(tok + shift, tok_count)},
            device_id_type=MESH,
        )
        return carry

    lax.fori_loop(1, tok_count, greet, 0)

    @pl.when(has_left)
    def _():
        pl.semaphore_signal(barrier, inc=1, device_id={"req": left}, device_id_type=MESH)

    @pl.when(has_right)
    def _():
        pl.semaphore_signal(barrier, inc=1, device_id={"req": right}, device_id_type=MESH)

    squares = jnp.zeros((rows, 1), jnp.float32)
    for c in range(chunks):
        part = hid_ref[:, c * cw : (c + 1) * cw].astype(jnp.float32)
        squares = squares + jnp.sum(part * part, axis=1, keepdims=True)
    scale = lax.rsqrt(squares / width + epsilon)
    for c in range(chunks):
        cols = slice(c * cw, (c + 1) * cw)
        tiles[mine, c] = (
            hid_ref[:, cols].astype(jnp.float32)
            * scale
            * gain_ref[0:1, cols].astype(jnp.float32)
        ).astype(jnp.bfloat16)

    def deal_copy(shift):
        peer = lax.rem(tok + shift, tok_count)
        peer_member = lax.rem(peer, members)
        return pltpu.make_async_remote_copy(
            src_ref=prefix_hbm.at[peer // members, peer_member],
            dst_ref=windows.at[z, tok, peer_member],
            send_sem=deal_ss.at[shift],
            recv_sem=deal_rs.at[shift],
            device_id={"tok": peer},
            device_id_type=MESH,
        )

    def dealt(shift):
        return pltpu.make_async_remote_copy(
            src_ref=prefix_hbm.at[0, 0],
            dst_ref=windows.at[z, lax.rem(tok - shift + tok_count, tok_count), member],
            send_sem=deal_ss.at[shift],
            recv_sem=deal_rs.at[shift],
            device_id={"tok": lax.rem(tok + shift, tok_count)},
            device_id_type=MESH,
        )

    def weight_copy(shift):
        peer = lax.rem(member - shift + members, members)
        return pltpu.make_async_remote_copy(
            src_ref=query_hbm,
            dst_ref=weights.at[:, shift * columns : (shift + 1) * columns],
            send_sem=weight_ss.at[shift],
            recv_sem=weight_rs.at[shift],
            device_id={"tok": mine * members + peer},
            device_id_type=MESH,
        )

    def tile_copy(tile, c, to_along, relayed):
        return pltpu.make_async_remote_copy(
            src_ref=tiles.at[tile, c],
            dst_ref=tiles.at[tile, c],
            send_sem=tile_ss.at[int(to_along), int(relayed), c],
            recv_sem=tile_rs.at[tile, c],
            device_id={"tok": (along if to_along else across) * members + member},
            device_id_type=MESH,
        )

    def hop_copy(side, slot):
        return pltpu.make_async_remote_copy(
            src_ref=windows.at[slot, :, member],
            dst_ref=windows.at[slot, :, member],
            send_sem=hop_ss.at[side, slot],
            recv_sem=hop_rs.at[slot],
            device_id={"req": right if side == 0 else left},
            device_id_type=MESH,
        )

    def core_copy(slot, shift, place):
        return pltpu.make_async_remote_copy(
            src_ref=windows.at[slot, :, place],
            dst_ref=windows.at[slot, :, place],
            send_sem=core_ss.at[slot, shift],
            recv_sem=core_rs.at[slot, shift],
            device_id={"tok": mine * members + lax.rem(member + shift, members)},
            device_id_type=MESH,
        )

    def suffix_copy(tile, shift, place):
        return pltpu.make_async_remote_copy(
            src_ref=suffix.at[tile, place],
            dst_ref=suffix.at[tile, place],
            send_sem=suffix_ss.at[tile, shift],
            recv_sem=suffix_rs.at[tile, shift],
            device_id={"tok": mine * members + lax.rem(member + shift, members)},
            device_id_type=MESH,
        )

    pl.semaphore_wait(
        barrier, tok_count - 1 + has_left.astype(jnp.int32) + has_right.astype(jnp.int32)
    )

    def start_deal(shift, carry):
        deal_copy(shift).start()
        return carry

    lax.fori_loop(1, tok_count, start_deal, 0)
    order = [c for pair in zip(range(chunks // 2), range(chunks // 2, chunks)) for c in pair]
    for a, b in zip(range(chunks // 2), range(chunks // 2, chunks)):
        tile_copy(mine, a, False, False).start()
        tile_copy(mine, b, True, False).start()
    for a, b in zip(range(chunks // 2), range(chunks // 2, chunks)):
        tile_copy(mine, b, False, False).start()
        tile_copy(mine, a, True, False).start()
    for shift in range(1, members):
        weight_copy(shift).start()

    ends = request_ends(lengths_ref, lengths_ref.shape[1])

    def turns(tile):
        row = (tile * members + member) * rows + lax.broadcasted_iota(
            jnp.int32, (1, rows), 1
        )
        start = jnp.zeros((1, rows), jnp.int32)
        for end in ends[:-1]:
            start = jnp.where(row >= end, end, start)
        positions = (row - start + PRE_LEN).astype(jnp.float32)
        level = lax.broadcasted_iota(jnp.int32, (half, 1), 0).astype(jnp.float32)
        angles = jnp.exp(level * (-2.0 * math.log(10000.0) / HD)) * positions
        return jnp.cos(angles), jnp.sin(angles)

    def project(tile):
        cosine, sine = turns(tile)
        result = None
        for c in range(chunks):
            term = jnp.dot(
                tiles[tile, c],
                weights[c * cw : (c + 1) * cw, :],
                preferred_element_type=jnp.float32,
            )
            result = term if result is None else result + term
        zeros = jnp.zeros((HD, rows), jnp.bfloat16)
        for pair in range(heads // 2):
            turned = result[:, pair * 2 * HD : (pair + 1) * 2 * HD].T
            for odd in range(2):
                low = turned[odd * HD : odd * HD + half]
                high = turned[odd * HD + half : (odd + 1) * HD]
                cols = slice((2 * pair + odd) * rows, (2 * pair + odd + 1) * rows)
                both = jnp.concatenate(
                    [low * cosine - high * sine, high * cosine + low * sine], axis=0
                )
                query_ref[tile, :HD, cols] = (
                    both * (HD**-0.5 * math.log2(math.e))
                ).astype(jnp.bfloat16)
                query_ref[tile, HD:, cols] = zeros
        turned = result[:, heads * HD :].T
        low, high = turned[:half], turned[half:HD]
        keyvals = jnp.concatenate(
            [low * cosine - high * sine, high * cosine + low * sine, turned[HD:]], axis=0
        )
        suffix[tile, member] = keyvals.T.astype(jnp.bfloat16)
        for shift in range(1, members):
            suffix_copy(tile, shift, member).start()

    def relay(step):
        for side, slot, valid in ((0, z - step, z >= step), (1, z + step, z + step < n)):

            @pl.when(valid)
            def _(side=side, slot=slot):
                hop_copy(side, slot).wait_recv()

                @pl.when(onward[side])
                def _():
                    hop_copy(side, slot).start()

                for shift in range(1, members):
                    core_copy(slot, shift, member).start()

    own_window.wait()

    def wait_deal(shift, carry):
        dealt(shift).wait_recv()
        return carry

    lax.fori_loop(1, tok_count, wait_deal, 0)
    for side in range(2):

        @pl.when(onward[side])
        def _(side=side):
            hop_copy(side, z).start()

    for shift in range(1, members):
        core_copy(z, shift, member).start()

    for a, b in zip(range(chunks // 2), range(chunks // 2, chunks)):
        tile_copy(across, a, False, False).wait_recv()
        tile_copy(across, a, True, True).start()
        tile_copy(along, b, True, False).wait_recv()
        tile_copy(along, b, False, True).start()
    own_query.wait()
    own_keyval.wait()
    for shift in range(1, members):
        weight_copy(shift).wait_recv()
    project(mine)
    for a, b in zip(range(chunks // 2), range(chunks // 2, chunks)):
        tile_copy(across, b, False, False).wait_recv()
        tile_copy(along, a, True, False).wait_recv()
    relay(1)
    project(across)
    project(along)
    relay(2)
    for a, b in zip(range(chunks // 2), range(chunks // 2, chunks)):
        tile_copy(diagonal, a, True, True).wait_recv()
        tile_copy(diagonal, b, False, True).wait_recv()
    project(diagonal)
    for step in range(3, n):
        relay(step)

    for tile in range(kv_count):
        for shift in range(1, members):
            peer = lax.rem(member - shift + members, members)
            suffix_copy(tile, shift, peer).wait_recv()
    suffix_ref[...] = suffix[...]

    def settle(slot, carry):
        for shift in range(1, members):
            peer = lax.rem(member - shift + members, members)
            core_copy(slot, shift, peer).wait_recv()
            core_copy(slot, shift, member).wait_send()

        @pl.when(has_right & (slot <= z))
        def _():
            hop_copy(0, slot).wait_send()

        @pl.when(has_left & (slot >= z))
        def _():
            hop_copy(1, slot).wait_send()

        return carry

    lax.fori_loop(0, n, settle, 0)
    for c in range(chunks):
        tile_copy(mine, c, False, False).wait_send()
        tile_copy(mine, c, True, False).wait_send()
        if c < chunks // 2:
            tile_copy(across, c, True, True).wait_send()
        else:
            tile_copy(along, c, False, True).wait_send()
    for shift in range(1, members):
        weight_copy(shift).wait_send()
    for tile in range(kv_count):
        for shift in range(1, members):
            suffix_copy(tile, shift, member).wait_send()

    def deal_sent(shift, carry):
        deal_copy(shift).wait_send()
        return carry

    lax.fori_loop(1, tok_count, deal_sent, 0)


def front(
    lengths,
    hidden,
    gains,
    query_weight,
    keyval_weight,
    prefix,
    owner_count,
    kv_count,
    tok_count,
):
    rows, width = hidden.shape
    members = tok_count // kv_count
    columns = query_weight.shape[1]
    heads = members * columns // HD
    piece = prefix.shape[2]
    n, chunks = owner_count, 4
    cw = width // chunks
    bf16 = jnp.bfloat16
    dma = pltpu.SemaphoreType.DMA
    vmem = pl.BlockSpec(memory_space=pltpu.VMEM)
    hbm = pl.BlockSpec(memory_space=pltpu.HBM)
    return pl.pallas_call(
        lambda *refs: front_kernel(n, kv_count, tok_count, *refs),
        out_shape=[
            jax.ShapeDtypeStruct((kv_count, 2 * HD, heads * rows), bf16),
            jax.ShapeDtypeStruct((kv_count, members, rows, 2 * HD), bf16),
            jax.ShapeDtypeStruct((n, tok_count, members, piece, 2 * HD), bf16),
        ],
        in_specs=[pl.BlockSpec(memory_space=pltpu.SMEM), vmem, vmem, hbm, hbm, hbm],
        out_specs=[vmem, vmem, hbm],
        scratch_shapes=[
            pltpu.VMEM((width, members * columns + 2 * HD), bf16),
            pltpu.VMEM((kv_count, chunks, rows, cw), bf16),
            pltpu.VMEM((kv_count, members, rows, 2 * HD), bf16),
            dma((3,)),
            dma((members,)),
            dma((members,)),
            dma((tok_count,)),
            dma((tok_count,)),
            dma((2, 2, chunks)),
            dma((kv_count, chunks)),
            dma((2, n)),
            dma((n,)),
            dma((n, members)),
            dma((n, members)),
            dma((kv_count, members)),
            dma((kv_count, members)),
        ],
        compiler_params=pltpu.CompilerParams(
            collective_id=0, has_side_effects=True, vmem_limit_bytes=40 * 2**20
        ),
        name="front",
    )(lengths, hidden, gains, query_weight, keyval_weight, prefix)


def back_kernel(owner_count, kv_count, tok_count, parts, rows, vocab_step, *refs):
    lengths_ref, att_ref, hid_ref = refs[:3]
    outw = refs[3 : 3 + parts]
    (
        gain_ref,
        gate_hbm,
        up_hbm,
        down_hbm,
        head_hbm,
        out_ref,
        rms_ref,
        stat_ref,
        w_in,
        w_down,
        w_head,
        part_send,
        part_recv,
        half_send,
        half_recv,
        total,
        tiles,
        acc,
        act,
        shares,
        from_left,
        from_right,
        picked,
        picked_all,
        logits,
        stats,
        stats_all,
        load_sem,
        part_ss,
        part_rs,
        half_ss,
        half_rs,
        tile_ss,
        tile_rs,
        share_ss,
        left_rs,
        right_rs,
        pick_ss,
        pick_rs,
        stat_ss,
        stat_rs,
    ) = refs[3 + parts :]
    n = owner_count
    width = hid_ref.shape[1]
    chunks = tiles.shape[1]
    cw = width // chunks
    units = w_down.shape[0]
    tok = lax.axis_index("tok")
    z = lax.axis_index("req")
    members = tok_count // kv_count
    mine, member = tok // members, lax.rem(tok, members)
    across = mine + 1 - 2 * lax.rem(mine, 2)
    along = lax.rem(mine + 2, 4)
    diagonal = 3 - mine
    has_left, has_right = z > 0, z < n - 1
    left, right = lax.rem(z - 1 + n, n), lax.rem(z + 1, n)

    loads = [
        pltpu.make_async_copy(gate_hbm, w_in.at[:, :units], load_sem.at[0]),
        pltpu.make_async_copy(up_hbm, w_in.at[:, units:], load_sem.at[1]),
        pltpu.make_async_copy(down_hbm, w_down, load_sem.at[2]),
        pltpu.make_async_copy(head_hbm, w_head, load_sem.at[3]),
    ]
    for load in loads:
        load.start()

    barrier = pltpu.get_barrier_semaphore()

    def greet(shift, carry):
        pl.semaphore_signal(
            barrier,
            inc=1,
            device_id={"tok": lax.rem(tok + shift, tok_count)},
            device_id_type=MESH,
        )
        return carry

    lax.fori_loop(1, tok_count, greet, 0)

    @pl.when(has_left)
    def _():
        pl.semaphore_signal(barrier, inc=1, device_id={"req": left}, device_id_type=MESH)

    @pl.when(has_right)
    def _():
        pl.semaphore_signal(barrier, inc=1, device_id={"req": right}, device_id_type=MESH)

    def product(tile, c):
        at = pl.ds(pl.multiple_of(tile * rows, rows), rows)
        depth = att_ref.shape[1] // parts
        result = None
        for i in range(parts):
            term = jnp.dot(
                att_ref[at, i * depth : (i + 1) * depth],
                outw[i][:, c * cw : (c + 1) * cw],
                preferred_element_type=jnp.float32,
            )
            result = term if result is None else result + term
        return result

    def part_copy(kind, c):
        peer = across if c < chunks // 2 else along
        return pltpu.make_async_remote_copy(
            src_ref=part_send.at[kind, c],
            dst_ref=part_recv.at[kind, c],
            send_sem=part_ss.at[kind, c],
            recv_sem=part_rs.at[kind, c],
            device_id={"tok": peer * members + member},
            device_id_type=MESH,
        )

    def half_copy(c):
        peer = along if c < chunks // 2 else across
        return pltpu.make_async_remote_copy(
            src_ref=half_send.at[c],
            dst_ref=half_recv.at[c],
            send_sem=half_ss.at[c],
            recv_sem=half_rs.at[c],
            device_id={"tok": peer * members + member},
            device_id_type=MESH,
        )

    order = [c for pair in zip(range(chunks // 2), range(chunks // 2, chunks)) for c in pair]
    for c in order:
        part_send[0, c] = product(diagonal, c).astype(jnp.bfloat16)
    pl.semaphore_wait(
        barrier, tok_count - 1 + has_left.astype(jnp.int32) + has_right.astype(jnp.int32)
    )

    for c in order:
        part_copy(0, c).start()
    for c in order:
        near = across if c < chunks // 2 else along
        part_send[1, c] = product(near, c).astype(jnp.bfloat16)
        part_copy(1, c).start()
    for c in order:
        far = along if c < chunks // 2 else across
        here = product(far, c)
        part_copy(0, c).wait_recv()
        half_send[c] = (here + part_recv[0, c].astype(jnp.float32)).astype(jnp.bfloat16)
        half_copy(c).start()
    for c in order:
        cols = slice(c * cw, (c + 1) * cw)
        total[:, cols] = hid_ref[:, cols].astype(jnp.float32) + product(mine, c)
    squares = jnp.zeros((rows, 1), jnp.float32)
    for c in order:
        cols = slice(c * cw, (c + 1) * cw)
        part_copy(1, c).wait_recv()
        half_copy(c).wait_recv()
        summed = (
            total[:, cols]
            + part_recv[1, c].astype(jnp.float32)
            + half_recv[c].astype(jnp.float32)
        )
        middle = summed.astype(jnp.bfloat16).astype(jnp.float32)
        total[:, cols] = middle
        squares = squares + jnp.sum(middle * middle, axis=1, keepdims=True)
    scale = lax.rsqrt(squares / width + epsilon)

    def tile_copy(side, tile, c):
        return pltpu.make_async_remote_copy(
            src_ref=tiles.at[tile, c],
            dst_ref=tiles.at[tile, c],
            send_sem=tile_ss.at[side, tile, c],
            recv_sem=tile_rs.at[tile, c],
            device_id={"req": right if side == 0 else left},
            device_id_type=MESH,
        )

    def share_copy(side, tile, c):
        return pltpu.make_async_remote_copy(
            src_ref=shares.at[tile, c],
            dst_ref=(from_left if side == 0 else from_right).at[tile, c],
            send_sem=share_ss.at[tile, c],
            recv_sem=(left_rs if side == 0 else right_rs).at[tile, c],
            device_id={"req": right if side == 0 else left},
            device_id_type=MESH,
        )

    onward = (has_right, has_left)
    for c in range(chunks):
        cols = slice(c * cw, (c + 1) * cw)
        tiles[z, c] = (
            total[:, cols] * scale * gain_ref[1:2, cols].astype(jnp.float32)
        ).astype(jnp.bfloat16)
        for side in range(2):

            @pl.when(onward[side])
            def _(side=side, c=c):
                tile_copy(side, z, c).start()

    for load in loads[:3]:
        load.wait()

    def step(s, carry):
        sources = (z - s, z + s)
        valid = (sources[0] >= 0, (sources[1] < n) & (s > 0))
        for c in range(chunks):
            for side in range(2):

                @pl.when(valid[side] & (s > 0))
                def _(side=side, c=c):
                    tile_copy(side, sources[side], c).wait_recv()

                    @pl.when(onward[side])
                    def _():
                        tile_copy(side, sources[side], c).start()

            for side in range(2):

                @pl.when(valid[side])
                def _(side=side, c=c):
                    term = jnp.dot(
                        tiles[sources[side], c],
                        w_in[c * cw : (c + 1) * cw, :],
                        preferred_element_type=jnp.float32,
                    )
                    if c == 0:
                        acc[side] = term
                    else:
                        acc[side] += term

        for side in range(2):

            @pl.when(valid[side])
            def _(side=side):
                gate_proj = acc[side, :, :units]
                lifted = acc[side, :, units:]
                act[...] = (gate_proj / (1.0 + jnp.exp(-gate_proj)) * lifted).astype(
                    jnp.bfloat16
                )
                starts_sum = (s > 0) & jnp.logical_not(onward[side])
                for c in range(chunks):
                    shares[sources[side], c] = jnp.dot(
                        act[...],
                        w_down[:, c * cw : (c + 1) * cw],
                        preferred_element_type=jnp.float32,
                    ).astype(jnp.bfloat16)

                    @pl.when(starts_sum)
                    def _(c=c):
                        share_copy(1 - side, sources[side], c).start()

        targets = (s - z, 2 * (n - 1) - s - z)
        coming = (
            has_left & (targets[0] >= z) & (targets[0] < n),
            has_right & (targets[1] <= z) & (targets[1] >= 0),
        )
        for side in range(2):

            @pl.when(coming[side])
            def _(side=side):
                target = targets[side]
                arrived = from_left if side == 0 else from_right
                for c in range(chunks):
                    share_copy(side, target, c).wait_recv()

                    @pl.when(target != z)
                    def _(c=c):
                        shares[target, c] = (
                            shares[target, c].astype(jnp.float32)
                            + arrived[target, c].astype(jnp.float32)
                        ).astype(jnp.bfloat16)
                        share_copy(side, target, c).start()

        return carry

    lax.fori_loop(0, 2 * n - 1, step, 0)

    sublane = lax.broadcasted_iota(jnp.int32, (8 * chunks, rows), 0)
    row = tok * rows + lax.broadcasted_iota(jnp.int32, (8 * chunks, rows), 1)
    picks = jnp.zeros((8 * chunks, rows), jnp.float32)
    for request, end in enumerate(request_ends(lengths_ref, lengths_ref.shape[1])):
        picks = jnp.where((lax.rem(sublane, 8) == request) & (row == end - 1), 1.0, picks)
    chosen = jnp.zeros((8 * chunks, cw), jnp.float32)
    for c in range(chunks):
        cols = slice(c * cw, (c + 1) * cw)
        total[:, cols] += shares[z, c].astype(jnp.float32)

        @pl.when(has_left)
        def _(c=c, cols=cols):
            total[:, cols] += from_left[z, c].astype(jnp.float32)

        @pl.when(has_right)
        def _(c=c, cols=cols):
            total[:, cols] += from_right[z, c].astype(jnp.float32)

        final = total[:, cols].astype(jnp.bfloat16)
        out_ref[:, cols] = final
        picker = jnp.where(sublane // 8 == c, picks, 0.0).astype(jnp.bfloat16)
        chosen = chosen + jnp.dot(picker, final, preferred_element_type=jnp.float32)
    picked[...] = chosen.astype(jnp.bfloat16)

    def spread(source, target, ss, rs):
        def peer_copy(shift):
            return pltpu.make_async_remote_copy(
                src_ref=source,
                dst_ref=target.at[tok],
                send_sem=ss.at[shift],
                recv_sem=rs.at[shift],
                device_id={"tok": lax.rem(tok + shift, tok_count)},
                device_id_type=MESH,
            )

        def begin(shift, carry):
            peer_copy(shift).start()
            return carry

        def end(shift, carry):
            peer_copy(shift).wait()
            return carry

        lax.fori_loop(1, tok_count, begin, 0)
        target[tok] = source[...]
        lax.fori_loop(1, tok_count, end, 0)

    spread(picked, picked_all, pick_ss, pick_rs)
    gathered = picked_all[0].astype(jnp.float32)
    for i in range(1, tok_count):
        gathered = gathered + picked_all[i].astype(jnp.float32)
    last = jnp.concatenate([gathered[8 * c : 8 * c + 8] for c in range(chunks)], axis=1)
    mean_square = jnp.mean(last * last, axis=1, keepdims=True)
    rms_ref[...] = jnp.broadcast_to(jnp.sqrt(mean_square + epsilon), rms_ref.shape)
    final_normed = (
        last * lax.rsqrt(mean_square + epsilon) * gain_ref[2:3, :].astype(jnp.float32)
    ).astype(jnp.bfloat16)
    final_normed = jnp.concatenate(
        [final_normed, jnp.zeros((128 - 8, width), jnp.bfloat16)], axis=0
    )
    loads[3].wait()

    def vocab(block, highest):
        at = pl.ds(pl.multiple_of(block * vocab_step, vocab_step), vocab_step)
        values = lax.dot_general(
            w_head[at, :],
            final_normed,
            (((1,), (1,)), ((), ())),
            preferred_element_type=jnp.float32,
        )
        logits[at, :] = values
        return jnp.maximum(highest, jnp.max(values, axis=0, keepdims=True))

    blocks = w_head.shape[0] // vocab_step
    top = lax.fori_loop(0, blocks, vocab, jnp.full((1, 128), -jnp.inf, jnp.float32))

    def exponents(block, amount):
        at = pl.ds(pl.multiple_of(block * vocab_step, vocab_step), vocab_step)
        return amount + jnp.sum(jnp.exp(logits[at, :] - top), axis=0, keepdims=True)

    amount = lax.fori_loop(0, blocks, exponents, jnp.zeros((1, 128), jnp.float32))
    stats[...] = jnp.concatenate([top, amount, jnp.zeros((6, 128), jnp.float32)], axis=0)
    spread(stats, stats_all, stat_ss, stat_rs)
    highest = stats_all[0, 0:1]
    for i in range(1, tok_count):
        highest = jnp.maximum(highest, stats_all[i, 0:1])
    amount = jnp.zeros((1, 128), jnp.float32)
    for i in range(tok_count):
        amount = amount + stats_all[i, 1:2] * jnp.exp(stats_all[i, 0:1] - highest)
    stat_ref[...] = jnp.concatenate(
        [highest, highest + jnp.log(amount), jnp.zeros((6, 128), jnp.float32)], axis=0
    )

    for c in order:
        part_copy(0, c).wait_send()
        part_copy(1, c).wait_send()
        half_copy(c).wait_send()

    def settle(tile, carry):
        for c in range(chunks):

            @pl.when(has_right & (tile <= z))
            def _(c=c):
                tile_copy(0, tile, c).wait_send()

            @pl.when(has_left & (tile >= z))
            def _(c=c):
                tile_copy(1, tile, c).wait_send()

            @pl.when(tile > z)
            def _(c=c):
                share_copy(0, tile, c).wait_send()

            @pl.when(tile < z)
            def _(c=c):
                share_copy(1, tile, c).wait_send()

        return carry

    lax.fori_loop(0, n, settle, 0)


def back(
    lengths,
    attended,
    hidden,
    out_parts,
    gains,
    gate_weight,
    up_weight,
    down_weight,
    head_weight,
    owner_count,
    kv_count,
    tok_count,
):
    rows, width = hidden.shape
    units = down_weight.shape[0]
    vocab_rows = head_weight.shape[0]
    vocab_step = max(b for b in range(16, 513, 16) if vocab_rows % b == 0)
    n, chunks = owner_count, 4
    cw = width // chunks
    bf16, f32 = jnp.bfloat16, jnp.float32
    dma = pltpu.SemaphoreType.DMA
    vmem = pl.BlockSpec(memory_space=pltpu.VMEM)
    hbm = pl.BlockSpec(memory_space=pltpu.HBM)
    parts = len(out_parts)
    return pl.pallas_call(
        lambda *refs: back_kernel(n, kv_count, tok_count, parts, rows, vocab_step, *refs),
        out_shape=[
            jax.ShapeDtypeStruct((rows, width), bf16),
            jax.ShapeDtypeStruct((8, 128), f32),
            jax.ShapeDtypeStruct((8, 128), f32),
        ],
        in_specs=[pl.BlockSpec(memory_space=pltpu.SMEM)] + [vmem] * (3 + parts) + [hbm] * 4,
        out_specs=[vmem] * 3,
        scratch_shapes=[
            pltpu.VMEM((width, 2 * units), bf16),
            pltpu.VMEM((units, width), bf16),
            pltpu.VMEM((vocab_rows, width), bf16),
            pltpu.VMEM((2, chunks, rows, cw), bf16),
            pltpu.VMEM((2, chunks, rows, cw), bf16),
            pltpu.VMEM((chunks, rows, cw), bf16),
            pltpu.VMEM((chunks, rows, cw), bf16),
            pltpu.VMEM((rows, width), f32),
            pltpu.VMEM((n, chunks, rows, cw), bf16),
            pltpu.VMEM((2, rows, 2 * units), f32),
            pltpu.VMEM((rows, units), bf16),
            pltpu.VMEM((n, chunks, rows, cw), bf16),
            pltpu.VMEM((n, chunks, rows, cw), bf16),
            pltpu.VMEM((n, chunks, rows, cw), bf16),
            pltpu.VMEM((8 * chunks, cw), bf16),
            pltpu.VMEM((tok_count, 8 * chunks, cw), bf16),
            pltpu.VMEM((vocab_rows, 128), f32),
            pltpu.VMEM((8, 128), f32),
            pltpu.VMEM((tok_count, 8, 128), f32),
            dma((4,)),
            dma((2, chunks)),
            dma((2, chunks)),
            dma((chunks,)),
            dma((chunks,)),
            dma((2, n, chunks)),
            dma((n, chunks)),
            dma((n, chunks)),
            dma((n, chunks)),
            dma((n, chunks)),
            dma((tok_count,)),
            dma((tok_count,)),
            dma((tok_count,)),
            dma((tok_count,)),
        ],
        compiler_params=pltpu.CompilerParams(
            collective_id=1, has_side_effects=True, vmem_limit_bytes=56 * 2**20
        ),
        name="back",
    )(
        lengths,
        attended,
        hidden,
        *out_parts,
        gains,
        gate_weight,
        up_weight,
        down_weight,
        head_weight,
    )


def shards(
    hidden_in,
    suffix_len,
    prefix_of,
    prefix_slot,
    prefix_cache,
    attn_gain,
    query_weight,
    keyval_weight,
    out_weight,
    mlp_gain,
    gate_weight,
    up_weight,
    down_weight,
    final_gain,
    head_weight,
):
    tok_count = lax.axis_size("tok")
    owner_count = lax.axis_size("req")
    tok_rows = hidden_in.shape[0]
    own_rows = tok_rows * tok_count
    kv_count = keyval_weight.shape[0]
    members = tok_count // kv_count

    def shifted(array, shift):
        pairs = [
            (h * members + (g + shift) % members, h * members + g)
            for h in range(kv_count)
            for g in range(members)
        ]
        return lax.ppermute(array, "tok", pairs)

    out_parts = [out_weight] + [shifted(out_weight, s) for s in range(1, members)]
    gains = jnp.stack([attn_gain, mlp_gain, final_gain])
    window_block = prefix_cache.shape[2]
    queries, suffix, windows = front(
        suffix_len,
        hidden_in,
        gains,
        query_weight,
        keyval_weight,
        prefix_cache.reshape(kv_count, members, window_block // members, 2 * HD),
        owner_count,
        kv_count,
        tok_count,
    )
    attended, suffix_cache = attention(
        suffix_len,
        prefix_of,
        prefix_slot,
        queries,
        windows.reshape(owner_count, window_block * tok_count, 2 * HD),
        suffix.reshape(own_rows, 2 * HD),
        tok_rows,
        tok_count,
    )
    request_count = suffix_len.shape[1]
    final_state, spread, tail = back(
        suffix_len,
        attended,
        hidden_in,
        out_parts,
        gains,
        gate_weight,
        up_weight,
        down_weight,
        head_weight,
        owner_count,
        kv_count,
        tok_count,
    )
    return (
        final_state,
        suffix_cache,
        spread[:request_count, 0][None, :],
        tail[0:1, :request_count],
        tail[1:2, :request_count],
    )


def solution(mesh):
    placed = (
        P(("req", "tok"), None),
        P("req", None),
        P("req", None),
        P(),
        P("req", None, "tok", None),
        P(),
        P(None, "tok"),
        P(),
        P("tok", None),
        P(),
        P(None, "req"),
        P(None, "req"),
        P("req", None),
        P(),
        P("tok", None),
    )
    return jax.shard_map(
        shards,
        mesh=mesh,
        in_specs=placed,
        out_specs=(
            P(("req", "tok"), None),
            P("req", "tok"),
            P("req", None),
            P("req", None),
            P("req", None),
        ),
        check_vma=False,
    )
```

```python
import math

import jax
import jax.numpy as jnp
from jax import lax
from jax.experimental import pallas as pl
from jax.experimental.pallas import tpu as pltpu
from jax.sharding import PartitionSpec as P

HD = 64
PRE_LEN = 16384
VMEM_LIMIT = 60 * 2**20


epsilon = 1e-05
neg_large = -1e30


def attention_kernel(
    most_rows,
    tok_count,
    kv_count,
    lengths_ref,
    chosen_ref,
    slot_ref,
    query_ref,
    windows,
    suffix_ref,
    out_ref,
    cache_ref,
    padded,
    band,
    band_values,
    score_scr,
):
    requests = lengths_ref.shape[1]
    units, unused, lanes = query_ref.shape
    rows = out_ref.shape[0] // kv_count
    unit_rows = out_ref.shape[0] // units
    per_tile = rows // unit_rows
    pairs = lanes // 2 // unit_rows
    window_len = windows.shape[1]
    own_rows = suffix_ref.shape[0]
    chunk = 256
    span = window_len + chunk
    tail_rows = band.shape[0] - window_len
    members = tok_count // kv_count
    tok = lax.axis_index("tok")
    member = lax.rem(tok, members)

    cache_width = cache_ref.shape[1]
    for place in range(2 * HD // cache_width):

        @pl.when(lax.rem(tok, 2 * HD // cache_width) == place)
        def _(place=place):
            cache_ref[...] = suffix_ref[:, place * cache_width : (place + 1) * cache_width]

    padded[:own_rows, :] = suffix_ref[...]
    padded[own_rows:, :] = jnp.zeros((padded.shape[0] - own_rows, 2 * HD), jnp.bfloat16)

    def turned(block):
        return block.astype(jnp.float32).T[HD:].astype(jnp.bfloat16)

    def folded(values, fold):
        return fold(values.reshape(values.shape[0] // 8, 8, lanes), axis=0)

    def one_request(request, start):
        end = start + lengths_ref[0, request]
        slot = slot_ref[chosen_ref[0, request]]
        touched = jnp.int32(0)
        for tile in range(kv_count):
            first_row = (tile * members + member) * rows
            touched = touched + ((start < first_row + rows) & (end > first_row)).astype(jnp.int32)

        @pl.when(touched > 0)
        def _():
            for first in range(0, window_len, chunk):
                block = windows[slot, first : first + chunk, :]
                band[first : first + chunk, :] = block
                band_values[:, first : first + chunk] = turned(block)
            base = pl.multiple_of(start // 16 * 16, 16)
            lifted = padded[pl.ds(base, tail_rows + 16), :].astype(jnp.float32)
            lifted = pltpu.roll(lifted, tail_rows + 16 - (start - base), axis=0)
            for first in range(0, tail_rows, 128):
                block = lifted[first : first + 128].astype(jnp.bfloat16)
                at = slice(window_len + first, window_len + first + 128)
                band[at, :] = block
                band_values[:, at] = turned(block)

        def one_unit(unit, carry):
            tile = unit // per_tile
            first_row = (tile * members + member) * rows + lax.rem(unit, per_tile) * unit_rows

            @pl.when((start < first_row + unit_rows) & (end > first_row))
            def _():
                query = query_ref[unit]
                lane_row = first_row + lax.broadcasted_iota(jnp.int32, (1, lanes), 1) % unit_rows
                offset = lane_row - start
                low = pl.multiple_of((jnp.maximum(first_row, start) - start) // 128 * 128, 128)
                high = None
                for first in range(0, span, chunk):
                    scores = jnp.dot(
                        band[pl.ds(low + first, chunk), :],
                        query,
                        preferred_element_type=jnp.float32,
                    )
                    place = low + first + lax.broadcasted_iota(jnp.int32, (chunk, 1), 0)
                    if first == 0:
                        scores = jnp.where(place > offset, scores, neg_large)
                    if first == span - chunk:
                        scores = jnp.where(place <= offset + window_len, scores, neg_large)
                    score_scr[first : first + chunk, :] = scores
                    top = folded(scores, jnp.max)
                    high = top if high is None else jnp.maximum(high, top)
                high = jnp.max(high, axis=0, keepdims=True)
                total, acc = None, None
                for first in range(0, span, chunk):
                    weights = jnp.exp2(score_scr[first : first + chunk, :] - high)
                    part = folded(weights, jnp.sum)
                    term = jnp.dot(
                        band_values[:, pl.ds(low + first, chunk)],
                        weights.astype(jnp.bfloat16),
                        preferred_element_type=jnp.float32,
                    )
                    total = part if total is None else total + part
                    acc = term if acc is None else acc + term
                result = acc / jnp.sum(total, axis=0, keepdims=True)
                both = jnp.concatenate([result[:, : lanes // 2], result[:, lanes // 2 :]], axis=0)
                flat = both.T
                at = pl.ds(pl.multiple_of(unit * unit_rows, unit_rows), unit_rows)
                row = first_row + lax.broadcasted_iota(jnp.int32, (unit_rows, 1), 0)
                mine = (row >= start) & (row < end)
                for pair in range(pairs):
                    cols = slice(pair * 2 * HD, (pair + 1) * 2 * HD)
                    new = flat[pair * unit_rows : (pair + 1) * unit_rows]
                    old = out_ref[at, cols].astype(jnp.float32)
                    out_ref[at, cols] = jnp.where(mine, new, old).astype(jnp.bfloat16)

            return carry

        lax.fori_loop(0, units, one_unit, 0)
        return end

    lax.fori_loop(0, requests, one_request, 0)


def attention(lengths, chosen, prefix_slot, queries, windows, suffix, rows, kv_count, tok_count):
    units, unused, lanes = queries.shape
    heads = units * lanes // (kv_count * rows)
    own_rows = suffix.shape[0]
    window_len = windows.shape[1]
    cache_width = kv_count * 2 * HD // tok_count
    tail_rows = own_rows // 2 + 256
    smem = pl.BlockSpec(memory_space=pltpu.SMEM)
    vmem = pl.BlockSpec(memory_space=pltpu.VMEM)
    return pl.pallas_call(
        lambda *refs: attention_kernel(own_rows // 2, tok_count, kv_count, *refs),
        out_shape=[
            jax.ShapeDtypeStruct((kv_count * rows, heads * HD), jnp.bfloat16),
            jax.ShapeDtypeStruct((own_rows, cache_width), jnp.bfloat16),
        ],
        in_specs=[smem] * 3 + [vmem] * 3,
        out_specs=[vmem] * 2,
        scratch_shapes=[
            pltpu.VMEM((own_rows + tail_rows + 16, 2 * HD), jnp.bfloat16),
            pltpu.VMEM((window_len + tail_rows, 2 * HD), jnp.bfloat16),
            pltpu.VMEM((HD, window_len + tail_rows), jnp.bfloat16),
            pltpu.VMEM((window_len + 256, lanes), jnp.float32),
        ],
        compiler_params=pltpu.CompilerParams(vmem_limit_bytes=VMEM_LIMIT),
        cost_estimate=pl.CostEstimate(
            flops=10_000_000_000, bytes_accessed=8_000_000, transcendentals=10_000_000
        ),
        name="attention",
    )(lengths, chosen, prefix_slot, queries, windows, suffix)


MESH = pl.DeviceIdType.MESH


def request_ends(lengths_ref, count):
    ends, end = [], 0
    for request in range(count):
        end = end + lengths_ref[0, request]
        ends.append(end)
    return ends


def front_kernel(
    owner_count,
    kv_count,
    tok_count,
    lengths_ref,
    hid_ref,
    gain_ref,
    query_hbm,
    keyval_hbm,
    prefix_hbm,
    query_ref,
    suffix_ref,
    windows,
    weights,
    tiles,
    suffix,
    local_sem,
    weight_ss,
    weight_rs,
    deal_ss,
    deal_rs,
    tile_ss,
    tile_rs,
    hop_ss,
    hop_rs,
    core_ss,
    core_rs,
    suffix_ss,
    suffix_rs,
):
    n = owner_count
    rows, width = hid_ref.shape
    chunks = tiles.shape[1]
    cw = width // chunks
    columns = query_hbm.shape[1]
    tok = lax.axis_index("tok")
    z = lax.axis_index("req")
    members = tok_count // kv_count
    mine, member = tok // members, lax.rem(tok, members)
    across = mine + 1 - 2 * lax.rem(mine, 2)
    along = lax.rem(mine + 2, 4)
    diagonal = 3 - mine
    has_left, has_right = z > 0, z < n - 1
    left, right = lax.rem(z - 1 + n, n), lax.rem(z + 1, n)
    onward = (has_right, has_left)
    half = HD // 2
    heads = members * columns // HD

    own_query = pltpu.make_async_copy(query_hbm, weights.at[:, :columns], local_sem.at[0])
    own_keyval = pltpu.make_async_copy(
        keyval_hbm.at[mine], weights.at[:, members * columns :], local_sem.at[1]
    )
    own_window = pltpu.make_async_copy(
        prefix_hbm.at[mine, member], windows.at[z, tok, member], local_sem.at[2]
    )
    own_query.start()
    own_keyval.start()
    own_window.start()

    barrier = pltpu.get_barrier_semaphore()

    def greet(shift, carry):
        pl.semaphore_signal(
            barrier,
            inc=1,
            device_id={"tok": lax.rem(tok + shift, tok_count)},
            device_id_type=MESH,
        )
        return carry

    lax.fori_loop(1, tok_count, greet, 0)

    @pl.when(has_left)
    def _():
        pl.semaphore_signal(barrier, inc=1, device_id={"req": left}, device_id_type=MESH)

    @pl.when(has_right)
    def _():
        pl.semaphore_signal(barrier, inc=1, device_id={"req": right}, device_id_type=MESH)

    squares = jnp.zeros((rows, 1), jnp.float32)
    for c in range(chunks):
        part = hid_ref[:, c * cw : (c + 1) * cw].astype(jnp.float32)
        squares = squares + jnp.sum(part * part, axis=1, keepdims=True)
    scale = lax.rsqrt(squares / width + epsilon)
    for c in range(chunks):
        cols = slice(c * cw, (c + 1) * cw)
        tiles[mine, c] = (
            hid_ref[:, cols].astype(jnp.float32)
            * scale
            * gain_ref[cols].astype(jnp.float32).reshape(1, cw)
        ).astype(jnp.bfloat16)

    def deal_copy(shift):
        peer = lax.rem(tok + shift, tok_count)
        peer_member = lax.rem(peer, members)
        return pltpu.make_async_remote_copy(
            src_ref=prefix_hbm.at[peer // members, peer_member],
            dst_ref=windows.at[z, tok, peer_member],
            send_sem=deal_ss.at[shift],
            recv_sem=deal_rs.at[shift],
            device_id={"tok": peer},
            device_id_type=MESH,
        )

    def dealt(shift):
        return pltpu.make_async_remote_copy(
            src_ref=prefix_hbm.at[0, 0],
            dst_ref=windows.at[z, lax.rem(tok - shift + tok_count, tok_count), member],
            send_sem=deal_ss.at[shift],
            recv_sem=deal_rs.at[shift],
            device_id={"tok": lax.rem(tok + shift, tok_count)},
            device_id_type=MESH,
        )

    def weight_copy(shift):
        peer = lax.rem(member - shift + members, members)
        return pltpu.make_async_remote_copy(
            src_ref=query_hbm,
            dst_ref=weights.at[:, shift * columns : (shift + 1) * columns],
            send_sem=weight_ss.at[shift],
            recv_sem=weight_rs.at[shift],
            device_id={"tok": mine * members + peer},
            device_id_type=MESH,
        )

    def tile_copy(tile, c, to_along, relayed):
        return pltpu.make_async_remote_copy(
            src_ref=tiles.at[tile, c],
            dst_ref=tiles.at[tile, c],
            send_sem=tile_ss.at[int(to_along), int(relayed), c],
            recv_sem=tile_rs.at[tile, c],
            device_id={"tok": (along if to_along else across) * members + member},
            device_id_type=MESH,
        )

    def hop_copy(side, slot):
        return pltpu.make_async_remote_copy(
            src_ref=windows.at[slot, :, member],
            dst_ref=windows.at[slot, :, member],
            send_sem=hop_ss.at[side, slot],
            recv_sem=hop_rs.at[slot],
            device_id={"req": right if side == 0 else left},
            device_id_type=MESH,
        )

    def core_copy(slot, shift, place):
        return pltpu.make_async_remote_copy(
            src_ref=windows.at[slot, :, place],
            dst_ref=windows.at[slot, :, place],
            send_sem=core_ss.at[slot, shift],
            recv_sem=core_rs.at[slot, shift],
            device_id={"tok": mine * members + lax.rem(member + shift, members)},
            device_id_type=MESH,
        )

    def suffix_copy(tile, shift, place):
        return pltpu.make_async_remote_copy(
            src_ref=suffix.at[tile, place],
            dst_ref=suffix.at[tile, place],
            send_sem=suffix_ss.at[tile, shift],
            recv_sem=suffix_rs.at[tile, shift],
            device_id={"tok": mine * members + lax.rem(member + shift, members)},
            device_id_type=MESH,
        )

    pl.semaphore_wait(
        barrier, tok_count - 1 + has_left.astype(jnp.int32) + has_right.astype(jnp.int32)
    )

    def start_deal(shift, carry):
        deal_copy(shift).start()
        return carry

    lax.fori_loop(1, tok_count, start_deal, 0)
    order = [c for pair in zip(range(chunks // 2), range(chunks // 2, chunks)) for c in pair]
    for a, b in zip(range(chunks // 2), range(chunks // 2, chunks)):
        tile_copy(mine, a, False, False).start()
        tile_copy(mine, b, True, False).start()
    for a, b in zip(range(chunks // 2), range(chunks // 2, chunks)):
        tile_copy(mine, b, False, False).start()
        tile_copy(mine, a, True, False).start()
    for shift in range(1, members):
        weight_copy(shift).start()

    ends = request_ends(lengths_ref, lengths_ref.shape[1])

    def turns(row):
        start = jnp.zeros((1, rows), jnp.int32)
        for end in ends[:-1]:
            start = jnp.where(row >= end, end, start)
        positions = (row - start + PRE_LEN).astype(jnp.float32)
        level = lax.broadcasted_iota(jnp.int32, (half, 1), 0).astype(jnp.float32)
        angles = jnp.exp(level * (-2.0 * math.log(10000.0) / HD)) * positions
        return jnp.cos(angles), jnp.sin(angles)

    unit_rows = 2 * rows // heads
    per_tile = rows // unit_rows

    def project(tile):
        result = None
        for c in range(chunks):
            term = jnp.dot(
                tiles[tile, c],
                weights[c * cw : (c + 1) * cw, :],
                preferred_element_type=jnp.float32,
            )
            result = term if result is None else result + term
        first_row = (tile * members + member) * rows
        lane = lax.broadcasted_iota(jnp.int32, (1, rows), 1)
        zeros = jnp.zeros((HD, 2 * rows), jnp.bfloat16)
        for u in range(per_tile):
            cosine, sine = turns(first_row + u * unit_rows + lax.rem(lane, unit_rows))
            block = result[u * unit_rows : (u + 1) * unit_rows]
            turned = jnp.concatenate(
                [block[:, p * 2 * HD : (p + 1) * 2 * HD] for p in range(heads // 2)], axis=0
            ).T
            for odd in range(2):
                low = turned[odd * HD : odd * HD + half]
                high = turned[odd * HD + half : (odd + 1) * HD]
                both = jnp.concatenate(
                    [low * cosine - high * sine, high * cosine + low * sine], axis=0
                )
                query_ref[tile * per_tile + u, :HD, odd * rows : (odd + 1) * rows] = (
                    both * (HD**-0.5 * math.log2(math.e))
                ).astype(jnp.bfloat16)
            query_ref[tile * per_tile + u, HD:, :] = zeros
        cosine, sine = turns(first_row + lane)
        turned = result[:, heads * HD :].T
        low, high = turned[:half], turned[half:HD]
        keyvals = jnp.concatenate(
            [low * cosine - high * sine, high * cosine + low * sine, turned[HD:]], axis=0
        )
        suffix[tile, member] = keyvals.T.astype(jnp.bfloat16)
        for shift in range(1, members):
            suffix_copy(tile, shift, member).start()

    def relay(step):
        for side, slot, valid in ((0, z - step, z >= step), (1, z + step, z + step < n)):

            @pl.when(valid)
            def _(side=side, slot=slot):
                hop_copy(side, slot).wait_recv()

                @pl.when(onward[side])
                def _():
                    hop_copy(side, slot).start()

                for shift in range(1, members):
                    core_copy(slot, shift, member).start()

    own_window.wait()

    def wait_deal(shift, carry):
        dealt(shift).wait_recv()
        return carry

    lax.fori_loop(1, tok_count, wait_deal, 0)
    for side in range(2):

        @pl.when(onward[side])
        def _(side=side):
            hop_copy(side, z).start()

    for shift in range(1, members):
        core_copy(z, shift, member).start()

    for a, b in zip(range(chunks // 2), range(chunks // 2, chunks)):
        tile_copy(across, a, False, False).wait_recv()
        tile_copy(across, a, True, True).start()
        tile_copy(along, b, True, False).wait_recv()
        tile_copy(along, b, False, True).start()
    own_query.wait()
    own_keyval.wait()
    for shift in range(1, members):
        weight_copy(shift).wait_recv()
    project(mine)
    for a, b in zip(range(chunks // 2), range(chunks // 2, chunks)):
        tile_copy(across, b, False, False).wait_recv()
        tile_copy(along, a, True, False).wait_recv()
    relay(1)
    project(across)
    project(along)
    relay(2)
    for a, b in zip(range(chunks // 2), range(chunks // 2, chunks)):
        tile_copy(diagonal, a, True, True).wait_recv()
        tile_copy(diagonal, b, False, True).wait_recv()
    project(diagonal)
    for step in range(3, n):
        relay(step)

    for tile in range(kv_count):
        for shift in range(1, members):
            peer = lax.rem(member - shift + members, members)
            suffix_copy(tile, shift, peer).wait_recv()
    suffix_ref[...] = suffix[...]

    def settle(slot, carry):
        for shift in range(1, members):
            peer = lax.rem(member - shift + members, members)
            core_copy(slot, shift, peer).wait_recv()
            core_copy(slot, shift, member).wait_send()

        @pl.when(has_right & (slot <= z))
        def _():
            hop_copy(0, slot).wait_send()

        @pl.when(has_left & (slot >= z))
        def _():
            hop_copy(1, slot).wait_send()

        return carry

    lax.fori_loop(0, n, settle, 0)
    for c in range(chunks):
        tile_copy(mine, c, False, False).wait_send()
        tile_copy(mine, c, True, False).wait_send()
        if c < chunks // 2:
            tile_copy(across, c, True, True).wait_send()
        else:
            tile_copy(along, c, False, True).wait_send()
    for shift in range(1, members):
        weight_copy(shift).wait_send()
    for tile in range(kv_count):
        for shift in range(1, members):
            suffix_copy(tile, shift, member).wait_send()

    def deal_sent(shift, carry):
        deal_copy(shift).wait_send()
        return carry

    lax.fori_loop(1, tok_count, deal_sent, 0)


def front(
    lengths,
    hidden,
    gain,
    query_weight,
    keyval_weight,
    prefix,
    owner_count,
    kv_count,
    tok_count,
):
    rows, width = hidden.shape
    members = tok_count // kv_count
    columns = query_weight.shape[1]
    heads = members * columns // HD
    piece = prefix.shape[2]
    n, chunks = owner_count, 4
    cw = width // chunks
    bf16 = jnp.bfloat16
    dma = pltpu.SemaphoreType.DMA
    vmem = pl.BlockSpec(memory_space=pltpu.VMEM)
    hbm = pl.BlockSpec(memory_space=pltpu.HBM)
    return pl.pallas_call(
        lambda *refs: front_kernel(n, kv_count, tok_count, *refs),
        out_shape=[
            jax.ShapeDtypeStruct((kv_count * heads // 2, 2 * HD, 2 * rows), bf16),
            jax.ShapeDtypeStruct((kv_count, members, rows, 2 * HD), bf16),
            jax.ShapeDtypeStruct((n, tok_count, members, piece, 2 * HD), bf16),
        ],
        in_specs=[pl.BlockSpec(memory_space=pltpu.SMEM), vmem, vmem, hbm, hbm, hbm],
        out_specs=[vmem, vmem, hbm],
        scratch_shapes=[
            pltpu.VMEM((width, members * columns + 2 * HD), bf16),
            pltpu.VMEM((kv_count, chunks, rows, cw), bf16),
            pltpu.VMEM((kv_count, members, rows, 2 * HD), bf16),
            dma((3,)),
            dma((members,)),
            dma((members,)),
            dma((tok_count,)),
            dma((tok_count,)),
            dma((2, 2, chunks)),
            dma((kv_count, chunks)),
            dma((2, n)),
            dma((n,)),
            dma((n, members)),
            dma((n, members)),
            dma((kv_count, members)),
            dma((kv_count, members)),
        ],
        compiler_params=pltpu.CompilerParams(
            collective_id=0, has_side_effects=True, vmem_limit_bytes=VMEM_LIMIT
        ),
        name="front",
    )(lengths, hidden, gain, query_weight, keyval_weight, prefix)


def back_kernel(owner_count, kv_count, tok_count, parts, rows, vocab_step, *refs):
    lengths_ref, att_ref, hid_ref = refs[:3]
    outw = refs[3 : 3 + parts]
    (
        gain_ref,
        final_gain_ref,
        gate_hbm,
        up_hbm,
        down_hbm,
        head_hbm,
        out_ref,
        rms_ref,
        stat_ref,
        w_in,
        w_down,
        w_head,
        part_send,
        part_recv,
        half_send,
        half_recv,
        total,
        tiles,
        acc,
        act,
        shares,
        from_left,
        from_right,
        picked,
        picked_all,
        logits,
        stats,
        stats_all,
        load_sem,
        part_ss,
        part_rs,
        half_ss,
        half_rs,
        tile_ss,
        tile_rs,
        share_ss,
        left_rs,
        right_rs,
        pick_ss,
        pick_rs,
        stat_ss,
        stat_rs,
    ) = refs[3 + parts :]
    n = owner_count
    width = hid_ref.shape[1]
    chunks = tiles.shape[1]
    cw = width // chunks
    units = w_down.shape[0]
    tok = lax.axis_index("tok")
    z = lax.axis_index("req")
    members = tok_count // kv_count
    mine, member = tok // members, lax.rem(tok, members)
    across = mine + 1 - 2 * lax.rem(mine, 2)
    along = lax.rem(mine + 2, 4)
    diagonal = 3 - mine
    has_left, has_right = z > 0, z < n - 1
    left, right = lax.rem(z - 1 + n, n), lax.rem(z + 1, n)

    loads = [
        pltpu.make_async_copy(gate_hbm, w_in.at[:, :units], load_sem.at[0]),
        pltpu.make_async_copy(up_hbm, w_in.at[:, units:], load_sem.at[1]),
        pltpu.make_async_copy(down_hbm, w_down, load_sem.at[2]),
        pltpu.make_async_copy(head_hbm, w_head, load_sem.at[3]),
    ]
    for load in loads:
        load.start()

    barrier = pltpu.get_barrier_semaphore()

    def greet(shift, carry):
        pl.semaphore_signal(
            barrier,
            inc=1,
            device_id={"tok": lax.rem(tok + shift, tok_count)},
            device_id_type=MESH,
        )
        return carry

    lax.fori_loop(1, tok_count, greet, 0)

    @pl.when(has_left)
    def _():
        pl.semaphore_signal(barrier, inc=1, device_id={"req": left}, device_id_type=MESH)

    @pl.when(has_right)
    def _():
        pl.semaphore_signal(barrier, inc=1, device_id={"req": right}, device_id_type=MESH)

    def product(tile, c):
        at = pl.ds(pl.multiple_of(tile * rows, rows), rows)
        depth = att_ref.shape[1] // parts
        result = None
        for i in range(parts):
            term = jnp.dot(
                att_ref[at, i * depth : (i + 1) * depth],
                outw[i][:, c * cw : (c + 1) * cw],
                preferred_element_type=jnp.float32,
            )
            result = term if result is None else result + term
        return result

    def part_copy(kind, c):
        peer = across if c < chunks // 2 else along
        return pltpu.make_async_remote_copy(
            src_ref=part_send.at[kind, c],
            dst_ref=part_recv.at[kind, c],
            send_sem=part_ss.at[kind, c],
            recv_sem=part_rs.at[kind, c],
            device_id={"tok": peer * members + member},
            device_id_type=MESH,
        )

    def half_copy(c):
        peer = along if c < chunks // 2 else across
        return pltpu.make_async_remote_copy(
            src_ref=half_send.at[c],
            dst_ref=half_recv.at[c],
            send_sem=half_ss.at[c],
            recv_sem=half_rs.at[c],
            device_id={"tok": peer * members + member},
            device_id_type=MESH,
        )

    order = [c for pair in zip(range(chunks // 2), range(chunks // 2, chunks)) for c in pair]
    for c in order:
        part_send[0, c] = product(diagonal, c).astype(jnp.bfloat16)
    pl.semaphore_wait(
        barrier, tok_count - 1 + has_left.astype(jnp.int32) + has_right.astype(jnp.int32)
    )

    for c in order:
        part_copy(0, c).start()
    for c in order:
        near = across if c < chunks // 2 else along
        part_send[1, c] = product(near, c).astype(jnp.bfloat16)
        part_copy(1, c).start()
    for c in order:
        far = along if c < chunks // 2 else across
        here = product(far, c)
        part_copy(0, c).wait_recv()
        half_send[c] = (here + part_recv[0, c].astype(jnp.float32)).astype(jnp.bfloat16)
        half_copy(c).start()
    for c in order:
        cols = slice(c * cw, (c + 1) * cw)
        total[:, cols] = hid_ref[:, cols].astype(jnp.float32) + product(mine, c)
    squares = jnp.zeros((rows, 1), jnp.float32)
    for c in order:
        cols = slice(c * cw, (c + 1) * cw)
        part_copy(1, c).wait_recv()
        half_copy(c).wait_recv()
        summed = (
            total[:, cols]
            + part_recv[1, c].astype(jnp.float32)
            + half_recv[c].astype(jnp.float32)
        )
        middle = summed.astype(jnp.bfloat16).astype(jnp.float32)
        total[:, cols] = middle
        squares = squares + jnp.sum(middle * middle, axis=1, keepdims=True)
    scale = lax.rsqrt(squares / width + epsilon)

    def tile_copy(side, tile, c):
        return pltpu.make_async_remote_copy(
            src_ref=tiles.at[tile, c],
            dst_ref=tiles.at[tile, c],
            send_sem=tile_ss.at[side, tile, c],
            recv_sem=tile_rs.at[tile, c],
            device_id={"req": right if side == 0 else left},
            device_id_type=MESH,
        )

    def share_copy(side, tile, c):
        return pltpu.make_async_remote_copy(
            src_ref=shares.at[tile, c],
            dst_ref=(from_left if side == 0 else from_right).at[tile, c],
            send_sem=share_ss.at[tile, c],
            recv_sem=(left_rs if side == 0 else right_rs).at[tile, c],
            device_id={"req": right if side == 0 else left},
            device_id_type=MESH,
        )

    onward = (has_right, has_left)
    for c in range(chunks):
        cols = slice(c * cw, (c + 1) * cw)
        tiles[z, c] = (
            total[:, cols] * scale * gain_ref[cols].astype(jnp.float32).reshape(1, cw)
        ).astype(jnp.bfloat16)
        for side in range(2):

            @pl.when(onward[side])
            def _(side=side, c=c):
                tile_copy(side, z, c).start()

    for load in loads[:3]:
        load.wait()

    def step(s, carry):
        sources = (z - s, z + s)
        valid = (sources[0] >= 0, (sources[1] < n) & (s > 0))
        for c in range(chunks):
            for side in range(2):

                @pl.when(valid[side] & (s > 0))
                def _(side=side, c=c):
                    tile_copy(side, sources[side], c).wait_recv()

                    @pl.when(onward[side])
                    def _():
                        tile_copy(side, sources[side], c).start()

            for side in range(2):

                @pl.when(valid[side])
                def _(side=side, c=c):
                    term = jnp.dot(
                        tiles[sources[side], c],
                        w_in[c * cw : (c + 1) * cw, :],
                        preferred_element_type=jnp.float32,
                    )
                    if c == 0:
                        acc[side] = term
                    else:
                        acc[side] += term

        for side in range(2):

            @pl.when(valid[side])
            def _(side=side):
                gate_proj = acc[side, :, :units]
                lifted = acc[side, :, units:]
                act[...] = (gate_proj / (1.0 + jnp.exp(-gate_proj)) * lifted).astype(
                    jnp.bfloat16
                )
                starts_sum = (s > 0) & jnp.logical_not(onward[side])
                for c in range(chunks):
                    shares[sources[side], c] = jnp.dot(
                        act[...],
                        w_down[:, c * cw : (c + 1) * cw],
                        preferred_element_type=jnp.float32,
                    ).astype(jnp.bfloat16)

                    @pl.when(starts_sum)
                    def _(c=c):
                        share_copy(1 - side, sources[side], c).start()

        targets = (s - z, 2 * (n - 1) - s - z)
        coming = (
            has_left & (targets[0] >= z) & (targets[0] < n),
            has_right & (targets[1] <= z) & (targets[1] >= 0),
        )
        for side in range(2):

            @pl.when(coming[side])
            def _(side=side):
                target = targets[side]
                arrived = from_left if side == 0 else from_right
                for c in range(chunks):
                    share_copy(side, target, c).wait_recv()

                    @pl.when(target != z)
                    def _(c=c):
                        shares[target, c] = (
                            shares[target, c].astype(jnp.float32)
                            + arrived[target, c].astype(jnp.float32)
                        ).astype(jnp.bfloat16)
                        share_copy(side, target, c).start()

        return carry

    lax.fori_loop(0, 2 * n - 1, step, 0)

    sublane = lax.broadcasted_iota(jnp.int32, (8 * chunks, rows), 0)
    row = tok * rows + lax.broadcasted_iota(jnp.int32, (8 * chunks, rows), 1)
    picks = jnp.zeros((8 * chunks, rows), jnp.float32)
    for request, end in enumerate(request_ends(lengths_ref, lengths_ref.shape[1])):
        picks = jnp.where((lax.rem(sublane, 8) == request) & (row == end - 1), 1.0, picks)
    chosen = jnp.zeros((8 * chunks, cw), jnp.float32)
    for c in range(chunks):
        cols = slice(c * cw, (c + 1) * cw)
        total[:, cols] += shares[z, c].astype(jnp.float32)

        @pl.when(has_left)
        def _(c=c, cols=cols):
            total[:, cols] += from_left[z, c].astype(jnp.float32)

        @pl.when(has_right)
        def _(c=c, cols=cols):
            total[:, cols] += from_right[z, c].astype(jnp.float32)

        final = total[:, cols].astype(jnp.bfloat16)
        out_ref[:, cols] = final
        picker = jnp.where(sublane // 8 == c, picks, 0.0).astype(jnp.bfloat16)
        chosen = chosen + jnp.dot(picker, final, preferred_element_type=jnp.float32)
    picked[...] = chosen.astype(jnp.bfloat16)

    def spread(source, target, ss, rs):
        def peer_copy(shift):
            return pltpu.make_async_remote_copy(
                src_ref=source,
                dst_ref=target.at[tok],
                send_sem=ss.at[shift],
                recv_sem=rs.at[shift],
                device_id={"tok": lax.rem(tok + shift, tok_count)},
                device_id_type=MESH,
            )

        def begin(shift, carry):
            peer_copy(shift).start()
            return carry

        def end(shift, carry):
            peer_copy(shift).wait()
            return carry

        lax.fori_loop(1, tok_count, begin, 0)
        target[tok] = source[...]
        lax.fori_loop(1, tok_count, end, 0)

    spread(picked, picked_all, pick_ss, pick_rs)
    gathered = picked_all[0].astype(jnp.float32)
    for i in range(1, tok_count):
        gathered = gathered + picked_all[i].astype(jnp.float32)
    last = jnp.concatenate([gathered[8 * c : 8 * c + 8] for c in range(chunks)], axis=1)
    mean_square = jnp.mean(last * last, axis=1, keepdims=True)
    rms_ref[...] = jnp.broadcast_to(jnp.sqrt(mean_square + epsilon), rms_ref.shape)
    final_normed = (
        last * lax.rsqrt(mean_square + epsilon) * final_gain_ref[...].astype(jnp.float32).reshape(1, width)
    ).astype(jnp.bfloat16)
    final_normed = jnp.concatenate(
        [final_normed, jnp.zeros((128 - 8, width), jnp.bfloat16)], axis=0
    )
    loads[3].wait()

    def vocab(block, highest):
        at = pl.ds(pl.multiple_of(block * vocab_step, vocab_step), vocab_step)
        values = lax.dot_general(
            w_head[at, :],
            final_normed,
            (((1,), (1,)), ((), ())),
            preferred_element_type=jnp.float32,
        )
        logits[at, :] = values
        return jnp.maximum(highest, jnp.max(values, axis=0, keepdims=True))

    blocks = w_head.shape[0] // vocab_step
    top = lax.fori_loop(0, blocks, vocab, jnp.full((1, 128), -jnp.inf, jnp.float32))

    def exponents(block, amount):
        at = pl.ds(pl.multiple_of(block * vocab_step, vocab_step), vocab_step)
        return amount + jnp.sum(jnp.exp(logits[at, :] - top), axis=0, keepdims=True)

    amount = lax.fori_loop(0, blocks, exponents, jnp.zeros((1, 128), jnp.float32))
    stats[...] = jnp.concatenate([top, amount, jnp.zeros((6, 128), jnp.float32)], axis=0)
    spread(stats, stats_all, stat_ss, stat_rs)
    highest = stats_all[0, 0:1]
    for i in range(1, tok_count):
        highest = jnp.maximum(highest, stats_all[i, 0:1])
    amount = jnp.zeros((1, 128), jnp.float32)
    for i in range(tok_count):
        amount = amount + stats_all[i, 1:2] * jnp.exp(stats_all[i, 0:1] - highest)
    stat_ref[...] = jnp.concatenate(
        [highest, highest + jnp.log(amount), jnp.zeros((6, 128), jnp.float32)], axis=0
    )

    for c in order:
        part_copy(0, c).wait_send()
        part_copy(1, c).wait_send()
        half_copy(c).wait_send()

    def settle(tile, carry):
        for c in range(chunks):

            @pl.when(has_right & (tile <= z))
            def _(c=c):
                tile_copy(0, tile, c).wait_send()

            @pl.when(has_left & (tile >= z))
            def _(c=c):
                tile_copy(1, tile, c).wait_send()

            @pl.when(tile > z)
            def _(c=c):
                share_copy(0, tile, c).wait_send()

            @pl.when(tile < z)
            def _(c=c):
                share_copy(1, tile, c).wait_send()

        return carry

    lax.fori_loop(0, n, settle, 0)


def back(
    lengths,
    attended,
    hidden,
    out_parts,
    mlp_gain,
    final_gain,
    gate_weight,
    up_weight,
    down_weight,
    head_weight,
    owner_count,
    kv_count,
    tok_count,
):
    rows, width = hidden.shape
    units = down_weight.shape[0]
    vocab_rows = head_weight.shape[0]
    vocab_step = max(b for b in range(16, 513, 16) if vocab_rows % b == 0)
    n, chunks = owner_count, 4
    cw = width // chunks
    bf16, f32 = jnp.bfloat16, jnp.float32
    dma = pltpu.SemaphoreType.DMA
    vmem = pl.BlockSpec(memory_space=pltpu.VMEM)
    hbm = pl.BlockSpec(memory_space=pltpu.HBM)
    parts = len(out_parts)
    return pl.pallas_call(
        lambda *refs: back_kernel(n, kv_count, tok_count, parts, rows, vocab_step, *refs),
        out_shape=[
            jax.ShapeDtypeStruct((rows, width), bf16),
            jax.ShapeDtypeStruct((8, 128), f32),
            jax.ShapeDtypeStruct((8, 128), f32),
        ],
        in_specs=[pl.BlockSpec(memory_space=pltpu.SMEM)] + [vmem] * (4 + parts) + [hbm] * 4,
        out_specs=[vmem] * 3,
        scratch_shapes=[
            pltpu.VMEM((width, 2 * units), bf16),
            pltpu.VMEM((units, width), bf16),
            pltpu.VMEM((vocab_rows, width), bf16),
            pltpu.VMEM((2, chunks, rows, cw), bf16),
            pltpu.VMEM((2, chunks, rows, cw), bf16),
            pltpu.VMEM((chunks, rows, cw), bf16),
            pltpu.VMEM((chunks, rows, cw), bf16),
            pltpu.VMEM((rows, width), f32),
            pltpu.VMEM((n, chunks, rows, cw), bf16),
            pltpu.VMEM((2, rows, 2 * units), f32),
            pltpu.VMEM((rows, units), bf16),
            pltpu.VMEM((n, chunks, rows, cw), bf16),
            pltpu.VMEM((n, chunks, rows, cw), bf16),
            pltpu.VMEM((n, chunks, rows, cw), bf16),
            pltpu.VMEM((8 * chunks, cw), bf16),
            pltpu.VMEM((tok_count, 8 * chunks, cw), bf16),
            pltpu.VMEM((vocab_rows, 128), f32),
            pltpu.VMEM((8, 128), f32),
            pltpu.VMEM((tok_count, 8, 128), f32),
            dma((4,)),
            dma((2, chunks)),
            dma((2, chunks)),
            dma((chunks,)),
            dma((chunks,)),
            dma((2, n, chunks)),
            dma((n, chunks)),
            dma((n, chunks)),
            dma((n, chunks)),
            dma((n, chunks)),
            dma((tok_count,)),
            dma((tok_count,)),
            dma((tok_count,)),
            dma((tok_count,)),
        ],
        compiler_params=pltpu.CompilerParams(
            collective_id=1, has_side_effects=True, vmem_limit_bytes=VMEM_LIMIT
        ),
        name="back",
    )(
        lengths,
        attended,
        hidden,
        *out_parts,
        mlp_gain,
        final_gain,
        gate_weight,
        up_weight,
        down_weight,
        head_weight,
    )


def shards(
    hidden_in,
    suffix_len,
    prefix_of,
    prefix_slot,
    prefix_cache,
    attn_gain,
    query_weight,
    keyval_weight,
    out_weight,
    mlp_gain,
    gate_weight,
    up_weight,
    down_weight,
    final_gain,
    head_weight,
):
    tok_count = lax.axis_size("tok")
    owner_count = lax.axis_size("req")
    tok_rows = hidden_in.shape[0]
    own_rows = tok_rows * tok_count
    kv_count = keyval_weight.shape[0]
    members = tok_count // kv_count

    def shifted(array, shift):
        pairs = [
            (h * members + (g + shift) % members, h * members + g)
            for h in range(kv_count)
            for g in range(members)
        ]
        return lax.ppermute(array, "tok", pairs)

    out_parts = [out_weight] + [shifted(out_weight, s) for s in range(1, members)]
    window_block = prefix_cache.shape[2]
    queries, suffix, windows = front(
        suffix_len,
        hidden_in,
        attn_gain,
        query_weight,
        keyval_weight,
        prefix_cache.reshape(kv_count, members, window_block // members, 2 * HD),
        owner_count,
        kv_count,
        tok_count,
    )
    attended, suffix_cache = attention(
        suffix_len,
        prefix_of,
        prefix_slot,
        queries,
        windows.reshape(owner_count, window_block * tok_count, 2 * HD),
        suffix.reshape(own_rows, 2 * HD),
        tok_rows,
        kv_count,
        tok_count,
    )
    request_count = suffix_len.shape[1]
    final_state, spread, tail = back(
        suffix_len,
        attended,
        hidden_in,
        out_parts,
        mlp_gain,
        final_gain,
        gate_weight,
        up_weight,
        down_weight,
        head_weight,
        owner_count,
        kv_count,
        tok_count,
    )
    return (
        final_state,
        suffix_cache,
        spread[:request_count, 0][None, :],
        tail[0:1, :request_count],
        tail[1:2, :request_count],
    )


def solution(mesh):
    placed = (
        P(("req", "tok"), None),
        P("req", None),
        P("req", None),
        P(),
        P("req", None, "tok", None),
        P(),
        P(None, "tok"),
        P(),
        P("tok", None),
        P(),
        P(None, "req"),
        P(None, "req"),
        P("req", None),
        P(),
        P("tok", None),
    )
    return jax.shard_map(
        shards,
        mesh=mesh,
        in_specs=placed,
        out_specs=(
            P(("req", "tok"), None),
            P("req", "tok"),
            P("req", None),
            P("req", None),
            P("req", None),
        ),
        check_vma=False,
    )
```

```python
import math

import jax
import jax.numpy as jnp
from jax import lax
from jax.experimental import pallas as pl
from jax.experimental.pallas import tpu as pltpu
from jax.sharding import PartitionSpec as P

HD = 64
PRE_LEN = 16384
VMEM_LIMIT = 60 * 2**20


epsilon = 1e-05
neg_large = -1e30


def attention_kernel(
    most_rows,
    tok_count,
    kv_count,
    lengths_ref,
    chosen_ref,
    slot_ref,
    query_ref,
    windows,
    suffix_ref,
    out_ref,
    cache_ref,
    padded,
    band,
    band_values,
    score_scr,
):
    requests = lengths_ref.shape[1]
    units, unused, lanes = query_ref.shape
    rows = out_ref.shape[0] // kv_count
    unit_rows = out_ref.shape[0] // units
    per_tile = rows // unit_rows
    pairs = lanes // 2 // unit_rows
    window_len = windows.shape[1]
    own_rows = suffix_ref.shape[0]
    chunk = 256
    span = window_len + chunk
    tail_rows = band.shape[0] - window_len
    members = tok_count // kv_count
    tok = lax.axis_index("tok")
    member = lax.rem(tok, members)

    cache_width = cache_ref.shape[0]
    for first in range(0, own_rows, chunk):
        block = suffix_ref[first : first + chunk, :].astype(jnp.float32).T.astype(jnp.bfloat16)
        for place in range(2 * HD // cache_width):

            @pl.when(lax.rem(tok, 2 * HD // cache_width) == place)
            def _(place=place, first=first, block=block):
                cache_ref[:, first : first + chunk] = block[
                    place * cache_width : (place + 1) * cache_width
                ]

    padded[:own_rows, :] = suffix_ref[...]
    padded[own_rows:, :] = jnp.zeros((padded.shape[0] - own_rows, 2 * HD), jnp.bfloat16)

    def turned(block):
        return block.astype(jnp.float32).T[HD:].astype(jnp.bfloat16)

    def folded(values, fold):
        return fold(values.reshape(values.shape[0] // 8, 8, lanes), axis=0)

    def one_request(request, start):
        end = start + lengths_ref[0, request]
        slot = slot_ref[chosen_ref[0, request]]
        touched = jnp.int32(0)
        for tile in range(kv_count):
            first_row = (tile * members + member) * rows
            touched = touched + ((start < first_row + rows) & (end > first_row)).astype(jnp.int32)

        @pl.when(touched > 0)
        def _():
            for first in range(0, window_len, chunk):
                block = windows[slot, first : first + chunk, :]
                band[first : first + chunk, :] = block
                band_values[:, first : first + chunk] = turned(block)
            base = pl.multiple_of(start // 16 * 16, 16)
            lifted = padded[pl.ds(base, tail_rows + 16), :].astype(jnp.float32)
            lifted = pltpu.roll(lifted, tail_rows + 16 - (start - base), axis=0)
            for first in range(0, tail_rows, 128):
                block = lifted[first : first + 128].astype(jnp.bfloat16)
                at = slice(window_len + first, window_len + first + 128)
                band[at, :] = block
                band_values[:, at] = turned(block)

        def one_unit(unit, carry):
            tile = unit // per_tile
            first_row = (tile * members + member) * rows + lax.rem(unit, per_tile) * unit_rows

            @pl.when((start < first_row + unit_rows) & (end > first_row))
            def _():
                query = query_ref[unit]
                lane_row = first_row + lax.broadcasted_iota(jnp.int32, (1, lanes), 1) % unit_rows
                offset = lane_row - start
                low = pl.multiple_of((jnp.maximum(first_row, start) - start) // 128 * 128, 128)
                high = None
                for first in range(0, span, chunk):
                    scores = jnp.dot(
                        band[pl.ds(low + first, chunk), :],
                        query,
                        preferred_element_type=jnp.float32,
                    )
                    place = low + first + lax.broadcasted_iota(jnp.int32, (chunk, 1), 0)
                    if first == 0:
                        scores = jnp.where(place > offset, scores, neg_large)
                    if first == span - chunk:
                        scores = jnp.where(place <= offset + window_len, scores, neg_large)
                    score_scr[first : first + chunk, :] = scores
                    top = folded(scores, jnp.max)
                    high = top if high is None else jnp.maximum(high, top)
                high = jnp.max(high, axis=0, keepdims=True)
                total, acc = None, None
                for first in range(0, span, chunk):
                    weights = jnp.exp2(score_scr[first : first + chunk, :] - high)
                    part = folded(weights, jnp.sum)
                    term = jnp.dot(
                        band_values[:, pl.ds(low + first, chunk)],
                        weights.astype(jnp.bfloat16),
                        preferred_element_type=jnp.float32,
                    )
                    total = part if total is None else total + part
                    acc = term if acc is None else acc + term
                result = acc / jnp.sum(total, axis=0, keepdims=True)
                both = jnp.concatenate([result[:, : lanes // 2], result[:, lanes // 2 :]], axis=0)
                flat = both.T
                at = pl.ds(pl.multiple_of(unit * unit_rows, unit_rows), unit_rows)
                row = first_row + lax.broadcasted_iota(jnp.int32, (unit_rows, 1), 0)
                mine = (row >= start) & (row < end)
                for pair in range(pairs):
                    cols = slice(pair * 2 * HD, (pair + 1) * 2 * HD)
                    new = flat[pair * unit_rows : (pair + 1) * unit_rows]
                    old = out_ref[at, cols].astype(jnp.float32)
                    out_ref[at, cols] = jnp.where(mine, new, old).astype(jnp.bfloat16)

            return carry

        lax.fori_loop(0, units, one_unit, 0)
        return end

    lax.fori_loop(0, requests, one_request, 0)


def attention(lengths, chosen, prefix_slot, queries, windows, suffix, rows, kv_count, tok_count):
    units, unused, lanes = queries.shape
    heads = units * lanes // (kv_count * rows)
    own_rows = suffix.shape[0]
    window_len = windows.shape[1]
    cache_width = kv_count * 2 * HD // tok_count
    tail_rows = own_rows // 2 + 256
    smem = pl.BlockSpec(memory_space=pltpu.SMEM)
    vmem = pl.BlockSpec(memory_space=pltpu.VMEM)
    return pl.pallas_call(
        lambda *refs: attention_kernel(own_rows // 2, tok_count, kv_count, *refs),
        out_shape=[
            jax.ShapeDtypeStruct((kv_count * rows, heads * HD), jnp.bfloat16),
            jax.ShapeDtypeStruct((cache_width, own_rows), jnp.bfloat16),
        ],
        in_specs=[smem] * 3 + [vmem] * 3,
        out_specs=[vmem] * 2,
        scratch_shapes=[
            pltpu.VMEM((own_rows + tail_rows + 16, 2 * HD), jnp.bfloat16),
            pltpu.VMEM((window_len + tail_rows, 2 * HD), jnp.bfloat16),
            pltpu.VMEM((HD, window_len + tail_rows), jnp.bfloat16),
            pltpu.VMEM((window_len + 256, lanes), jnp.float32),
        ],
        compiler_params=pltpu.CompilerParams(vmem_limit_bytes=VMEM_LIMIT),
        cost_estimate=pl.CostEstimate(
            flops=10_000_000_000, bytes_accessed=8_000_000, transcendentals=10_000_000
        ),
        name="attention",
    )(lengths, chosen, prefix_slot, queries, windows, suffix)


MESH = pl.DeviceIdType.MESH


def request_ends(lengths_ref, count):
    ends, end = [], 0
    for request in range(count):
        end = end + lengths_ref[0, request]
        ends.append(end)
    return ends


def front_kernel(
    owner_count,
    kv_count,
    tok_count,
    lengths_ref,
    hid_ref,
    gain_ref,
    query_hbm,
    keyval_hbm,
    prefix_hbm,
    query_ref,
    suffix_ref,
    windows,
    weights,
    tiles,
    suffix,
    local_sem,
    weight_ss,
    weight_rs,
    deal_ss,
    deal_rs,
    tile_ss,
    tile_rs,
    hop_ss,
    hop_rs,
    core_ss,
    core_rs,
    suffix_ss,
    suffix_rs,
):
    n = owner_count
    rows, width = hid_ref.shape
    chunks = tiles.shape[1]
    cw = width // chunks
    columns = query_hbm.shape[1]
    tok = lax.axis_index("tok")
    z = lax.axis_index("req")
    members = tok_count // kv_count
    mine, member = tok // members, lax.rem(tok, members)
    across = mine + 1 - 2 * lax.rem(mine, 2)
    along = lax.rem(mine + 2, 4)
    diagonal = 3 - mine
    has_left, has_right = z > 0, z < n - 1
    left, right = lax.rem(z - 1 + n, n), lax.rem(z + 1, n)
    onward = (has_right, has_left)
    half = HD // 2
    heads = members * columns // HD

    own_query = pltpu.make_async_copy(query_hbm, weights.at[:, :columns], local_sem.at[0])
    own_keyval = pltpu.make_async_copy(
        keyval_hbm.at[mine], weights.at[:, members * columns :], local_sem.at[1]
    )
    own_window = pltpu.make_async_copy(
        prefix_hbm.at[mine, member], windows.at[z, tok, member], local_sem.at[2]
    )
    own_query.start()
    own_keyval.start()
    own_window.start()

    barrier = pltpu.get_barrier_semaphore()

    def greet(shift, carry):
        pl.semaphore_signal(
            barrier,
            inc=1,
            device_id={"tok": lax.rem(tok + shift, tok_count)},
            device_id_type=MESH,
        )
        return carry

    lax.fori_loop(1, tok_count, greet, 0)

    @pl.when(has_left)
    def _():
        pl.semaphore_signal(barrier, inc=1, device_id={"req": left}, device_id_type=MESH)

    @pl.when(has_right)
    def _():
        pl.semaphore_signal(barrier, inc=1, device_id={"req": right}, device_id_type=MESH)

    squares = jnp.zeros((rows, 1), jnp.float32)
    for c in range(chunks):
        part = hid_ref[:, c * cw : (c + 1) * cw].astype(jnp.float32)
        squares = squares + jnp.sum(part * part, axis=1, keepdims=True)
    scale = lax.rsqrt(squares / width + epsilon)
    for c in range(chunks):
        cols = slice(c * cw, (c + 1) * cw)
        tiles[mine, c] = (
            hid_ref[:, cols].astype(jnp.float32)
            * scale
            * gain_ref[cols].astype(jnp.float32).reshape(1, cw)
        ).astype(jnp.bfloat16)

    def deal_copy(shift):
        peer = lax.rem(tok + shift, tok_count)
        peer_member = lax.rem(peer, members)
        return pltpu.make_async_remote_copy(
            src_ref=prefix_hbm.at[peer // members, peer_member],
            dst_ref=windows.at[z, tok, peer_member],
            send_sem=deal_ss.at[shift],
            recv_sem=deal_rs.at[shift],
            device_id={"tok": peer},
            device_id_type=MESH,
        )

    def dealt(shift):
        return pltpu.make_async_remote_copy(
            src_ref=prefix_hbm.at[0, 0],
            dst_ref=windows.at[z, lax.rem(tok - shift + tok_count, tok_count), member],
            send_sem=deal_ss.at[shift],
            recv_sem=deal_rs.at[shift],
            device_id={"tok": lax.rem(tok + shift, tok_count)},
            device_id_type=MESH,
        )

    def weight_copy(shift):
        peer = lax.rem(member - shift + members, members)
        return pltpu.make_async_remote_copy(
            src_ref=query_hbm,
            dst_ref=weights.at[:, shift * columns : (shift + 1) * columns],
            send_sem=weight_ss.at[shift],
            recv_sem=weight_rs.at[shift],
            device_id={"tok": mine * members + peer},
            device_id_type=MESH,
        )

    def tile_copy(tile, c, to_along, relayed):
        return pltpu.make_async_remote_copy(
            src_ref=tiles.at[tile, c],
            dst_ref=tiles.at[tile, c],
            send_sem=tile_ss.at[int(to_along), int(relayed), c],
            recv_sem=tile_rs.at[tile, c],
            device_id={"tok": (along if to_along else across) * members + member},
            device_id_type=MESH,
        )

    def hop_copy(side, slot):
        return pltpu.make_async_remote_copy(
            src_ref=windows.at[slot, :, member],
            dst_ref=windows.at[slot, :, member],
            send_sem=hop_ss.at[side, slot],
            recv_sem=hop_rs.at[slot],
            device_id={"req": right if side == 0 else left},
            device_id_type=MESH,
        )

    def core_copy(slot, shift, place):
        return pltpu.make_async_remote_copy(
            src_ref=windows.at[slot, :, place],
            dst_ref=windows.at[slot, :, place],
            send_sem=core_ss.at[slot, shift],
            recv_sem=core_rs.at[slot, shift],
            device_id={"tok": mine * members + lax.rem(member + shift, members)},
            device_id_type=MESH,
        )

    def suffix_copy(tile, shift, place):
        return pltpu.make_async_remote_copy(
            src_ref=suffix.at[tile, place],
            dst_ref=suffix.at[tile, place],
            send_sem=suffix_ss.at[tile, shift],
            recv_sem=suffix_rs.at[tile, shift],
            device_id={"tok": mine * members + lax.rem(member + shift, members)},
            device_id_type=MESH,
        )

    pl.semaphore_wait(
        barrier, tok_count - 1 + has_left.astype(jnp.int32) + has_right.astype(jnp.int32)
    )

    def start_deal(shift, carry):
        deal_copy(shift).start()
        return carry

    lax.fori_loop(1, tok_count, start_deal, 0)
    order = [c for pair in zip(range(chunks // 2), range(chunks // 2, chunks)) for c in pair]
    for a, b in zip(range(chunks // 2), range(chunks // 2, chunks)):
        tile_copy(mine, a, False, False).start()
        tile_copy(mine, b, True, False).start()
    for a, b in zip(range(chunks // 2), range(chunks // 2, chunks)):
        tile_copy(mine, b, False, False).start()
        tile_copy(mine, a, True, False).start()
    for shift in range(1, members):
        weight_copy(shift).start()

    ends = request_ends(lengths_ref, lengths_ref.shape[1])

    def turns(row):
        start = jnp.zeros((1, rows), jnp.int32)
        for end in ends[:-1]:
            start = jnp.where(row >= end, end, start)
        positions = (row - start + PRE_LEN).astype(jnp.float32)
        level = lax.broadcasted_iota(jnp.int32, (half, 1), 0).astype(jnp.float32)
        angles = jnp.exp(level * (-2.0 * math.log(10000.0) / HD)) * positions
        return jnp.cos(angles), jnp.sin(angles)

    unit_rows = 2 * rows // heads
    per_tile = rows // unit_rows

    def project(tile):
        result = None
        for c in range(chunks):
            term = jnp.dot(
                tiles[tile, c],
                weights[c * cw : (c + 1) * cw, :],
                preferred_element_type=jnp.float32,
            )
            result = term if result is None else result + term
        first_row = (tile * members + member) * rows
        lane = lax.broadcasted_iota(jnp.int32, (1, rows), 1)
        zeros = jnp.zeros((HD, 2 * rows), jnp.bfloat16)
        for u in range(per_tile):
            cosine, sine = turns(first_row + u * unit_rows + lax.rem(lane, unit_rows))
            block = result[u * unit_rows : (u + 1) * unit_rows]
            turned = jnp.concatenate(
                [block[:, p * 2 * HD : (p + 1) * 2 * HD] for p in range(heads // 2)], axis=0
            ).T
            for odd in range(2):
                low = turned[odd * HD : odd * HD + half]
                high = turned[odd * HD + half : (odd + 1) * HD]
                both = jnp.concatenate(
                    [low * cosine - high * sine, high * cosine + low * sine], axis=0
                )
                query_ref[tile * per_tile + u, :HD, odd * rows : (odd + 1) * rows] = (
                    both * (HD**-0.5 * math.log2(math.e))
                ).astype(jnp.bfloat16)
            query_ref[tile * per_tile + u, HD:, :] = zeros
        cosine, sine = turns(first_row + lane)
        turned = result[:, heads * HD :].T
        low, high = turned[:half], turned[half:HD]
        keyvals = jnp.concatenate(
            [low * cosine - high * sine, high * cosine + low * sine, turned[HD:]], axis=0
        )
        suffix[tile, member] = keyvals.T.astype(jnp.bfloat16)
        for shift in range(1, members):
            suffix_copy(tile, shift, member).start()

    def relay(step):
        for side, slot, valid in ((0, z - step, z >= step), (1, z + step, z + step < n)):

            @pl.when(valid)
            def _(side=side, slot=slot):
                hop_copy(side, slot).wait_recv()

                @pl.when(onward[side])
                def _():
                    hop_copy(side, slot).start()

                for shift in range(1, members):
                    core_copy(slot, shift, member).start()

    own_window.wait()

    def wait_deal(shift, carry):
        dealt(shift).wait_recv()
        return carry

    lax.fori_loop(1, tok_count, wait_deal, 0)
    for side in range(2):

        @pl.when(onward[side])
        def _(side=side):
            hop_copy(side, z).start()

    for shift in range(1, members):
        core_copy(z, shift, member).start()

    for a, b in zip(range(chunks // 2), range(chunks // 2, chunks)):
        tile_copy(across, a, False, False).wait_recv()
        tile_copy(across, a, True, True).start()
        tile_copy(along, b, True, False).wait_recv()
        tile_copy(along, b, False, True).start()
    own_query.wait()
    own_keyval.wait()
    for shift in range(1, members):
        weight_copy(shift).wait_recv()
    project(mine)
    for a, b in zip(range(chunks // 2), range(chunks // 2, chunks)):
        tile_copy(across, b, False, False).wait_recv()
        tile_copy(along, a, True, False).wait_recv()
    relay(1)
    project(across)
    project(along)
    relay(2)
    for a, b in zip(range(chunks // 2), range(chunks // 2, chunks)):
        tile_copy(diagonal, a, True, True).wait_recv()
        tile_copy(diagonal, b, False, True).wait_recv()
    project(diagonal)
    for step in range(3, n):
        relay(step)

    for tile in range(kv_count):
        for shift in range(1, members):
            peer = lax.rem(member - shift + members, members)
            suffix_copy(tile, shift, peer).wait_recv()
    suffix_ref[...] = suffix[...]

    def settle(slot, carry):
        for shift in range(1, members):
            peer = lax.rem(member - shift + members, members)
            core_copy(slot, shift, peer).wait_recv()
            core_copy(slot, shift, member).wait_send()

        @pl.when(has_right & (slot <= z))
        def _():
            hop_copy(0, slot).wait_send()

        @pl.when(has_left & (slot >= z))
        def _():
            hop_copy(1, slot).wait_send()

        return carry

    lax.fori_loop(0, n, settle, 0)
    for c in range(chunks):
        tile_copy(mine, c, False, False).wait_send()
        tile_copy(mine, c, True, False).wait_send()
        if c < chunks // 2:
            tile_copy(across, c, True, True).wait_send()
        else:
            tile_copy(along, c, False, True).wait_send()
    for shift in range(1, members):
        weight_copy(shift).wait_send()
    for tile in range(kv_count):
        for shift in range(1, members):
            suffix_copy(tile, shift, member).wait_send()

    def deal_sent(shift, carry):
        deal_copy(shift).wait_send()
        return carry

    lax.fori_loop(1, tok_count, deal_sent, 0)


def front(
    lengths,
    hidden,
    gain,
    query_weight,
    keyval_weight,
    prefix,
    owner_count,
    kv_count,
    tok_count,
):
    rows, width = hidden.shape
    members = tok_count // kv_count
    columns = query_weight.shape[1]
    heads = members * columns // HD
    piece = prefix.shape[2]
    n, chunks = owner_count, 4
    cw = width // chunks
    bf16 = jnp.bfloat16
    dma = pltpu.SemaphoreType.DMA
    vmem = pl.BlockSpec(memory_space=pltpu.VMEM)
    hbm = pl.BlockSpec(memory_space=pltpu.HBM)
    return pl.pallas_call(
        lambda *refs: front_kernel(n, kv_count, tok_count, *refs),
        out_shape=[
            jax.ShapeDtypeStruct((kv_count * heads // 2, 2 * HD, 2 * rows), bf16),
            jax.ShapeDtypeStruct((kv_count, members, rows, 2 * HD), bf16),
            jax.ShapeDtypeStruct((n, tok_count, members, piece, 2 * HD), bf16),
        ],
        in_specs=[pl.BlockSpec(memory_space=pltpu.SMEM), vmem, vmem, hbm, hbm, hbm],
        out_specs=[vmem, vmem, hbm],
        scratch_shapes=[
            pltpu.VMEM((width, members * columns + 2 * HD), bf16),
            pltpu.VMEM((kv_count, chunks, rows, cw), bf16),
            pltpu.VMEM((kv_count, members, rows, 2 * HD), bf16),
            dma((3,)),
            dma((members,)),
            dma((members,)),
            dma((tok_count,)),
            dma((tok_count,)),
            dma((2, 2, chunks)),
            dma((kv_count, chunks)),
            dma((2, n)),
            dma((n,)),
            dma((n, members)),
            dma((n, members)),
            dma((kv_count, members)),
            dma((kv_count, members)),
        ],
        compiler_params=pltpu.CompilerParams(
            collective_id=0, has_side_effects=True, vmem_limit_bytes=VMEM_LIMIT
        ),
        name="front",
    )(lengths, hidden, gain, query_weight, keyval_weight, prefix)


def back_kernel(owner_count, kv_count, tok_count, parts, rows, vocab_step, *refs):
    lengths_ref, att_ref, hid_ref = refs[:3]
    outw = refs[3 : 3 + parts]
    (
        gain_ref,
        final_gain_ref,
        gate_hbm,
        up_hbm,
        down_hbm,
        head_hbm,
        out_ref,
        rms_ref,
        stat_ref,
        w_in,
        w_down,
        w_head,
        part_send,
        part_recv,
        half_send,
        half_recv,
        total,
        tiles,
        acc,
        act,
        shares,
        from_left,
        from_right,
        picked,
        picked_all,
        logits,
        stats,
        stats_all,
        load_sem,
        part_ss,
        part_rs,
        half_ss,
        half_rs,
        tile_ss,
        tile_rs,
        share_ss,
        left_rs,
        right_rs,
        pick_ss,
        pick_rs,
        stat_ss,
        stat_rs,
    ) = refs[3 + parts :]
    n = owner_count
    width = hid_ref.shape[1]
    chunks = tiles.shape[1] // 2
    cw = width // chunks
    units = w_down.shape[0]
    tok = lax.axis_index("tok")
    z = lax.axis_index("req")
    members = tok_count // kv_count
    mine, member = tok // members, lax.rem(tok, members)
    across = mine + 1 - 2 * lax.rem(mine, 2)
    along = lax.rem(mine + 2, 4)
    diagonal = 3 - mine
    has_left, has_right = z > 0, z < n - 1
    left, right = lax.rem(z - 1 + n, n), lax.rem(z + 1, n)

    loads = [
        pltpu.make_async_copy(gate_hbm, w_in.at[:, :units], load_sem.at[0]),
        pltpu.make_async_copy(up_hbm, w_in.at[:, units:], load_sem.at[1]),
        pltpu.make_async_copy(down_hbm, w_down, load_sem.at[2]),
        pltpu.make_async_copy(head_hbm, w_head, load_sem.at[3]),
    ]
    for load in loads:
        load.start()

    barrier = pltpu.get_barrier_semaphore()

    def greet(shift, carry):
        pl.semaphore_signal(
            barrier,
            inc=1,
            device_id={"tok": lax.rem(tok + shift, tok_count)},
            device_id_type=MESH,
        )
        return carry

    lax.fori_loop(1, tok_count, greet, 0)

    @pl.when(has_left)
    def _():
        pl.semaphore_signal(barrier, inc=1, device_id={"req": left}, device_id_type=MESH)

    @pl.when(has_right)
    def _():
        pl.semaphore_signal(barrier, inc=1, device_id={"req": right}, device_id_type=MESH)

    half = rows // 2
    pieces = 2 * chunks

    def product(tile, h, c):
        at = pl.ds(pl.multiple_of(tile * rows + h * half, half), half)
        depth = att_ref.shape[1] // parts
        result = None
        for i in range(parts):
            term = jnp.dot(
                att_ref[at, i * depth : (i + 1) * depth],
                outw[i][:, c * cw : (c + 1) * cw],
                preferred_element_type=jnp.float32,
            )
            result = term if result is None else result + term
        return result

    def part_copy(kind, h, c):
        peer = across if c < chunks // 2 else along
        j = h * chunks + c
        return pltpu.make_async_remote_copy(
            src_ref=part_send.at[kind, j],
            dst_ref=part_recv.at[kind, j],
            send_sem=part_ss.at[kind, j],
            recv_sem=part_rs.at[kind, j],
            device_id={"tok": peer * members + member},
            device_id_type=MESH,
        )

    def half_copy(h, c):
        peer = along if c < chunks // 2 else across
        j = h * chunks + c
        return pltpu.make_async_remote_copy(
            src_ref=half_send.at[j],
            dst_ref=half_recv.at[j],
            send_sem=half_ss.at[j],
            recv_sem=half_rs.at[j],
            device_id={"tok": peer * members + member},
            device_id_type=MESH,
        )

    order = [c for pair in zip(range(chunks // 2), range(chunks // 2, chunks)) for c in pair]

    def send_diagonal(h):
        for c in order:
            part_send[0, h * chunks + c] = product(diagonal, h, c).astype(jnp.bfloat16)
            if h > 0:
                part_copy(0, h, c).start()

    def send_near(h):
        for c in order:
            near = across if c < chunks // 2 else along
            part_send[1, h * chunks + c] = product(near, h, c).astype(jnp.bfloat16)
            part_copy(1, h, c).start()

    def send_far(h):
        for c in order:
            j = h * chunks + c
            far = along if c < chunks // 2 else across
            here = product(far, h, c)
            part_copy(0, h, c).wait_recv()
            half_send[j] = (here + part_recv[0, j].astype(jnp.float32)).astype(jnp.bfloat16)
            half_copy(h, c).start()

    def keep_own(h):
        at = slice(h * half, (h + 1) * half)
        for c in order:
            cols = slice(c * cw, (c + 1) * cw)
            total[at, cols] = hid_ref[at, cols].astype(jnp.float32) + product(mine, h, c)

    def tile_copy(side, tile, c):
        return pltpu.make_async_remote_copy(
            src_ref=tiles.at[tile, c],
            dst_ref=tiles.at[tile, c],
            send_sem=tile_ss.at[side, tile, c],
            recv_sem=tile_rs.at[tile, c],
            device_id={"req": right if side == 0 else left},
            device_id_type=MESH,
        )

    def share_copy(side, tile, c):
        return pltpu.make_async_remote_copy(
            src_ref=shares.at[tile, c],
            dst_ref=(from_left if side == 0 else from_right).at[tile, c],
            send_sem=share_ss.at[tile, c],
            recv_sem=(left_rs if side == 0 else right_rs).at[tile, c],
            device_id={"req": right if side == 0 else left},
            device_id_type=MESH,
        )

    onward = (has_right, has_left)

    def hand_on(h):
        at = slice(h * half, (h + 1) * half)
        squares = jnp.zeros((half, 1), jnp.float32)
        for c in order:
            j = h * chunks + c
            cols = slice(c * cw, (c + 1) * cw)
            part_copy(1, h, c).wait_recv()
            half_copy(h, c).wait_recv()
            summed = (
                total[at, cols]
                + part_recv[1, j].astype(jnp.float32)
                + half_recv[j].astype(jnp.float32)
            )
            middle = summed.astype(jnp.bfloat16).astype(jnp.float32)
            total[at, cols] = middle
            squares = squares + jnp.sum(middle * middle, axis=1, keepdims=True)
        scale = lax.rsqrt(squares / width + epsilon)
        for c in range(chunks):
            j = h * chunks + c
            cols = slice(c * cw, (c + 1) * cw)
            tiles[z, j] = (
                total[at, cols] * scale * gain_ref[cols].astype(jnp.float32).reshape(1, cw)
            ).astype(jnp.bfloat16)
            for side in range(2):

                @pl.when(onward[side])
                def _(side=side, j=j):
                    tile_copy(side, z, j).start()

    send_diagonal(0)
    pl.semaphore_wait(
        barrier, tok_count - 1 + has_left.astype(jnp.int32) + has_right.astype(jnp.int32)
    )
    for c in order:
        part_copy(0, 0, c).start()
    send_near(0)
    send_diagonal(1)
    send_far(0)
    send_near(1)
    keep_own(0)
    keep_own(1)
    hand_on(0)
    send_far(1)

    def pass_on(side, source, j):
        tile_copy(side, source, j).wait_recv()

        @pl.when(onward[side])
        def _():
            tile_copy(side, source, j).start()

    for j in range(chunks):
        for side, source, valid in ((0, left, has_left), (1, right, has_right)):

            @pl.when(valid)
            def _(side=side, source=source, j=j):
                pass_on(side, source, j)

    hand_on(1)
    for load in loads[:3]:
        load.wait()
    own_step = jnp.maximum(z, n - 1 - z) + 1

    def step(t, carry):
        s, h = t // 2, lax.rem(t, 2)
        own = s == own_step
        sources = (jnp.where(own, z, z - s), z + s)
        valid = (sources[0] >= 0, sources[1] < n)
        for c in range(chunks):
            j = h * chunks + c
            for side in range(2):

                @pl.when(valid[side] & jnp.logical_not(own) & (t > 2))
                def _(side=side, j=j):
                    pass_on(side, sources[side], j)

            for side in range(2):

                @pl.when(valid[side])
                def _(side=side, c=c, j=j):
                    term = jnp.dot(
                        tiles[sources[side], j],
                        w_in[c * cw : (c + 1) * cw, :],
                        preferred_element_type=jnp.float32,
                    )
                    if c == 0:
                        acc[side] = term
                    else:
                        acc[side] += term

        for side in range(2):

            @pl.when(valid[side])
            def _(side=side):
                gate_proj = acc[side, :, :units]
                lifted = acc[side, :, units:]
                act[...] = (gate_proj / (1.0 + jnp.exp(-gate_proj)) * lifted).astype(
                    jnp.bfloat16
                )
                starts_sum = jnp.logical_not(own) & jnp.logical_not(onward[side])
                for c in range(chunks):
                    j = h * chunks + c
                    shares[sources[side], j] = jnp.dot(
                        act[...],
                        w_down[:, c * cw : (c + 1) * cw],
                        preferred_element_type=jnp.float32,
                    ).astype(jnp.bfloat16)

                    @pl.when(starts_sum)
                    def _(j=j):
                        share_copy(1 - side, sources[side], j).start()

        targets = (s - z, 2 * (n - 1) - s - z)
        coming = (
            has_left & (targets[0] > z) & (targets[0] < n),
            has_right & (targets[1] < z) & (targets[1] >= 0),
        )
        for side in range(2):

            @pl.when(coming[side])
            def _(side=side):
                target = targets[side]
                arrived = from_left if side == 0 else from_right
                for c in range(chunks):
                    j = h * chunks + c
                    share_copy(side, target, j).wait_recv()
                    shares[target, j] = (
                        shares[target, j].astype(jnp.float32)
                        + arrived[target, j].astype(jnp.float32)
                    ).astype(jnp.bfloat16)
                    share_copy(side, target, j).start()

        return carry

    lax.fori_loop(2, 2 * (2 * n - 2), step, 0)

    sublane = lax.broadcasted_iota(jnp.int32, (8 * chunks, rows), 0)
    row = tok * rows + lax.broadcasted_iota(jnp.int32, (8 * chunks, rows), 1)
    picks = jnp.zeros((8 * chunks, rows), jnp.float32)
    for request, end in enumerate(request_ends(lengths_ref, lengths_ref.shape[1])):
        picks = jnp.where((lax.rem(sublane, 8) == request) & (row == end - 1), 1.0, picks)
    chosen = jnp.zeros((8 * chunks, cw), jnp.float32)
    for h in range(2):
        at = slice(h * half, (h + 1) * half)
        for c in range(chunks):
            cols = slice(c * cw, (c + 1) * cw)
            j = h * chunks + c
            total[at, cols] += shares[z, j].astype(jnp.float32)

            @pl.when(has_left)
            def _(at=at, cols=cols, j=j):
                share_copy(0, z, j).wait_recv()
                total[at, cols] += from_left[z, j].astype(jnp.float32)

            @pl.when(has_right)
            def _(at=at, cols=cols, j=j):
                share_copy(1, z, j).wait_recv()
                total[at, cols] += from_right[z, j].astype(jnp.float32)

    for c in range(chunks):
        cols = slice(c * cw, (c + 1) * cw)
        final = total[:, cols].astype(jnp.bfloat16)
        out_ref[:, cols] = final
        picker = jnp.where(sublane // 8 == c, picks, 0.0).astype(jnp.bfloat16)
        chosen = chosen + jnp.dot(picker, final, preferred_element_type=jnp.float32)
    picked[...] = chosen.astype(jnp.bfloat16)

    def spread(source, target, ss, rs):
        def peer_copy(shift):
            return pltpu.make_async_remote_copy(
                src_ref=source,
                dst_ref=target.at[tok],
                send_sem=ss.at[shift],
                recv_sem=rs.at[shift],
                device_id={"tok": lax.rem(tok + shift, tok_count)},
                device_id_type=MESH,
            )

        def begin(shift, carry):
            peer_copy(shift).start()
            return carry

        def end(shift, carry):
            peer_copy(shift).wait()
            return carry

        lax.fori_loop(1, tok_count, begin, 0)
        target[tok] = source[...]
        lax.fori_loop(1, tok_count, end, 0)

    spread(picked, picked_all, pick_ss, pick_rs)
    gathered = picked_all[0].astype(jnp.float32)
    for i in range(1, tok_count):
        gathered = gathered + picked_all[i].astype(jnp.float32)
    last = jnp.concatenate([gathered[8 * c : 8 * c + 8] for c in range(chunks)], axis=1)
    mean_square = jnp.mean(last * last, axis=1, keepdims=True)
    rms_ref[...] = jnp.broadcast_to(jnp.sqrt(mean_square + epsilon), rms_ref.shape)
    final_normed = (
        last * lax.rsqrt(mean_square + epsilon) * final_gain_ref[...].astype(jnp.float32).reshape(1, width)
    ).astype(jnp.bfloat16)
    final_normed = jnp.concatenate(
        [final_normed, jnp.zeros((128 - 8, width), jnp.bfloat16)], axis=0
    )
    loads[3].wait()

    def vocab(block, highest):
        at = pl.ds(pl.multiple_of(block * vocab_step, vocab_step), vocab_step)
        values = lax.dot_general(
            w_head[at, :],
            final_normed,
            (((1,), (1,)), ((), ())),
            preferred_element_type=jnp.float32,
        )
        logits[at, :] = values
        return jnp.maximum(highest, jnp.max(values, axis=0, keepdims=True))

    blocks = w_head.shape[0] // vocab_step
    top = lax.fori_loop(0, blocks, vocab, jnp.full((1, 128), -jnp.inf, jnp.float32))

    def exponents(block, amount):
        at = pl.ds(pl.multiple_of(block * vocab_step, vocab_step), vocab_step)
        return amount + jnp.sum(jnp.exp(logits[at, :] - top), axis=0, keepdims=True)

    amount = lax.fori_loop(0, blocks, exponents, jnp.zeros((1, 128), jnp.float32))
    stats[...] = jnp.concatenate([top, amount, jnp.zeros((6, 128), jnp.float32)], axis=0)
    spread(stats, stats_all, stat_ss, stat_rs)
    highest = stats_all[0, 0:1]
    for i in range(1, tok_count):
        highest = jnp.maximum(highest, stats_all[i, 0:1])
    amount = jnp.zeros((1, 128), jnp.float32)
    for i in range(tok_count):
        amount = amount + stats_all[i, 1:2] * jnp.exp(stats_all[i, 0:1] - highest)
    stat_ref[...] = jnp.concatenate(
        [highest, highest + jnp.log(amount), jnp.zeros((6, 128), jnp.float32)], axis=0
    )

    for h in range(2):
        for c in order:
            part_copy(0, h, c).wait_send()
            part_copy(1, h, c).wait_send()
            half_copy(h, c).wait_send()

    def settle(tile, carry):
        for c in range(pieces):

            @pl.when(has_right & (tile <= z))
            def _(c=c):
                tile_copy(0, tile, c).wait_send()

            @pl.when(has_left & (tile >= z))
            def _(c=c):
                tile_copy(1, tile, c).wait_send()

            @pl.when(tile > z)
            def _(c=c):
                share_copy(0, tile, c).wait_send()

            @pl.when(tile < z)
            def _(c=c):
                share_copy(1, tile, c).wait_send()

        return carry

    lax.fori_loop(0, n, settle, 0)


def back(
    lengths,
    attended,
    hidden,
    out_parts,
    mlp_gain,
    final_gain,
    gate_weight,
    up_weight,
    down_weight,
    head_weight,
    owner_count,
    kv_count,
    tok_count,
):
    rows, width = hidden.shape
    units = down_weight.shape[0]
    vocab_rows = head_weight.shape[0]
    vocab_step = max(b for b in range(16, 513, 16) if vocab_rows % b == 0)
    n, chunks = owner_count, 4
    cw = width // chunks
    bf16, f32 = jnp.bfloat16, jnp.float32
    dma = pltpu.SemaphoreType.DMA
    vmem = pl.BlockSpec(memory_space=pltpu.VMEM)
    hbm = pl.BlockSpec(memory_space=pltpu.HBM)
    parts = len(out_parts)
    return pl.pallas_call(
        lambda *refs: back_kernel(n, kv_count, tok_count, parts, rows, vocab_step, *refs),
        out_shape=[
            jax.ShapeDtypeStruct((rows, width), bf16),
            jax.ShapeDtypeStruct((8, 128), f32),
            jax.ShapeDtypeStruct((8, 128), f32),
        ],
        in_specs=[pl.BlockSpec(memory_space=pltpu.SMEM)] + [vmem] * (4 + parts) + [hbm] * 4,
        out_specs=[vmem] * 3,
        scratch_shapes=[
            pltpu.VMEM((width, 2 * units), bf16),
            pltpu.VMEM((units, width), bf16),
            pltpu.VMEM((vocab_rows, width), bf16),
            pltpu.VMEM((2, 2 * chunks, rows // 2, cw), bf16),
            pltpu.VMEM((2, 2 * chunks, rows // 2, cw), bf16),
            pltpu.VMEM((2 * chunks, rows // 2, cw), bf16),
            pltpu.VMEM((2 * chunks, rows // 2, cw), bf16),
            pltpu.VMEM((rows, width), f32),
            pltpu.VMEM((n, 2 * chunks, rows // 2, cw), bf16),
            pltpu.VMEM((2, rows // 2, 2 * units), f32),
            pltpu.VMEM((rows // 2, units), bf16),
            pltpu.VMEM((n, 2 * chunks, rows // 2, cw), bf16),
            pltpu.VMEM((n, 2 * chunks, rows // 2, cw), bf16),
            pltpu.VMEM((n, 2 * chunks, rows // 2, cw), bf16),
            pltpu.VMEM((8 * chunks, cw), bf16),
            pltpu.VMEM((tok_count, 8 * chunks, cw), bf16),
            pltpu.VMEM((vocab_rows, 128), f32),
            pltpu.VMEM((8, 128), f32),
            pltpu.VMEM((tok_count, 8, 128), f32),
            dma((4,)),
            dma((2, 2 * chunks)),
            dma((2, 2 * chunks)),
            dma((2 * chunks,)),
            dma((2 * chunks,)),
            dma((2, n, 2 * chunks)),
            dma((n, 2 * chunks)),
            dma((n, 2 * chunks)),
            dma((n, 2 * chunks)),
            dma((n, 2 * chunks)),
            dma((tok_count,)),
            dma((tok_count,)),
            dma((tok_count,)),
            dma((tok_count,)),
        ],
        compiler_params=pltpu.CompilerParams(
            collective_id=1, has_side_effects=True, vmem_limit_bytes=VMEM_LIMIT
        ),
        name="back",
    )(
        lengths,
        attended,
        hidden,
        *out_parts,
        mlp_gain,
        final_gain,
        gate_weight,
        up_weight,
        down_weight,
        head_weight,
    )


def shards(
    hidden_in,
    suffix_len,
    prefix_of,
    prefix_slot,
    prefix_cache,
    attn_gain,
    query_weight,
    keyval_weight,
    out_weight,
    mlp_gain,
    gate_weight,
    up_weight,
    down_weight,
    final_gain,
    head_weight,
):
    tok_count = lax.axis_size("tok")
    owner_count = lax.axis_size("req")
    tok_rows = hidden_in.shape[0]
    own_rows = tok_rows * tok_count
    kv_count = keyval_weight.shape[0]
    members = tok_count // kv_count

    def shifted(array, shift):
        pairs = [
            (h * members + (g + shift) % members, h * members + g)
            for h in range(kv_count)
            for g in range(members)
        ]
        return lax.ppermute(array, "tok", pairs)

    out_parts = [out_weight] + [shifted(out_weight, s) for s in range(1, members)]
    window_block = prefix_cache.shape[2]
    queries, suffix, windows = front(
        suffix_len,
        hidden_in,
        attn_gain,
        query_weight,
        keyval_weight,
        prefix_cache.reshape(kv_count, members, window_block // members, 2 * HD),
        owner_count,
        kv_count,
        tok_count,
    )
    attended, suffix_cache = attention(
        suffix_len,
        prefix_of,
        prefix_slot,
        queries,
        windows.reshape(owner_count, window_block * tok_count, 2 * HD),
        suffix.reshape(own_rows, 2 * HD),
        tok_rows,
        kv_count,
        tok_count,
    )
    request_count = suffix_len.shape[1]
    final_state, spread, tail = back(
        suffix_len,
        attended,
        hidden_in,
        out_parts,
        mlp_gain,
        final_gain,
        gate_weight,
        up_weight,
        down_weight,
        head_weight,
        owner_count,
        kv_count,
        tok_count,
    )
    return (
        final_state,
        suffix_cache.T,
        spread[:request_count, 0][None, :],
        tail[0:1, :request_count],
        tail[1:2, :request_count],
    )


def solution(mesh):
    placed = (
        P(("req", "tok"), None),
        P("req", None),
        P("req", None),
        P(),
        P("req", None, "tok", None),
        P(),
        P(None, "tok"),
        P(),
        P("tok", None),
        P(),
        P(None, "req"),
        P(None, "req"),
        P("req", None),
        P(),
        P("tok", None),
    )
    return jax.shard_map(
        shards,
        mesh=mesh,
        in_specs=placed,
        out_specs=(
            P(("req", "tok"), None),
            P("req", "tok"),
            P("req", None),
            P("req", None),
            P("req", None),
        ),
        check_vma=False,
    )
```

```python
import math

import jax
import jax.numpy as jnp
from jax import lax
from jax.experimental import pallas as pl
from jax.experimental.pallas import tpu as pltpu
from jax.sharding import PartitionSpec as P

HD = 64
PRE_LEN = 16384
VMEM_LIMIT = 60 * 2**20


epsilon = 1e-05
neg_large = -1e30


def attention_kernel(
    most_rows,
    tok_count,
    kv_count,
    lengths_ref,
    chosen_ref,
    slot_ref,
    query_ref,
    windows,
    suffix_ref,
    out_ref,
    cache_ref,
    padded,
    band,
    band_values,
    score_scr,
):
    requests = lengths_ref.shape[1]
    units, unused, narrow = query_ref.shape
    units, lanes = units // 2, 2 * narrow
    rows = out_ref.shape[0] // kv_count
    unit_rows = out_ref.shape[0] // units
    per_tile = rows // unit_rows
    step_rows = unit_rows // 2
    pairs = narrow // 2 // step_rows
    window_len = windows.shape[1]
    own_rows = suffix_ref.shape[0]
    chunk = 256
    span = window_len + chunk
    tail_rows = band.shape[0] - window_len
    members = tok_count // kv_count
    tok = lax.axis_index("tok")
    member = lax.rem(tok, members)

    cache_width = cache_ref.shape[0]
    for first in range(0, own_rows, chunk):
        block = suffix_ref[first : first + chunk, :].astype(jnp.float32).T.astype(jnp.bfloat16)
        for place in range(2 * HD // cache_width):

            @pl.when(lax.rem(tok, 2 * HD // cache_width) == place)
            def _(place=place, first=first, block=block):
                cache_ref[:, first : first + chunk] = block[
                    place * cache_width : (place + 1) * cache_width
                ]

    padded[:own_rows, :] = suffix_ref[...]
    padded[own_rows:, :] = jnp.zeros((padded.shape[0] - own_rows, 2 * HD), jnp.bfloat16)

    def turned(block):
        return block.astype(jnp.float32).T[HD:].astype(jnp.bfloat16)

    def folded(values, fold):
        return fold(values.reshape(values.shape[0] // 8, 8, lanes), axis=0)

    def one_request(request, start):
        end = start + lengths_ref[0, request]
        slot = slot_ref[chosen_ref[0, request]]
        touched = jnp.int32(0)
        for tile in range(kv_count):
            first_row = (tile * members + member) * rows
            touched = touched + ((start < first_row + rows) & (end > first_row)).astype(jnp.int32)

        @pl.when(touched > 0)
        def _():
            for first in range(0, window_len, chunk):
                block = windows[slot, first : first + chunk, :]
                band[first : first + chunk, :] = block
                band_values[:, first : first + chunk] = turned(block)
            base = pl.multiple_of(start // 16 * 16, 16)
            lifted = padded[pl.ds(base, tail_rows + 16), :].astype(jnp.float32)
            lifted = pltpu.roll(lifted, tail_rows + 16 - (start - base), axis=0)
            for first in range(0, tail_rows, 128):
                block = lifted[first : first + 128].astype(jnp.bfloat16)
                at = slice(window_len + first, window_len + first + 128)
                band[at, :] = block
                band_values[:, at] = turned(block)

        def one_unit(unit, carry):
            tile = unit // per_tile
            first_row = (tile * members + member) * rows + lax.rem(unit, per_tile) * unit_rows

            @pl.when((start < first_row + unit_rows) & (end > first_row))
            def _():
                query = jnp.concatenate([query_ref[2 * unit], query_ref[2 * unit + 1]], axis=1)
                lane = lax.broadcasted_iota(jnp.int32, (1, lanes), 1)
                lane_row = first_row + lane // narrow * step_rows + lane % step_rows
                offset = lane_row - start
                low = pl.multiple_of((jnp.maximum(first_row, start) - start) // 128 * 128, 128)
                high = None
                for first in range(0, span, chunk):
                    scores = jnp.dot(
                        band[pl.ds(low + first, chunk), :],
                        query,
                        preferred_element_type=jnp.float32,
                    )
                    place = low + first + lax.broadcasted_iota(jnp.int32, (chunk, 1), 0)
                    if first == 0:
                        scores = jnp.where(place > offset, scores, neg_large)
                    if first == span - chunk:
                        scores = jnp.where(place <= offset + window_len, scores, neg_large)
                    score_scr[first : first + chunk, :] = scores
                    top = folded(scores, jnp.max)
                    high = top if high is None else jnp.maximum(high, top)
                high = jnp.max(high, axis=0, keepdims=True)
                total, acc = None, None
                for first in range(0, span, chunk):
                    weights = jnp.exp2(score_scr[first : first + chunk, :] - high)
                    part = folded(weights, jnp.sum)
                    term = jnp.dot(
                        band_values[:, pl.ds(low + first, chunk)],
                        weights.astype(jnp.bfloat16),
                        preferred_element_type=jnp.float32,
                    )
                    total = part if total is None else total + part
                    acc = term if acc is None else acc + term
                result = acc / jnp.sum(total, axis=0, keepdims=True)
                for odd in range(2):
                    part = result[:, odd * narrow : (odd + 1) * narrow]
                    both = jnp.concatenate(
                        [part[:, : narrow // 2], part[:, narrow // 2 :]], axis=0
                    )
                    flat = both.T
                    at = pl.ds(
                        pl.multiple_of(unit * unit_rows + odd * step_rows, step_rows), step_rows
                    )
                    row = (
                        first_row
                        + odd * step_rows
                        + lax.broadcasted_iota(jnp.int32, (step_rows, 1), 0)
                    )
                    mine = (row >= start) & (row < end)
                    for pair in range(pairs):
                        cols = slice(pair * 2 * HD, (pair + 1) * 2 * HD)
                        new = flat[pair * step_rows : (pair + 1) * step_rows]
                        old = out_ref[at, cols].astype(jnp.float32)
                        out_ref[at, cols] = jnp.where(mine, new, old).astype(jnp.bfloat16)

            return carry

        lax.fori_loop(0, units, one_unit, 0)
        return end

    lax.fori_loop(0, requests, one_request, 0)


def attention(lengths, chosen, prefix_slot, queries, windows, suffix, rows, kv_count, tok_count):
    units, unused, lanes = queries.shape
    heads = units * lanes // (kv_count * rows)
    own_rows = suffix.shape[0]
    window_len = windows.shape[1]
    cache_width = kv_count * 2 * HD // tok_count
    tail_rows = own_rows // 2 + 256
    smem = pl.BlockSpec(memory_space=pltpu.SMEM)
    vmem = pl.BlockSpec(memory_space=pltpu.VMEM)
    return pl.pallas_call(
        lambda *refs: attention_kernel(own_rows // 2, tok_count, kv_count, *refs),
        out_shape=[
            jax.ShapeDtypeStruct((kv_count * rows, heads * HD), jnp.bfloat16),
            jax.ShapeDtypeStruct((cache_width, own_rows), jnp.bfloat16),
        ],
        in_specs=[smem] * 3 + [vmem] * 3,
        out_specs=[vmem] * 2,
        scratch_shapes=[
            pltpu.VMEM((own_rows + tail_rows + 16, 2 * HD), jnp.bfloat16),
            pltpu.VMEM((window_len + tail_rows, 2 * HD), jnp.bfloat16),
            pltpu.VMEM((HD, window_len + tail_rows), jnp.bfloat16),
            pltpu.VMEM((window_len + 256, 2 * lanes), jnp.float32),
        ],
        compiler_params=pltpu.CompilerParams(vmem_limit_bytes=VMEM_LIMIT),
        cost_estimate=pl.CostEstimate(
            flops=10_000_000_000, bytes_accessed=8_000_000, transcendentals=10_000_000
        ),
        name="attention",
    )(lengths, chosen, prefix_slot, queries, windows, suffix)


MESH = pl.DeviceIdType.MESH


def request_ends(lengths_ref, count):
    ends, end = [], 0
    for request in range(count):
        end = end + lengths_ref[0, request]
        ends.append(end)
    return ends


def front_kernel(
    owner_count,
    kv_count,
    tok_count,
    lengths_ref,
    hid_ref,
    gain_ref,
    query_hbm,
    keyval_hbm,
    prefix_hbm,
    query_ref,
    suffix_ref,
    windows,
    weights,
    tiles,
    suffix,
    local_sem,
    weight_ss,
    weight_rs,
    deal_ss,
    deal_rs,
    tile_ss,
    tile_rs,
    hop_ss,
    hop_rs,
    core_ss,
    core_rs,
    suffix_ss,
    suffix_rs,
):
    n = owner_count
    rows, width = hid_ref.shape
    chunks = tiles.shape[1]
    cw = width // chunks
    columns = query_hbm.shape[1]
    tok = lax.axis_index("tok")
    z = lax.axis_index("req")
    members = tok_count // kv_count
    mine, member = tok // members, lax.rem(tok, members)
    across = mine + 1 - 2 * lax.rem(mine, 2)
    along = lax.rem(mine + 2, 4)
    diagonal = 3 - mine
    has_left, has_right = z > 0, z < n - 1
    left, right = lax.rem(z - 1 + n, n), lax.rem(z + 1, n)
    onward = (has_right, has_left)
    half = HD // 2
    heads = members * columns // HD

    own_query = pltpu.make_async_copy(query_hbm, weights.at[:, :columns], local_sem.at[0])
    own_keyval = pltpu.make_async_copy(
        keyval_hbm.at[mine], weights.at[:, members * columns :], local_sem.at[1]
    )
    own_window = pltpu.make_async_copy(
        prefix_hbm.at[mine, member], windows.at[z, tok, member], local_sem.at[2]
    )
    own_query.start()
    own_keyval.start()
    own_window.start()

    barrier = pltpu.get_barrier_semaphore()

    def greet(shift, carry):
        pl.semaphore_signal(
            barrier,
            inc=1,
            device_id={"tok": lax.rem(tok + shift, tok_count)},
            device_id_type=MESH,
        )
        return carry

    lax.fori_loop(1, tok_count, greet, 0)

    @pl.when(has_left)
    def _():
        pl.semaphore_signal(barrier, inc=1, device_id={"req": left}, device_id_type=MESH)

    @pl.when(has_right)
    def _():
        pl.semaphore_signal(barrier, inc=1, device_id={"req": right}, device_id_type=MESH)

    squares = jnp.zeros((rows, 1), jnp.float32)
    for c in range(chunks):
        part = hid_ref[:, c * cw : (c + 1) * cw].astype(jnp.float32)
        squares = squares + jnp.sum(part * part, axis=1, keepdims=True)
    scale = lax.rsqrt(squares / width + epsilon)
    for c in range(chunks):
        cols = slice(c * cw, (c + 1) * cw)
        tiles[mine, c] = (
            hid_ref[:, cols].astype(jnp.float32)
            * scale
            * gain_ref[cols].astype(jnp.float32).reshape(1, cw)
        ).astype(jnp.bfloat16)

    def deal_copy(shift):
        peer = lax.rem(tok + shift, tok_count)
        peer_member = lax.rem(peer, members)
        return pltpu.make_async_remote_copy(
            src_ref=prefix_hbm.at[peer // members, peer_member],
            dst_ref=windows.at[z, tok, peer_member],
            send_sem=deal_ss.at[shift],
            recv_sem=deal_rs.at[shift],
            device_id={"tok": peer},
            device_id_type=MESH,
        )

    def dealt(shift):
        return pltpu.make_async_remote_copy(
            src_ref=prefix_hbm.at[0, 0],
            dst_ref=windows.at[z, lax.rem(tok - shift + tok_count, tok_count), member],
            send_sem=deal_ss.at[shift],
            recv_sem=deal_rs.at[shift],
            device_id={"tok": lax.rem(tok + shift, tok_count)},
            device_id_type=MESH,
        )

    def weight_copy(shift):
        peer = lax.rem(member - shift + members, members)
        return pltpu.make_async_remote_copy(
            src_ref=query_hbm,
            dst_ref=weights.at[:, shift * columns : (shift + 1) * columns],
            send_sem=weight_ss.at[shift],
            recv_sem=weight_rs.at[shift],
            device_id={"tok": mine * members + peer},
            device_id_type=MESH,
        )

    def tile_copy(tile, c, to_along, relayed):
        return pltpu.make_async_remote_copy(
            src_ref=tiles.at[tile, c],
            dst_ref=tiles.at[tile, c],
            send_sem=tile_ss.at[int(to_along), int(relayed), c],
            recv_sem=tile_rs.at[tile, c],
            device_id={"tok": (along if to_along else across) * members + member},
            device_id_type=MESH,
        )

    def hop_copy(side, slot):
        return pltpu.make_async_remote_copy(
            src_ref=windows.at[slot, :, member],
            dst_ref=windows.at[slot, :, member],
            send_sem=hop_ss.at[side, slot],
            recv_sem=hop_rs.at[slot],
            device_id={"req": right if side == 0 else left},
            device_id_type=MESH,
        )

    def core_copy(slot, shift, place):
        return pltpu.make_async_remote_copy(
            src_ref=windows.at[slot, :, place],
            dst_ref=windows.at[slot, :, place],
            send_sem=core_ss.at[slot, shift],
            recv_sem=core_rs.at[slot, shift],
            device_id={"tok": mine * members + lax.rem(member + shift, members)},
            device_id_type=MESH,
        )

    def suffix_copy(tile, shift, place):
        return pltpu.make_async_remote_copy(
            src_ref=suffix.at[tile, place],
            dst_ref=suffix.at[tile, place],
            send_sem=suffix_ss.at[tile, shift],
            recv_sem=suffix_rs.at[tile, shift],
            device_id={"tok": mine * members + lax.rem(member + shift, members)},
            device_id_type=MESH,
        )

    pl.semaphore_wait(
        barrier, tok_count - 1 + has_left.astype(jnp.int32) + has_right.astype(jnp.int32)
    )

    def start_deal(shift, carry):
        deal_copy(shift).start()
        return carry

    lax.fori_loop(1, tok_count, start_deal, 0)
    order = [c for pair in zip(range(chunks // 2), range(chunks // 2, chunks)) for c in pair]
    for a, b in zip(range(chunks // 2), range(chunks // 2, chunks)):
        tile_copy(mine, a, False, False).start()
        tile_copy(mine, b, True, False).start()
    for a, b in zip(range(chunks // 2), range(chunks // 2, chunks)):
        tile_copy(mine, b, False, False).start()
        tile_copy(mine, a, True, False).start()
    for shift in range(1, members):
        weight_copy(shift).start()

    ends = request_ends(lengths_ref, lengths_ref.shape[1])

    def turns(row):
        start = jnp.zeros((1, rows), jnp.int32)
        for end in ends[:-1]:
            start = jnp.where(row >= end, end, start)
        positions = (row - start + PRE_LEN).astype(jnp.float32)
        level = lax.broadcasted_iota(jnp.int32, (half, 1), 0).astype(jnp.float32)
        angles = jnp.exp(level * (-2.0 * math.log(10000.0) / HD)) * positions
        return jnp.cos(angles), jnp.sin(angles)

    unit_rows = 2 * rows // heads
    per_tile = rows // unit_rows

    def project(tile):
        result = None
        for c in range(chunks):
            term = jnp.dot(
                tiles[tile, c],
                weights[c * cw : (c + 1) * cw, :],
                preferred_element_type=jnp.float32,
            )
            result = term if result is None else result + term
        first_row = (tile * members + member) * rows
        lane = lax.broadcasted_iota(jnp.int32, (1, rows), 1)
        zeros = jnp.zeros((HD, 2 * rows), jnp.bfloat16)
        for u in range(per_tile):
            cosine, sine = turns(first_row + u * unit_rows + lax.rem(lane, unit_rows))
            block = result[u * unit_rows : (u + 1) * unit_rows]
            turned = jnp.concatenate(
                [block[:, p * 2 * HD : (p + 1) * 2 * HD] for p in range(heads // 2)], axis=0
            ).T
            for odd in range(2):
                low = turned[odd * HD : odd * HD + half]
                high = turned[odd * HD + half : (odd + 1) * HD]
                both = jnp.concatenate(
                    [low * cosine - high * sine, high * cosine + low * sine], axis=0
                )
                query_ref[tile * per_tile + u, :HD, odd * rows : (odd + 1) * rows] = (
                    both * (HD**-0.5 * math.log2(math.e))
                ).astype(jnp.bfloat16)
            query_ref[tile * per_tile + u, HD:, :] = zeros
        cosine, sine = turns(first_row + lane)
        turned = result[:, heads * HD :].T
        low, high = turned[:half], turned[half:HD]
        keyvals = jnp.concatenate(
            [low * cosine - high * sine, high * cosine + low * sine, turned[HD:]], axis=0
        )
        suffix[tile, member] = keyvals.T.astype(jnp.bfloat16)
        for shift in range(1, members):
            suffix_copy(tile, shift, member).start()

    def relay(step):
        for side, slot, valid in ((0, z - step, z >= step), (1, z + step, z + step < n)):

            @pl.when(valid)
            def _(side=side, slot=slot):
                hop_copy(side, slot).wait_recv()

                @pl.when(onward[side])
                def _():
                    hop_copy(side, slot).start()

                for shift in range(1, members):
                    core_copy(slot, shift, member).start()

    own_window.wait()

    def wait_deal(shift, carry):
        dealt(shift).wait_recv()
        return carry

    lax.fori_loop(1, tok_count, wait_deal, 0)
    for side in range(2):

        @pl.when(onward[side])
        def _(side=side):
            hop_copy(side, z).start()

    for shift in range(1, members):
        core_copy(z, shift, member).start()

    for a, b in zip(range(chunks // 2), range(chunks // 2, chunks)):
        tile_copy(across, a, False, False).wait_recv()
        tile_copy(across, a, True, True).start()
        tile_copy(along, b, True, False).wait_recv()
        tile_copy(along, b, False, True).start()
    own_query.wait()
    own_keyval.wait()
    for shift in range(1, members):
        weight_copy(shift).wait_recv()
    project(mine)
    for a, b in zip(range(chunks // 2), range(chunks // 2, chunks)):
        tile_copy(across, b, False, False).wait_recv()
        tile_copy(along, a, True, False).wait_recv()
    relay(1)
    project(across)
    project(along)
    relay(2)
    for a, b in zip(range(chunks // 2), range(chunks // 2, chunks)):
        tile_copy(diagonal, a, True, True).wait_recv()
        tile_copy(diagonal, b, False, True).wait_recv()
    project(diagonal)
    for step in range(3, n):
        relay(step)

    for tile in range(kv_count):
        for shift in range(1, members):
            peer = lax.rem(member - shift + members, members)
            suffix_copy(tile, shift, peer).wait_recv()
    suffix_ref[...] = suffix[...]

    def settle(slot, carry):
        for shift in range(1, members):
            peer = lax.rem(member - shift + members, members)
            core_copy(slot, shift, peer).wait_recv()
            core_copy(slot, shift, member).wait_send()

        @pl.when(has_right & (slot <= z))
        def _():
            hop_copy(0, slot).wait_send()

        @pl.when(has_left & (slot >= z))
        def _():
            hop_copy(1, slot).wait_send()

        return carry

    lax.fori_loop(0, n, settle, 0)
    for c in range(chunks):
        tile_copy(mine, c, False, False).wait_send()
        tile_copy(mine, c, True, False).wait_send()
        if c < chunks // 2:
            tile_copy(across, c, True, True).wait_send()
        else:
            tile_copy(along, c, False, True).wait_send()
    for shift in range(1, members):
        weight_copy(shift).wait_send()
    for tile in range(kv_count):
        for shift in range(1, members):
            suffix_copy(tile, shift, member).wait_send()

    def deal_sent(shift, carry):
        deal_copy(shift).wait_send()
        return carry

    lax.fori_loop(1, tok_count, deal_sent, 0)


def front(
    lengths,
    hidden,
    gain,
    query_weight,
    keyval_weight,
    prefix,
    owner_count,
    kv_count,
    tok_count,
):
    rows, width = hidden.shape
    members = tok_count // kv_count
    columns = query_weight.shape[1]
    heads = members * columns // HD
    piece = prefix.shape[2]
    n, chunks = owner_count, 4
    cw = width // chunks
    bf16 = jnp.bfloat16
    dma = pltpu.SemaphoreType.DMA
    vmem = pl.BlockSpec(memory_space=pltpu.VMEM)
    hbm = pl.BlockSpec(memory_space=pltpu.HBM)
    return pl.pallas_call(
        lambda *refs: front_kernel(n, kv_count, tok_count, *refs),
        out_shape=[
            jax.ShapeDtypeStruct((kv_count * heads // 2, 2 * HD, 2 * rows), bf16),
            jax.ShapeDtypeStruct((kv_count, members, rows, 2 * HD), bf16),
            jax.ShapeDtypeStruct((n, tok_count, members, piece, 2 * HD), bf16),
        ],
        in_specs=[pl.BlockSpec(memory_space=pltpu.SMEM), vmem, vmem, hbm, hbm, hbm],
        out_specs=[vmem, vmem, hbm],
        scratch_shapes=[
            pltpu.VMEM((width, members * columns + 2 * HD), bf16),
            pltpu.VMEM((kv_count, chunks, rows, cw), bf16),
            pltpu.VMEM((kv_count, members, rows, 2 * HD), bf16),
            dma((3,)),
            dma((members,)),
            dma((members,)),
            dma((tok_count,)),
            dma((tok_count,)),
            dma((2, 2, chunks)),
            dma((kv_count, chunks)),
            dma((2, n)),
            dma((n,)),
            dma((n, members)),
            dma((n, members)),
            dma((kv_count, members)),
            dma((kv_count, members)),
        ],
        compiler_params=pltpu.CompilerParams(
            collective_id=0, has_side_effects=True, vmem_limit_bytes=VMEM_LIMIT
        ),
        name="front",
    )(lengths, hidden, gain, query_weight, keyval_weight, prefix)


def back_kernel(owner_count, kv_count, tok_count, parts, rows, vocab_step, *refs):
    lengths_ref, att_ref, hid_ref = refs[:3]
    outw = refs[3 : 3 + parts]
    (
        gain_ref,
        final_gain_ref,
        gate_hbm,
        up_hbm,
        down_hbm,
        head_hbm,
        out_ref,
        stat_ref,
        w_in,
        w_down,
        w_head,
        part_send,
        part_recv,
        half_send,
        half_recv,
        total,
        tiles,
        acc,
        act,
        shares,
        from_left,
        from_right,
        picked,
        picked_all,
        logits,
        stats,
        stats_all,
        load_sem,
        part_ss,
        part_rs,
        half_ss,
        half_rs,
        tile_ss,
        tile_rs,
        share_ss,
        left_rs,
        right_rs,
        pick_ss,
        pick_rs,
        stat_ss,
        stat_rs,
    ) = refs[3 + parts :]
    n = owner_count
    width = hid_ref.shape[1]
    chunks = tiles.shape[1] // 2
    cw = width // chunks
    units = w_down.shape[0]
    tok = lax.axis_index("tok")
    z = lax.axis_index("req")
    members = tok_count // kv_count
    mine, member = tok // members, lax.rem(tok, members)
    across = mine + 1 - 2 * lax.rem(mine, 2)
    along = lax.rem(mine + 2, 4)
    diagonal = 3 - mine
    has_left, has_right = z > 0, z < n - 1
    left, right = lax.rem(z - 1 + n, n), lax.rem(z + 1, n)

    loads = [
        pltpu.make_async_copy(gate_hbm, w_in.at[:, :units], load_sem.at[0]),
        pltpu.make_async_copy(up_hbm, w_in.at[:, units:], load_sem.at[1]),
        pltpu.make_async_copy(down_hbm, w_down, load_sem.at[2]),
        pltpu.make_async_copy(head_hbm, w_head, load_sem.at[3]),
    ]
    for load in loads:
        load.start()

    barrier = pltpu.get_barrier_semaphore()

    def greet(shift, carry):
        pl.semaphore_signal(
            barrier,
            inc=1,
            device_id={"tok": lax.rem(tok + shift, tok_count)},
            device_id_type=MESH,
        )
        return carry

    lax.fori_loop(1, tok_count, greet, 0)

    @pl.when(has_left)
    def _():
        pl.semaphore_signal(barrier, inc=1, device_id={"req": left}, device_id_type=MESH)

    @pl.when(has_right)
    def _():
        pl.semaphore_signal(barrier, inc=1, device_id={"req": right}, device_id_type=MESH)

    half = rows // 2
    pieces = 2 * chunks

    def product(tile, h, c):
        at = pl.ds(pl.multiple_of(tile * rows + h * half, half), half)
        depth = att_ref.shape[1] // parts
        result = None
        for i in range(parts):
            term = jnp.dot(
                att_ref[at, i * depth : (i + 1) * depth],
                outw[i][:, c * cw : (c + 1) * cw],
                preferred_element_type=jnp.float32,
            )
            result = term if result is None else result + term
        return result

    def part_copy(kind, h, c):
        peer = across if c < chunks // 2 else along
        j = h * chunks + c
        return pltpu.make_async_remote_copy(
            src_ref=part_send.at[kind, j],
            dst_ref=part_recv.at[kind, j],
            send_sem=part_ss.at[kind, j],
            recv_sem=part_rs.at[kind, j],
            device_id={"tok": peer * members + member},
            device_id_type=MESH,
        )

    def half_copy(h, c):
        peer = along if c < chunks // 2 else across
        j = h * chunks + c
        return pltpu.make_async_remote_copy(
            src_ref=half_send.at[j],
            dst_ref=half_recv.at[j],
            send_sem=half_ss.at[j],
            recv_sem=half_rs.at[j],
            device_id={"tok": peer * members + member},
            device_id_type=MESH,
        )

    order = [c for pair in zip(range(chunks // 2), range(chunks // 2, chunks)) for c in pair]

    def send_diagonal(h):
        for c in order:
            part_send[0, h * chunks + c] = product(diagonal, h, c).astype(jnp.bfloat16)
            if h > 0:
                part_copy(0, h, c).start()

    def send_near(h):
        for c in order:
            near = across if c < chunks // 2 else along
            part_send[1, h * chunks + c] = product(near, h, c).astype(jnp.bfloat16)
            part_copy(1, h, c).start()

    def send_far(h):
        for c in order:
            j = h * chunks + c
            far = along if c < chunks // 2 else across
            here = product(far, h, c)
            part_copy(0, h, c).wait_recv()
            half_send[j] = (here + part_recv[0, j].astype(jnp.float32)).astype(jnp.bfloat16)
            half_copy(h, c).start()

    def keep_own(h):
        at = slice(h * half, (h + 1) * half)
        for c in order:
            cols = slice(c * cw, (c + 1) * cw)
            total[at, cols] = hid_ref[at, cols].astype(jnp.float32) + product(mine, h, c)

    def tile_copy(side, tile, c):
        return pltpu.make_async_remote_copy(
            src_ref=tiles.at[tile, c],
            dst_ref=tiles.at[tile, c],
            send_sem=tile_ss.at[side, tile, c],
            recv_sem=tile_rs.at[tile, c],
            device_id={"req": right if side == 0 else left},
            device_id_type=MESH,
        )

    def share_copy(side, tile, c):
        return pltpu.make_async_remote_copy(
            src_ref=shares.at[tile, c],
            dst_ref=(from_left if side == 0 else from_right).at[tile, c],
            send_sem=share_ss.at[tile, c],
            recv_sem=(left_rs if side == 0 else right_rs).at[tile, c],
            device_id={"req": right if side == 0 else left},
            device_id_type=MESH,
        )

    onward = (has_right, has_left)

    def hand_on(h):
        at = slice(h * half, (h + 1) * half)
        squares = jnp.zeros((half, 1), jnp.float32)
        for c in order:
            j = h * chunks + c
            cols = slice(c * cw, (c + 1) * cw)
            part_copy(1, h, c).wait_recv()
            half_copy(h, c).wait_recv()
            summed = (
                total[at, cols]
                + part_recv[1, j].astype(jnp.float32)
                + half_recv[j].astype(jnp.float32)
            )
            middle = summed.astype(jnp.bfloat16).astype(jnp.float32)
            total[at, cols] = middle
            squares = squares + jnp.sum(middle * middle, axis=1, keepdims=True)
        scale = lax.rsqrt(squares / width + epsilon)
        for c in range(chunks):
            j = h * chunks + c
            cols = slice(c * cw, (c + 1) * cw)
            tiles[z, j] = (
                total[at, cols] * scale * gain_ref[cols].astype(jnp.float32).reshape(1, cw)
            ).astype(jnp.bfloat16)
            for side in range(2):

                @pl.when(onward[side])
                def _(side=side, j=j):
                    tile_copy(side, z, j).start()

    send_diagonal(0)
    pl.semaphore_wait(
        barrier, tok_count - 1 + has_left.astype(jnp.int32) + has_right.astype(jnp.int32)
    )
    for c in order:
        part_copy(0, 0, c).start()
    send_near(0)
    send_diagonal(1)
    send_far(0)
    send_near(1)
    keep_own(0)
    keep_own(1)
    hand_on(0)
    send_far(1)

    def pass_on(side, source, j):
        tile_copy(side, source, j).wait_recv()

        @pl.when(onward[side])
        def _():
            tile_copy(side, source, j).start()

    for j in range(chunks):
        for side, source, valid in ((0, left, has_left), (1, right, has_right)):

            @pl.when(valid)
            def _(side=side, source=source, j=j):
                pass_on(side, source, j)

    hand_on(1)
    for load in loads[:3]:
        load.wait()
    own_step = jnp.maximum(z, n - 1 - z) + 1

    def step(t, carry):
        s, h = t // 2, lax.rem(t, 2)
        own = s == own_step
        sources = (jnp.where(own, z, z - s), z + s)
        valid = (sources[0] >= 0, sources[1] < n)
        for c in range(chunks):
            j = h * chunks + c
            for side in range(2):

                @pl.when(valid[side] & jnp.logical_not(own) & (t > 2))
                def _(side=side, j=j):
                    pass_on(side, sources[side], j)

            for side in range(2):

                @pl.when(valid[side])
                def _(side=side, c=c, j=j):
                    term = jnp.dot(
                        tiles[sources[side], j],
                        w_in[c * cw : (c + 1) * cw, :],
                        preferred_element_type=jnp.float32,
                    )
                    if c == 0:
                        acc[side] = term
                    else:
                        acc[side] += term

        for side in range(2):

            @pl.when(valid[side])
            def _(side=side):
                gate_proj = acc[side, :, :units]
                lifted = acc[side, :, units:]
                act[...] = (gate_proj / (1.0 + jnp.exp(-gate_proj)) * lifted).astype(
                    jnp.bfloat16
                )
                starts_sum = jnp.logical_not(own) & jnp.logical_not(onward[side])
                for c in range(chunks):
                    j = h * chunks + c
                    shares[sources[side], j] = jnp.dot(
                        act[...],
                        w_down[:, c * cw : (c + 1) * cw],
                        preferred_element_type=jnp.float32,
                    ).astype(jnp.bfloat16)

                    @pl.when(starts_sum)
                    def _(j=j):
                        share_copy(1 - side, sources[side], j).start()

        begun = (t - z, t - (n - 1 - z))
        targets = (begun[0] // 2, n - 1 - begun[1] // 2)
        coming = (
            has_left & (begun[0] >= 0) & (targets[0] > z) & (targets[0] < n),
            has_right & (begun[1] >= 0) & (targets[1] < z) & (targets[1] >= 0),
        )
        for side in range(2):

            @pl.when(coming[side])
            def _(side=side):
                target = targets[side]
                arrived = from_left if side == 0 else from_right
                for c in range(chunks):
                    j = lax.rem(begun[side], 2) * chunks + c
                    share_copy(side, target, j).wait_recv()
                    shares[target, j] = (
                        shares[target, j].astype(jnp.float32)
                        + arrived[target, j].astype(jnp.float32)
                    ).astype(jnp.bfloat16)
                    share_copy(side, target, j).start()

        return carry

    lax.fori_loop(2, max(2 * n + 2, 3 * n - 2), step, 0)

    sublane = lax.broadcasted_iota(jnp.int32, (8 * chunks, rows), 0)
    row = tok * rows + lax.broadcasted_iota(jnp.int32, (8 * chunks, rows), 1)
    picks = jnp.zeros((8 * chunks, rows), jnp.float32)
    for request, end in enumerate(request_ends(lengths_ref, lengths_ref.shape[1])):
        picks = jnp.where((lax.rem(sublane, 8) == request) & (row == end - 1), 1.0, picks)
    chosen = jnp.zeros((8 * chunks, cw), jnp.float32)
    for h in range(2):
        at = slice(h * half, (h + 1) * half)
        for c in range(chunks):
            cols = slice(c * cw, (c + 1) * cw)
            j = h * chunks + c
            total[at, cols] += shares[z, j].astype(jnp.float32)

            @pl.when(has_left)
            def _(at=at, cols=cols, j=j):
                share_copy(0, z, j).wait_recv()
                total[at, cols] += from_left[z, j].astype(jnp.float32)

            @pl.when(has_right)
            def _(at=at, cols=cols, j=j):
                share_copy(1, z, j).wait_recv()
                total[at, cols] += from_right[z, j].astype(jnp.float32)

    for c in range(chunks):
        cols = slice(c * cw, (c + 1) * cw)
        final = total[:, cols].astype(jnp.bfloat16)
        out_ref[:, cols] = final
        picker = jnp.where(sublane // 8 == c, picks, 0.0).astype(jnp.bfloat16)
        chosen = chosen + jnp.dot(picker, final, preferred_element_type=jnp.float32)
    picked[...] = chosen.astype(jnp.bfloat16)

    def spread(source, target, ss, rs):
        def peer_copy(shift):
            return pltpu.make_async_remote_copy(
                src_ref=source,
                dst_ref=target.at[tok],
                send_sem=ss.at[shift],
                recv_sem=rs.at[shift],
                device_id={"tok": lax.rem(tok + shift, tok_count)},
                device_id_type=MESH,
            )

        def begin(shift, carry):
            peer_copy(shift).start()
            return carry

        def end(shift, carry):
            peer_copy(shift).wait()
            return carry

        lax.fori_loop(1, tok_count, begin, 0)
        target[tok] = source[...]
        lax.fori_loop(1, tok_count, end, 0)

    spread(picked, picked_all, pick_ss, pick_rs)
    gathered = picked_all[0].astype(jnp.float32)
    for i in range(1, tok_count):
        gathered = gathered + picked_all[i].astype(jnp.float32)
    last = jnp.concatenate([gathered[8 * c : 8 * c + 8] for c in range(chunks)], axis=1)
    mean_square = jnp.mean(last * last, axis=1, keepdims=True)
    diagonal_mask = lax.broadcasted_iota(jnp.int32, (8, 128), 0) == lax.broadcasted_iota(
        jnp.int32, (8, 128), 1
    )
    spread_row = jnp.sum(
        jnp.where(diagonal_mask, jnp.sqrt(mean_square + epsilon), 0.0), axis=0, keepdims=True
    )
    final_normed = (
        last * lax.rsqrt(mean_square + epsilon) * final_gain_ref[...].astype(jnp.float32).reshape(1, width)
    ).astype(jnp.bfloat16)
    final_normed = jnp.concatenate(
        [final_normed, jnp.zeros((128 - 8, width), jnp.bfloat16)], axis=0
    )
    loads[3].wait()

    def vocab(block, highest):
        at = pl.ds(pl.multiple_of(block * vocab_step, vocab_step), vocab_step)
        values = lax.dot_general(
            w_head[at, :],
            final_normed,
            (((1,), (1,)), ((), ())),
            preferred_element_type=jnp.float32,
        )
        logits[at, :] = values
        return jnp.maximum(highest, jnp.max(values, axis=0, keepdims=True))

    blocks = w_head.shape[0] // vocab_step
    top = lax.fori_loop(0, blocks, vocab, jnp.full((1, 128), -jnp.inf, jnp.float32))

    def exponents(block, amount):
        at = pl.ds(pl.multiple_of(block * vocab_step, vocab_step), vocab_step)
        return amount + jnp.sum(jnp.exp(logits[at, :] - top), axis=0, keepdims=True)

    amount = lax.fori_loop(0, blocks, exponents, jnp.zeros((1, 128), jnp.float32))
    stats[...] = jnp.concatenate([top, amount, jnp.zeros((6, 128), jnp.float32)], axis=0)
    spread(stats, stats_all, stat_ss, stat_rs)
    highest = stats_all[0, 0:1]
    for i in range(1, tok_count):
        highest = jnp.maximum(highest, stats_all[i, 0:1])
    amount = jnp.zeros((1, 128), jnp.float32)
    for i in range(tok_count):
        amount = amount + stats_all[i, 1:2] * jnp.exp(stats_all[i, 0:1] - highest)
    stat_ref[...] = jnp.concatenate(
        [spread_row, highest, highest + jnp.log(amount), jnp.zeros((5, 128), jnp.float32)], axis=0
    )

    for h in range(2):
        for c in order:
            part_copy(0, h, c).wait_send()
            part_copy(1, h, c).wait_send()
            half_copy(h, c).wait_send()

    def settle(tile, carry):
        for c in range(pieces):

            @pl.when(has_right & (tile <= z))
            def _(c=c):
                tile_copy(0, tile, c).wait_send()

            @pl.when(has_left & (tile >= z))
            def _(c=c):
                tile_copy(1, tile, c).wait_send()

            @pl.when(tile > z)
            def _(c=c):
                share_copy(0, tile, c).wait_send()

            @pl.when(tile < z)
            def _(c=c):
                share_copy(1, tile, c).wait_send()

        return carry

    lax.fori_loop(0, n, settle, 0)


def back(
    lengths,
    attended,
    hidden,
    out_parts,
    mlp_gain,
    final_gain,
    gate_weight,
    up_weight,
    down_weight,
    head_weight,
    owner_count,
    kv_count,
    tok_count,
):
    rows, width = hidden.shape
    units = down_weight.shape[0]
    vocab_rows = head_weight.shape[0]
    vocab_step = max(b for b in range(16, 513, 16) if vocab_rows % b == 0)
    n, chunks = owner_count, 4
    cw = width // chunks
    bf16, f32 = jnp.bfloat16, jnp.float32
    dma = pltpu.SemaphoreType.DMA
    vmem = pl.BlockSpec(memory_space=pltpu.VMEM)
    hbm = pl.BlockSpec(memory_space=pltpu.HBM)
    parts = len(out_parts)
    return pl.pallas_call(
        lambda *refs: back_kernel(n, kv_count, tok_count, parts, rows, vocab_step, *refs),
        out_shape=[
            jax.ShapeDtypeStruct((rows, width), bf16),
            jax.ShapeDtypeStruct((8, 128), f32),
        ],
        in_specs=[pl.BlockSpec(memory_space=pltpu.SMEM)] + [vmem] * (4 + parts) + [hbm] * 4,
        out_specs=[vmem] * 2,
        scratch_shapes=[
            pltpu.VMEM((width, 2 * units), bf16),
            pltpu.VMEM((units, width), bf16),
            pltpu.VMEM((vocab_rows, width), bf16),
            pltpu.VMEM((2, 2 * chunks, rows // 2, cw), bf16),
            pltpu.VMEM((2, 2 * chunks, rows // 2, cw), bf16),
            pltpu.VMEM((2 * chunks, rows // 2, cw), bf16),
            pltpu.VMEM((2 * chunks, rows // 2, cw), bf16),
            pltpu.VMEM((rows, width), f32),
            pltpu.VMEM((n, 2 * chunks, rows // 2, cw), bf16),
            pltpu.VMEM((2, rows // 2, 2 * units), f32),
            pltpu.VMEM((rows // 2, units), bf16),
            pltpu.VMEM((n, 2 * chunks, rows // 2, cw), bf16),
            pltpu.VMEM((n, 2 * chunks, rows // 2, cw), bf16),
            pltpu.VMEM((n, 2 * chunks, rows // 2, cw), bf16),
            pltpu.VMEM((8 * chunks, cw), bf16),
            pltpu.VMEM((tok_count, 8 * chunks, cw), bf16),
            pltpu.VMEM((vocab_rows, 128), f32),
            pltpu.VMEM((8, 128), f32),
            pltpu.VMEM((tok_count, 8, 128), f32),
            dma((4,)),
            dma((2, 2 * chunks)),
            dma((2, 2 * chunks)),
            dma((2 * chunks,)),
            dma((2 * chunks,)),
            dma((2, n, 2 * chunks)),
            dma((n, 2 * chunks)),
            dma((n, 2 * chunks)),
            dma((n, 2 * chunks)),
            dma((n, 2 * chunks)),
            dma((tok_count,)),
            dma((tok_count,)),
            dma((tok_count,)),
            dma((tok_count,)),
        ],
        compiler_params=pltpu.CompilerParams(
            collective_id=1, has_side_effects=True, vmem_limit_bytes=VMEM_LIMIT
        ),
        name="back",
    )(
        lengths,
        attended,
        hidden,
        *out_parts,
        mlp_gain,
        final_gain,
        gate_weight,
        up_weight,
        down_weight,
        head_weight,
    )


def shards(
    hidden_in,
    suffix_len,
    prefix_of,
    prefix_slot,
    prefix_cache,
    attn_gain,
    query_weight,
    keyval_weight,
    out_weight,
    mlp_gain,
    gate_weight,
    up_weight,
    down_weight,
    final_gain,
    head_weight,
):
    tok_count = lax.axis_size("tok")
    owner_count = lax.axis_size("req")
    tok_rows = hidden_in.shape[0]
    own_rows = tok_rows * tok_count
    kv_count = keyval_weight.shape[0]
    members = tok_count // kv_count

    def shifted(array, shift):
        pairs = [
            (h * members + (g + shift) % members, h * members + g)
            for h in range(kv_count)
            for g in range(members)
        ]
        return lax.ppermute(array, "tok", pairs)

    out_parts = [out_weight] + [shifted(out_weight, s) for s in range(1, members)]
    window_block = prefix_cache.shape[2]
    queries, suffix, windows = front(
        suffix_len,
        hidden_in,
        attn_gain,
        query_weight,
        keyval_weight,
        prefix_cache.reshape(kv_count, members, window_block // members, 2 * HD),
        owner_count,
        kv_count,
        tok_count,
    )
    attended, suffix_cache = attention(
        suffix_len,
        prefix_of,
        prefix_slot,
        queries,
        windows.reshape(owner_count, window_block * tok_count, 2 * HD),
        suffix.reshape(own_rows, 2 * HD),
        tok_rows,
        kv_count,
        tok_count,
    )
    request_count = suffix_len.shape[1]
    final_state, tail = back(
        suffix_len,
        attended,
        hidden_in,
        out_parts,
        mlp_gain,
        final_gain,
        gate_weight,
        up_weight,
        down_weight,
        head_weight,
        owner_count,
        kv_count,
        tok_count,
    )
    return (
        final_state,
        suffix_cache.T,
        tail[0:1, :request_count],
        tail[1:2, :request_count],
        tail[2:3, :request_count],
    )


def solution(mesh):
    placed = (
        P(("req", "tok"), None),
        P("req", None),
        P("req", None),
        P(),
        P("req", None, "tok", None),
        P(),
        P(None, "tok"),
        P(),
        P("tok", None),
        P(),
        P(None, "req"),
        P(None, "req"),
        P("req", None),
        P(),
        P("tok", None),
    )
    return jax.shard_map(
        shards,
        mesh=mesh,
        in_specs=placed,
        out_specs=(
            P(("req", "tok"), None),
            P("req", "tok"),
            P("req", None),
            P("req", None),
            P("req", None),
        ),
        check_vma=False,
    )
```

```python
import math

import jax
import jax.numpy as jnp
from jax import lax
from jax.experimental import pallas as pl
from jax.experimental.pallas import tpu as pltpu
from jax.sharding import PartitionSpec as P

HD = 64
PRE_LEN = 16384
VMEM_LIMIT = 60 * 2**20


epsilon = 1e-05
neg_large = -1e30


def attention_kernel(
    most_rows,
    tok_count,
    kv_count,
    lengths_ref,
    chosen_ref,
    slot_ref,
    query_ref,
    windows,
    suffix_ref,
    out_ref,
    cache_ref,
    padded,
    band,
    band_values,
    score_scr,
):
    requests = lengths_ref.shape[1]
    units, unused, narrow = query_ref.shape
    units, lanes = units // 2, 2 * narrow
    rows = out_ref.shape[0] // kv_count
    unit_rows = out_ref.shape[0] // units
    per_tile = rows // unit_rows
    step_rows = unit_rows // 2
    pairs = narrow // 2 // step_rows
    window_len = windows.shape[1]
    own_rows = suffix_ref.shape[0]
    chunk = 256
    span = window_len + chunk
    tail_rows = band.shape[0] - window_len
    members = tok_count // kv_count
    tok = lax.axis_index("tok")
    member = lax.rem(tok, members)

    cache_width = cache_ref.shape[0]
    for first in range(0, own_rows, chunk):
        block = suffix_ref[first : first + chunk, :].astype(jnp.float32).T.astype(jnp.bfloat16)
        for place in range(2 * HD // cache_width):

            @pl.when(lax.rem(tok, 2 * HD // cache_width) == place)
            def _(place=place, first=first, block=block):
                cache_ref[:, first : first + chunk] = block[
                    place * cache_width : (place + 1) * cache_width
                ]

    padded[:own_rows, :] = suffix_ref[...]
    padded[own_rows:, :] = jnp.zeros((padded.shape[0] - own_rows, 2 * HD), jnp.bfloat16)

    def turned(block):
        return block.astype(jnp.float32).T[HD:].astype(jnp.bfloat16)

    def folded(values, fold):
        return fold(values.reshape(values.shape[0] // 8, 8, lanes), axis=0)

    def one_request(request, start):
        end = start + lengths_ref[0, request]
        slot = slot_ref[chosen_ref[0, request]]
        touched = jnp.int32(0)
        for tile in range(kv_count):
            first_row = (tile * members + member) * rows
            touched = touched + ((start < first_row + rows) & (end > first_row)).astype(jnp.int32)

        @pl.when(touched > 0)
        def _():
            for first in range(0, window_len, chunk):
                block = windows[slot, first : first + chunk, :]
                band[first : first + chunk, :] = block
                band_values[:, first : first + chunk] = turned(block)
            base = pl.multiple_of(start // 16 * 16, 16)
            lifted = padded[pl.ds(base, tail_rows + 16), :].astype(jnp.float32)
            lifted = pltpu.roll(lifted, tail_rows + 16 - (start - base), axis=0)
            for first in range(0, tail_rows, 128):
                block = lifted[first : first + 128].astype(jnp.bfloat16)
                at = slice(window_len + first, window_len + first + 128)
                band[at, :] = block
                band_values[:, at] = turned(block)

        def one_unit(unit, carry):
            tile = unit // per_tile
            first_row = (tile * members + member) * rows + lax.rem(unit, per_tile) * unit_rows

            @pl.when((start < first_row + unit_rows) & (end > first_row))
            def _():
                query = jnp.concatenate([query_ref[2 * unit], query_ref[2 * unit + 1]], axis=1)
                lane = lax.broadcasted_iota(jnp.int32, (1, lanes), 1)
                lane_row = first_row + lane // narrow * step_rows + lane % step_rows
                offset = lane_row - start
                low = pl.multiple_of((jnp.maximum(first_row, start) - start) // 128 * 128, 128)
                high = None
                for first in range(0, span, chunk):
                    scores = jnp.dot(
                        band[pl.ds(low + first, chunk), :],
                        query,
                        preferred_element_type=jnp.float32,
                    )
                    place = low + first + lax.broadcasted_iota(jnp.int32, (chunk, 1), 0)
                    if first == 0:
                        scores = jnp.where(place > offset, scores, neg_large)
                    if first == span - chunk:
                        scores = jnp.where(place <= offset + window_len, scores, neg_large)
                    score_scr[first : first + chunk, :] = scores
                    top = folded(scores, jnp.max)
                    high = top if high is None else jnp.maximum(high, top)
                high = jnp.max(high, axis=0, keepdims=True)
                total, acc = None, None
                for first in range(0, span, chunk):
                    weights = jnp.exp2(score_scr[first : first + chunk, :] - high)
                    part = folded(weights, jnp.sum)
                    term = jnp.dot(
                        band_values[:, pl.ds(low + first, chunk)],
                        weights.astype(jnp.bfloat16),
                        preferred_element_type=jnp.float32,
                    )
                    total = part if total is None else total + part
                    acc = term if acc is None else acc + term
                result = acc / jnp.sum(total, axis=0, keepdims=True)
                for odd in range(2):
                    part = result[:, odd * narrow : (odd + 1) * narrow]
                    both = jnp.concatenate(
                        [part[:, : narrow // 2], part[:, narrow // 2 :]], axis=0
                    )
                    flat = both.T
                    at = pl.ds(
                        pl.multiple_of(unit * unit_rows + odd * step_rows, step_rows), step_rows
                    )
                    row = (
                        first_row
                        + odd * step_rows
                        + lax.broadcasted_iota(jnp.int32, (step_rows, 1), 0)
                    )
                    mine = (row >= start) & (row < end)
                    for pair in range(pairs):
                        cols = slice(pair * 2 * HD, (pair + 1) * 2 * HD)
                        new = flat[pair * step_rows : (pair + 1) * step_rows]
                        old = out_ref[at, cols].astype(jnp.float32)
                        out_ref[at, cols] = jnp.where(mine, new, old).astype(jnp.bfloat16)

            return carry

        lax.fori_loop(0, units, one_unit, 0)
        return end

    lax.fori_loop(0, requests, one_request, 0)


def attention(lengths, chosen, prefix_slot, queries, windows, suffix, rows, kv_count, tok_count):
    units, unused, lanes = queries.shape
    heads = units * lanes // (kv_count * rows)
    own_rows = suffix.shape[0]
    window_len = windows.shape[1]
    cache_width = kv_count * 2 * HD // tok_count
    tail_rows = own_rows // 2 + 256
    smem = pl.BlockSpec(memory_space=pltpu.SMEM)
    vmem = pl.BlockSpec(memory_space=pltpu.VMEM)
    return pl.pallas_call(
        lambda *refs: attention_kernel(own_rows // 2, tok_count, kv_count, *refs),
        out_shape=[
            jax.ShapeDtypeStruct((kv_count * rows, heads * HD), jnp.bfloat16),
            jax.ShapeDtypeStruct((cache_width, own_rows), jnp.bfloat16),
        ],
        in_specs=[smem] * 3 + [vmem] * 3,
        out_specs=[vmem] * 2,
        scratch_shapes=[
            pltpu.VMEM((own_rows + tail_rows + 16, 2 * HD), jnp.bfloat16),
            pltpu.VMEM((window_len + tail_rows, 2 * HD), jnp.bfloat16),
            pltpu.VMEM((HD, window_len + tail_rows), jnp.bfloat16),
            pltpu.VMEM((window_len + 256, 2 * lanes), jnp.float32),
        ],
        compiler_params=pltpu.CompilerParams(vmem_limit_bytes=VMEM_LIMIT),
        cost_estimate=pl.CostEstimate(
            flops=10_000_000_000, bytes_accessed=8_000_000, transcendentals=10_000_000
        ),
        name="attention",
    )(lengths, chosen, prefix_slot, queries, windows, suffix)


MESH = pl.DeviceIdType.MESH


def request_ends(lengths_ref, count):
    ends, end = [], 0
    for request in range(count):
        end = end + lengths_ref[0, request]
        ends.append(end)
    return ends


def front_kernel(
    owner_count,
    kv_count,
    tok_count,
    lengths_ref,
    hid_ref,
    gain_ref,
    query_hbm,
    keyval_hbm,
    prefix_hbm,
    project_hbm,
    query_ref,
    suffix_ref,
    windows,
    projects,
    weights,
    tiles,
    suffix,
    local_sem,
    weight_ss,
    weight_rs,
    project_ss,
    project_rs,
    deal_ss,
    deal_rs,
    tile_ss,
    tile_rs,
    hop_ss,
    hop_rs,
    core_ss,
    core_rs,
    suffix_ss,
    suffix_rs,
):
    n = owner_count
    rows, width = hid_ref.shape
    chunks = tiles.shape[1]
    cw = width // chunks
    columns = query_hbm.shape[1]
    tok = lax.axis_index("tok")
    z = lax.axis_index("req")
    members = tok_count // kv_count
    mine, member = tok // members, lax.rem(tok, members)
    across = mine + 1 - 2 * lax.rem(mine, 2)
    along = lax.rem(mine + 2, 4)
    diagonal = 3 - mine
    has_left, has_right = z > 0, z < n - 1
    left, right = lax.rem(z - 1 + n, n), lax.rem(z + 1, n)
    onward = (has_right, has_left)
    half = HD // 2
    heads = members * columns // HD
    run = tok_count // 2

    own_query = pltpu.make_async_copy(query_hbm, weights.at[:, :columns], local_sem.at[0])
    own_keyval = pltpu.make_async_copy(
        keyval_hbm.at[mine], weights.at[:, members * columns :], local_sem.at[1]
    )
    own_window = pltpu.make_async_copy(
        prefix_hbm.at[mine, member], windows.at[z, tok, member], local_sem.at[2]
    )
    own_query.start()
    own_keyval.start()
    own_window.start()

    barrier = pltpu.get_barrier_semaphore()

    def greet(shift, carry):
        pl.semaphore_signal(
            barrier,
            inc=1,
            device_id={"tok": lax.rem(tok + shift, tok_count)},
            device_id_type=MESH,
        )
        return carry

    lax.fori_loop(1, tok_count, greet, 0)

    @pl.when(has_left)
    def _():
        pl.semaphore_signal(barrier, inc=1, device_id={"req": left}, device_id_type=MESH)

    @pl.when(has_right)
    def _():
        pl.semaphore_signal(barrier, inc=1, device_id={"req": right}, device_id_type=MESH)

    squares = jnp.zeros((rows, 1), jnp.float32)
    for c in range(chunks):
        part = hid_ref[:, c * cw : (c + 1) * cw].astype(jnp.float32)
        squares = squares + jnp.sum(part * part, axis=1, keepdims=True)
    scale = lax.rsqrt(squares / width + epsilon)
    for c in range(chunks):
        cols = slice(c * cw, (c + 1) * cw)
        tiles[mine, c] = (
            hid_ref[:, cols].astype(jnp.float32)
            * scale
            * gain_ref[cols].astype(jnp.float32).reshape(1, cw)
        ).astype(jnp.bfloat16)

    def deal_copy(shift):
        peer = lax.rem(tok + shift, tok_count)
        peer_member = lax.rem(peer, members)
        return pltpu.make_async_remote_copy(
            src_ref=prefix_hbm.at[peer // members, peer_member],
            dst_ref=windows.at[z, tok, peer_member],
            send_sem=deal_ss.at[shift],
            recv_sem=deal_rs.at[shift],
            device_id={"tok": peer},
            device_id_type=MESH,
        )

    def dealt(shift):
        return pltpu.make_async_remote_copy(
            src_ref=prefix_hbm.at[0, 0],
            dst_ref=windows.at[z, lax.rem(tok - shift + tok_count, tok_count), member],
            send_sem=deal_ss.at[shift],
            recv_sem=deal_rs.at[shift],
            device_id={"tok": lax.rem(tok + shift, tok_count)},
            device_id_type=MESH,
        )

    def weight_copy(shift):
        peer = lax.rem(member - shift + members, members)
        return pltpu.make_async_remote_copy(
            src_ref=query_hbm,
            dst_ref=weights.at[:, shift * columns : (shift + 1) * columns],
            send_sem=weight_ss.at[shift],
            recv_sem=weight_rs.at[shift],
            device_id={"tok": mine * members + peer},
            device_id_type=MESH,
        )

    def project_copy(shift):
        peer = lax.rem(member - shift + members, members)
        return pltpu.make_async_remote_copy(
            src_ref=project_hbm,
            dst_ref=projects.at[shift - 1],
            send_sem=project_ss.at[shift],
            recv_sem=project_rs.at[shift],
            device_id={"tok": mine * members + peer},
            device_id_type=MESH,
        )

    def tile_copy(tile, c, to_along, relayed):
        return pltpu.make_async_remote_copy(
            src_ref=tiles.at[tile, c],
            dst_ref=tiles.at[tile, c],
            send_sem=tile_ss.at[int(to_along), int(relayed), c],
            recv_sem=tile_rs.at[tile, c],
            device_id={"tok": (along if to_along else across) * members + member},
            device_id_type=MESH,
        )

    def hop_copy(side, slot, part):
        return pltpu.make_async_remote_copy(
            src_ref=windows.at[slot, part * run : (part + 1) * run, member],
            dst_ref=windows.at[slot, part * run : (part + 1) * run, member],
            send_sem=hop_ss.at[side, slot, part],
            recv_sem=hop_rs.at[slot, part],
            device_id={"req": right if side == 0 else left},
            device_id_type=MESH,
        )

    def core_copy(slot, shift, place):
        return pltpu.make_async_remote_copy(
            src_ref=windows.at[slot, :, place],
            dst_ref=windows.at[slot, :, place],
            send_sem=core_ss.at[slot, shift],
            recv_sem=core_rs.at[slot, shift],
            device_id={"tok": mine * members + lax.rem(member + shift, members)},
            device_id_type=MESH,
        )

    def suffix_copy(tile, shift, place):
        return pltpu.make_async_remote_copy(
            src_ref=suffix.at[tile, place],
            dst_ref=suffix.at[tile, place],
            send_sem=suffix_ss.at[tile, shift],
            recv_sem=suffix_rs.at[tile, shift],
            device_id={"tok": mine * members + lax.rem(member + shift, members)},
            device_id_type=MESH,
        )

    pl.semaphore_wait(
        barrier, tok_count - 1 + has_left.astype(jnp.int32) + has_right.astype(jnp.int32)
    )

    def start_deal(shift, carry):
        deal_copy(shift).start()
        return carry

    lax.fori_loop(1, tok_count, start_deal, 0)
    order = [c for pair in zip(range(chunks // 2), range(chunks // 2, chunks)) for c in pair]
    for a, b in zip(range(chunks // 2), range(chunks // 2, chunks)):
        tile_copy(mine, a, False, False).start()
        tile_copy(mine, b, True, False).start()
    for a, b in zip(range(chunks // 2), range(chunks // 2, chunks)):
        tile_copy(mine, b, False, False).start()
        tile_copy(mine, a, True, False).start()
    for shift in range(1, members):
        weight_copy(shift).start()

    ends = request_ends(lengths_ref, lengths_ref.shape[1])

    def turns(row):
        start = jnp.zeros((1, rows), jnp.int32)
        for end in ends[:-1]:
            start = jnp.where(row >= end, end, start)
        positions = (row - start + PRE_LEN).astype(jnp.float32)
        level = lax.broadcasted_iota(jnp.int32, (half, 1), 0).astype(jnp.float32)
        angles = jnp.exp(level * (-2.0 * math.log(10000.0) / HD)) * positions
        return jnp.cos(angles), jnp.sin(angles)

    unit_rows = 2 * rows // heads
    per_tile = rows // unit_rows

    def project(tile):
        result = None
        for c in range(chunks):
            term = jnp.dot(
                tiles[tile, c],
                weights[c * cw : (c + 1) * cw, :],
                preferred_element_type=jnp.float32,
            )
            result = term if result is None else result + term
        first_row = (tile * members + member) * rows
        lane = lax.broadcasted_iota(jnp.int32, (1, rows), 1)
        zeros = jnp.zeros((HD, 2 * rows), jnp.bfloat16)
        for u in range(per_tile):
            cosine, sine = turns(first_row + u * unit_rows + lax.rem(lane, unit_rows))
            block = result[u * unit_rows : (u + 1) * unit_rows]
            turned = jnp.concatenate(
                [block[:, p * 2 * HD : (p + 1) * 2 * HD] for p in range(heads // 2)], axis=0
            ).T
            for odd in range(2):
                low = turned[odd * HD : odd * HD + half]
                high = turned[odd * HD + half : (odd + 1) * HD]
                both = jnp.concatenate(
                    [low * cosine - high * sine, high * cosine + low * sine], axis=0
                )
                query_ref[tile * per_tile + u, :HD, odd * rows : (odd + 1) * rows] = (
                    both * (HD**-0.5 * math.log2(math.e))
                ).astype(jnp.bfloat16)
            query_ref[tile * per_tile + u, HD:, :] = zeros
        cosine, sine = turns(first_row + lane)
        turned = result[:, heads * HD :].T
        low, high = turned[:half], turned[half:HD]
        keyvals = jnp.concatenate(
            [low * cosine - high * sine, high * cosine + low * sine, turned[HD:]], axis=0
        )
        suffix[tile, member] = keyvals.T.astype(jnp.bfloat16)
        for shift in range(1, members):
            suffix_copy(tile, shift, member).start()

    def relay(step):
        sources = ((0, z - step, z >= step), (1, z + step, z + step < n))
        for part in range(2):
            for side, slot, valid in sources:

                @pl.when(valid)
                def _(side=side, slot=slot, part=part):
                    hop_copy(side, slot, part).wait_recv()

                    @pl.when(onward[side])
                    def _():
                        hop_copy(side, slot, part).start()

        for side, slot, valid in sources:

            @pl.when(valid)
            def _(slot=slot):
                for shift in range(1, members):
                    core_copy(slot, shift, member).start()

    own_window.wait()

    def wait_deal(shift, carry):
        dealt(shift).wait_recv()
        return carry

    lax.fori_loop(1, tok_count, wait_deal, 0)
    for side in range(2):

        @pl.when(onward[side])
        def _(side=side):
            for part in range(2):
                hop_copy(side, z, part).start()

    for shift in range(1, members):
        core_copy(z, shift, member).start()

    for a, b in zip(range(chunks // 2), range(chunks // 2, chunks)):
        tile_copy(across, a, False, False).wait_recv()
        tile_copy(across, a, True, True).start()
        tile_copy(along, b, True, False).wait_recv()
        tile_copy(along, b, False, True).start()
    own_query.wait()
    own_keyval.wait()
    for shift in range(1, members):
        weight_copy(shift).wait_recv()
        project_copy(shift).start()
    project(mine)
    for a, b in zip(range(chunks // 2), range(chunks // 2, chunks)):
        tile_copy(across, b, False, False).wait_recv()
        tile_copy(along, a, True, False).wait_recv()
    relay(1)
    project(across)
    project(along)
    relay(2)
    for a, b in zip(range(chunks // 2), range(chunks // 2, chunks)):
        tile_copy(diagonal, a, True, True).wait_recv()
        tile_copy(diagonal, b, False, True).wait_recv()
    project(diagonal)
    for step in range(3, n):
        relay(step)

    for tile in range(kv_count):
        for shift in range(1, members):
            peer = lax.rem(member - shift + members, members)
            suffix_copy(tile, shift, peer).wait_recv()
    suffix_ref[...] = suffix[...]

    def settle(slot, carry):
        for shift in range(1, members):
            peer = lax.rem(member - shift + members, members)
            core_copy(slot, shift, peer).wait_recv()
            core_copy(slot, shift, member).wait_send()

        @pl.when(has_right & (slot <= z))
        def _():
            for part in range(2):
                hop_copy(0, slot, part).wait_send()

        @pl.when(has_left & (slot >= z))
        def _():
            for part in range(2):
                hop_copy(1, slot, part).wait_send()

        return carry

    lax.fori_loop(0, n, settle, 0)
    for c in range(chunks):
        tile_copy(mine, c, False, False).wait_send()
        tile_copy(mine, c, True, False).wait_send()
        if c < chunks // 2:
            tile_copy(across, c, True, True).wait_send()
        else:
            tile_copy(along, c, False, True).wait_send()
    for shift in range(1, members):
        weight_copy(shift).wait_send()
        project_copy(shift).wait()
    for tile in range(kv_count):
        for shift in range(1, members):
            suffix_copy(tile, shift, member).wait_send()

    def deal_sent(shift, carry):
        deal_copy(shift).wait_send()
        return carry

    lax.fori_loop(1, tok_count, deal_sent, 0)


def front(
    lengths,
    hidden,
    gain,
    query_weight,
    keyval_weight,
    prefix,
    out_weight,
    owner_count,
    kv_count,
    tok_count,
):
    rows, width = hidden.shape
    members = tok_count // kv_count
    columns = query_weight.shape[1]
    heads = members * columns // HD
    piece = prefix.shape[2]
    n, chunks = owner_count, 4
    cw = width // chunks
    bf16 = jnp.bfloat16
    dma = pltpu.SemaphoreType.DMA
    vmem = pl.BlockSpec(memory_space=pltpu.VMEM)
    hbm = pl.BlockSpec(memory_space=pltpu.HBM)
    return pl.pallas_call(
        lambda *refs: front_kernel(n, kv_count, tok_count, *refs),
        out_shape=[
            jax.ShapeDtypeStruct((kv_count * heads // 2, 2 * HD, 2 * rows), bf16),
            jax.ShapeDtypeStruct((kv_count, members, rows, 2 * HD), bf16),
            jax.ShapeDtypeStruct((n, tok_count, members, piece, 2 * HD), bf16),
            jax.ShapeDtypeStruct((members - 1,) + out_weight.shape, bf16),
        ],
        in_specs=[pl.BlockSpec(memory_space=pltpu.SMEM), vmem, vmem, hbm, hbm, hbm, hbm],
        out_specs=[vmem, vmem, hbm, hbm],
        scratch_shapes=[
            pltpu.VMEM((width, members * columns + 2 * HD), bf16),
            pltpu.VMEM((kv_count, chunks, rows, cw), bf16),
            pltpu.VMEM((kv_count, members, rows, 2 * HD), bf16),
            dma((3,)),
            dma((members,)),
            dma((members,)),
            dma((members,)),
            dma((members,)),
            dma((tok_count,)),
            dma((tok_count,)),
            dma((2, 2, chunks)),
            dma((kv_count, chunks)),
            dma((2, n, 2)),
            dma((n, 2)),
            dma((n, members)),
            dma((n, members)),
            dma((kv_count, members)),
            dma((kv_count, members)),
        ],
        compiler_params=pltpu.CompilerParams(
            collective_id=0, has_side_effects=True, vmem_limit_bytes=VMEM_LIMIT
        ),
        name="front",
    )(lengths, hidden, gain, query_weight, keyval_weight, prefix, out_weight)


def back_kernel(owner_count, kv_count, tok_count, parts, rows, vocab_step, *refs):
    lengths_ref, att_ref, hid_ref = refs[:3]
    outw = (refs[3],) + tuple(refs[4].at[i] for i in range(parts - 1))
    (
        gain_ref,
        final_gain_ref,
        gate_hbm,
        up_hbm,
        down_hbm,
        head_hbm,
        out_ref,
        stat_ref,
        w_in,
        w_down,
        w_head,
        part_send,
        part_recv,
        half_send,
        half_recv,
        total,
        tiles,
        acc,
        act,
        shares,
        from_left,
        from_right,
        picked,
        picked_all,
        logits,
        stats,
        stats_all,
        load_sem,
        part_ss,
        part_rs,
        half_ss,
        half_rs,
        tile_ss,
        tile_rs,
        share_ss,
        left_rs,
        right_rs,
        pick_ss,
        pick_rs,
        stat_ss,
        stat_rs,
    ) = refs[5:]
    n = owner_count
    width = hid_ref.shape[1]
    chunks = tiles.shape[1] // 2
    cw = width // chunks
    units = w_down.shape[0]
    tok = lax.axis_index("tok")
    z = lax.axis_index("req")
    members = tok_count // kv_count
    mine, member = tok // members, lax.rem(tok, members)
    across = mine + 1 - 2 * lax.rem(mine, 2)
    along = lax.rem(mine + 2, 4)
    diagonal = 3 - mine
    has_left, has_right = z > 0, z < n - 1
    left, right = lax.rem(z - 1 + n, n), lax.rem(z + 1, n)

    loads = [
        pltpu.make_async_copy(gate_hbm, w_in.at[:, :units], load_sem.at[0]),
        pltpu.make_async_copy(up_hbm, w_in.at[:, units:], load_sem.at[1]),
        pltpu.make_async_copy(down_hbm, w_down, load_sem.at[2]),
        pltpu.make_async_copy(head_hbm, w_head, load_sem.at[3]),
    ]
    for load in loads:
        load.start()

    barrier = pltpu.get_barrier_semaphore()

    def greet(shift, carry):
        pl.semaphore_signal(
            barrier,
            inc=1,
            device_id={"tok": lax.rem(tok + shift, tok_count)},
            device_id_type=MESH,
        )
        return carry

    lax.fori_loop(1, tok_count, greet, 0)

    @pl.when(has_left)
    def _():
        pl.semaphore_signal(barrier, inc=1, device_id={"req": left}, device_id_type=MESH)

    @pl.when(has_right)
    def _():
        pl.semaphore_signal(barrier, inc=1, device_id={"req": right}, device_id_type=MESH)

    half = rows // 2
    pieces = 2 * chunks

    def product(tile, h, c):
        at = pl.ds(pl.multiple_of(tile * rows + h * half, half), half)
        depth = att_ref.shape[1] // parts
        result = None
        for i in range(parts):
            term = jnp.dot(
                att_ref[at, i * depth : (i + 1) * depth],
                outw[i][:, c * cw : (c + 1) * cw],
                preferred_element_type=jnp.float32,
            )
            result = term if result is None else result + term
        return result

    def part_copy(kind, h, c):
        peer = across if c < chunks // 2 else along
        j = h * chunks + c
        return pltpu.make_async_remote_copy(
            src_ref=part_send.at[kind, j],
            dst_ref=part_recv.at[kind, j],
            send_sem=part_ss.at[kind, j],
            recv_sem=part_rs.at[kind, j],
            device_id={"tok": peer * members + member},
            device_id_type=MESH,
        )

    def half_copy(h, c):
        peer = along if c < chunks // 2 else across
        j = h * chunks + c
        return pltpu.make_async_remote_copy(
            src_ref=half_send.at[j],
            dst_ref=half_recv.at[j],
            send_sem=half_ss.at[j],
            recv_sem=half_rs.at[j],
            device_id={"tok": peer * members + member},
            device_id_type=MESH,
        )

    order = [c for pair in zip(range(chunks // 2), range(chunks // 2, chunks)) for c in pair]

    def send_diagonal(h):
        for c in order:
            part_send[0, h * chunks + c] = product(diagonal, h, c).astype(jnp.bfloat16)
            if h > 0:
                part_copy(0, h, c).start()

    def send_near(h):
        for c in order:
            near = across if c < chunks // 2 else along
            part_send[1, h * chunks + c] = product(near, h, c).astype(jnp.bfloat16)
            part_copy(1, h, c).start()

    def send_far(h):
        for c in order:
            j = h * chunks + c
            far = along if c < chunks // 2 else across
            here = product(far, h, c)
            part_copy(0, h, c).wait_recv()
            half_send[j] = (here + part_recv[0, j].astype(jnp.float32)).astype(jnp.bfloat16)
            half_copy(h, c).start()

    def keep_own(h):
        at = slice(h * half, (h + 1) * half)
        for c in order:
            cols = slice(c * cw, (c + 1) * cw)
            total[at, cols] = hid_ref[at, cols].astype(jnp.float32) + product(mine, h, c)

    def tile_copy(side, tile, c):
        return pltpu.make_async_remote_copy(
            src_ref=tiles.at[tile, c],
            dst_ref=tiles.at[tile, c],
            send_sem=tile_ss.at[side, tile, c],
            recv_sem=tile_rs.at[tile, c],
            device_id={"req": right if side == 0 else left},
            device_id_type=MESH,
        )

    def share_copy(side, tile, c):
        return pltpu.make_async_remote_copy(
            src_ref=shares.at[tile, c],
            dst_ref=(from_left if side == 0 else from_right).at[tile, c],
            send_sem=share_ss.at[tile, c],
            recv_sem=(left_rs if side == 0 else right_rs).at[tile, c],
            device_id={"req": right if side == 0 else left},
            device_id_type=MESH,
        )

    onward = (has_right, has_left)

    def hand_on(h):
        at = slice(h * half, (h + 1) * half)
        squares = jnp.zeros((half, 1), jnp.float32)
        for c in order:
            j = h * chunks + c
            cols = slice(c * cw, (c + 1) * cw)
            part_copy(1, h, c).wait_recv()
            half_copy(h, c).wait_recv()
            summed = (
                total[at, cols]
                + part_recv[1, j].astype(jnp.float32)
                + half_recv[j].astype(jnp.float32)
            )
            middle = summed.astype(jnp.bfloat16).astype(jnp.float32)
            total[at, cols] = middle
            squares = squares + jnp.sum(middle * middle, axis=1, keepdims=True)
        scale = lax.rsqrt(squares / width + epsilon)
        for c in range(chunks):
            j = h * chunks + c
            cols = slice(c * cw, (c + 1) * cw)
            tiles[z, j] = (
                total[at, cols] * scale * gain_ref[cols].astype(jnp.float32).reshape(1, cw)
            ).astype(jnp.bfloat16)
            for side in range(2):

                @pl.when(onward[side])
                def _(side=side, j=j):
                    tile_copy(side, z, j).start()

    send_diagonal(0)
    pl.semaphore_wait(
        barrier, tok_count - 1 + has_left.astype(jnp.int32) + has_right.astype(jnp.int32)
    )
    for c in order:
        part_copy(0, 0, c).start()
    send_near(0)
    send_diagonal(1)
    send_far(0)
    send_near(1)
    keep_own(0)
    keep_own(1)
    hand_on(0)
    send_far(1)

    def pass_on(side, source, j):
        tile_copy(side, source, j).wait_recv()

        @pl.when(onward[side])
        def _():
            tile_copy(side, source, j).start()

    for j in range(chunks):
        for side, source, valid in ((0, left, has_left), (1, right, has_right)):

            @pl.when(valid)
            def _(side=side, source=source, j=j):
                pass_on(side, source, j)

    hand_on(1)
    for load in loads[:3]:
        load.wait()
    own_step = jnp.maximum(z, n - 1 - z) + 1

    def step(t, carry):
        s, h = t // 2, lax.rem(t, 2)
        own = s == own_step
        sources = (jnp.where(own, z, z - s), z + s)
        valid = (sources[0] >= 0, sources[1] < n)
        for c in range(chunks):
            j = h * chunks + c
            for side in range(2):

                @pl.when(valid[side] & jnp.logical_not(own) & (t > 2))
                def _(side=side, j=j):
                    pass_on(side, sources[side], j)

            for side in range(2):

                @pl.when(valid[side])
                def _(side=side, c=c, j=j):
                    term = jnp.dot(
                        tiles[sources[side], j],
                        w_in[c * cw : (c + 1) * cw, :],
                        preferred_element_type=jnp.float32,
                    )
                    if c == 0:
                        acc[side] = term
                    else:
                        acc[side] += term

        for side in range(2):

            @pl.when(valid[side])
            def _(side=side):
                gate_proj = acc[side, :, :units]
                lifted = acc[side, :, units:]
                act[...] = (gate_proj / (1.0 + jnp.exp(-gate_proj)) * lifted).astype(
                    jnp.bfloat16
                )
                starts_sum = jnp.logical_not(own) & jnp.logical_not(onward[side])
                for c in range(chunks):
                    j = h * chunks + c
                    shares[sources[side], j] = jnp.dot(
                        act[...],
                        w_down[:, c * cw : (c + 1) * cw],
                        preferred_element_type=jnp.float32,
                    ).astype(jnp.bfloat16)

                    @pl.when(starts_sum)
                    def _(j=j):
                        share_copy(1 - side, sources[side], j).start()

        begun = (t - z, t - (n - 1 - z))
        targets = (begun[0] // 2, n - 1 - begun[1] // 2)
        coming = (
            has_left & (begun[0] >= 0) & (targets[0] > z) & (targets[0] < n),
            has_right & (begun[1] >= 0) & (targets[1] < z) & (targets[1] >= 0),
        )
        for side in range(2):

            @pl.when(coming[side])
            def _(side=side):
                target = targets[side]
                arrived = from_left if side == 0 else from_right
                for c in range(chunks):
                    j = lax.rem(begun[side], 2) * chunks + c
                    share_copy(side, target, j).wait_recv()
                    shares[target, j] = (
                        shares[target, j].astype(jnp.float32)
                        + arrived[target, j].astype(jnp.float32)
                    ).astype(jnp.bfloat16)
                    share_copy(side, target, j).start()

        return carry

    lax.fori_loop(2, max(2 * n + 2, 3 * n - 2), step, 0)

    sublane = lax.broadcasted_iota(jnp.int32, (8 * chunks, rows), 0)
    row = tok * rows + lax.broadcasted_iota(jnp.int32, (8 * chunks, rows), 1)
    picks = jnp.zeros((8 * chunks, rows), jnp.float32)
    for request, end in enumerate(request_ends(lengths_ref, lengths_ref.shape[1])):
        picks = jnp.where((lax.rem(sublane, 8) == request) & (row == end - 1), 1.0, picks)
    chosen = jnp.zeros((8 * chunks, cw), jnp.float32)
    for h in range(2):
        at = slice(h * half, (h + 1) * half)
        for c in range(chunks):
            cols = slice(c * cw, (c + 1) * cw)
            j = h * chunks + c
            total[at, cols] += shares[z, j].astype(jnp.float32)

            @pl.when(has_left)
            def _(at=at, cols=cols, j=j):
                share_copy(0, z, j).wait_recv()
                total[at, cols] += from_left[z, j].astype(jnp.float32)

            @pl.when(has_right)
            def _(at=at, cols=cols, j=j):
                share_copy(1, z, j).wait_recv()
                total[at, cols] += from_right[z, j].astype(jnp.float32)

    for c in range(chunks):
        cols = slice(c * cw, (c + 1) * cw)
        final = total[:, cols].astype(jnp.bfloat16)
        out_ref[:, cols] = final
        picker = jnp.where(sublane // 8 == c, picks, 0.0).astype(jnp.bfloat16)
        chosen = chosen + jnp.dot(picker, final, preferred_element_type=jnp.float32)
    picked[...] = chosen.astype(jnp.bfloat16)

    def spread(source, target, ss, rs):
        def peer_copy(shift):
            return pltpu.make_async_remote_copy(
                src_ref=source,
                dst_ref=target.at[tok],
                send_sem=ss.at[shift],
                recv_sem=rs.at[shift],
                device_id={"tok": lax.rem(tok + shift, tok_count)},
                device_id_type=MESH,
            )

        def begin(shift, carry):
            peer_copy(shift).start()
            return carry

        def end(shift, carry):
            peer_copy(shift).wait()
            return carry

        lax.fori_loop(1, tok_count, begin, 0)
        target[tok] = source[...]
        lax.fori_loop(1, tok_count, end, 0)

    spread(picked, picked_all, pick_ss, pick_rs)
    gathered = picked_all[0].astype(jnp.float32)
    for i in range(1, tok_count):
        gathered = gathered + picked_all[i].astype(jnp.float32)
    last = jnp.concatenate([gathered[8 * c : 8 * c + 8] for c in range(chunks)], axis=1)
    mean_square = jnp.mean(last * last, axis=1, keepdims=True)
    diagonal_mask = lax.broadcasted_iota(jnp.int32, (8, 128), 0) == lax.broadcasted_iota(
        jnp.int32, (8, 128), 1
    )
    spread_row = jnp.sum(
        jnp.where(diagonal_mask, jnp.sqrt(mean_square + epsilon), 0.0), axis=0, keepdims=True
    )
    final_normed = (
        last * lax.rsqrt(mean_square + epsilon) * final_gain_ref[...].astype(jnp.float32).reshape(1, width)
    ).astype(jnp.bfloat16)
    final_normed = jnp.concatenate(
        [final_normed, jnp.zeros((128 - 8, width), jnp.bfloat16)], axis=0
    )
    loads[3].wait()

    def vocab(block, highest):
        at = pl.ds(pl.multiple_of(block * vocab_step, vocab_step), vocab_step)
        values = lax.dot_general(
            w_head[at, :],
            final_normed,
            (((1,), (1,)), ((), ())),
            preferred_element_type=jnp.float32,
        )
        logits[at, :] = values
        return jnp.maximum(highest, jnp.max(values, axis=0, keepdims=True))

    blocks = w_head.shape[0] // vocab_step
    top = lax.fori_loop(0, blocks, vocab, jnp.full((1, 128), -jnp.inf, jnp.float32))

    def exponents(block, amount):
        at = pl.ds(pl.multiple_of(block * vocab_step, vocab_step), vocab_step)
        return amount + jnp.sum(jnp.exp(logits[at, :] - top), axis=0, keepdims=True)

    amount = lax.fori_loop(0, blocks, exponents, jnp.zeros((1, 128), jnp.float32))
    stats[...] = jnp.concatenate([top, amount, jnp.zeros((6, 128), jnp.float32)], axis=0)
    spread(stats, stats_all, stat_ss, stat_rs)
    highest = stats_all[0, 0:1]
    for i in range(1, tok_count):
        highest = jnp.maximum(highest, stats_all[i, 0:1])
    amount = jnp.zeros((1, 128), jnp.float32)
    for i in range(tok_count):
        amount = amount + stats_all[i, 1:2] * jnp.exp(stats_all[i, 0:1] - highest)
    stat_ref[...] = jnp.concatenate(
        [spread_row, highest, highest + jnp.log(amount), jnp.zeros((5, 128), jnp.float32)], axis=0
    )

    for h in range(2):
        for c in order:
            part_copy(0, h, c).wait_send()
            part_copy(1, h, c).wait_send()
            half_copy(h, c).wait_send()

    def settle(tile, carry):
        for c in range(pieces):

            @pl.when(has_right & (tile <= z))
            def _(c=c):
                tile_copy(0, tile, c).wait_send()

            @pl.when(has_left & (tile >= z))
            def _(c=c):
                tile_copy(1, tile, c).wait_send()

            @pl.when(tile > z)
            def _(c=c):
                share_copy(0, tile, c).wait_send()

            @pl.when(tile < z)
            def _(c=c):
                share_copy(1, tile, c).wait_send()

        return carry

    lax.fori_loop(0, n, settle, 0)


def back(
    lengths,
    attended,
    hidden,
    out_weight,
    projects,
    mlp_gain,
    final_gain,
    gate_weight,
    up_weight,
    down_weight,
    head_weight,
    owner_count,
    kv_count,
    tok_count,
):
    rows, width = hidden.shape
    units = down_weight.shape[0]
    vocab_rows = head_weight.shape[0]
    vocab_step = max(b for b in range(16, 2049, 16) if vocab_rows % b == 0)
    n, chunks = owner_count, 4
    cw = width // chunks
    bf16, f32 = jnp.bfloat16, jnp.float32
    dma = pltpu.SemaphoreType.DMA
    vmem = pl.BlockSpec(memory_space=pltpu.VMEM)
    hbm = pl.BlockSpec(memory_space=pltpu.HBM)
    parts = tok_count // kv_count
    return pl.pallas_call(
        lambda *refs: back_kernel(n, kv_count, tok_count, parts, rows, vocab_step, *refs),
        out_shape=[
            jax.ShapeDtypeStruct((rows, width), bf16),
            jax.ShapeDtypeStruct((8, 128), f32),
        ],
        in_specs=[pl.BlockSpec(memory_space=pltpu.SMEM)] + [vmem] * 6 + [hbm] * 4,
        out_specs=[vmem] * 2,
        scratch_shapes=[
            pltpu.VMEM((width, 2 * units), bf16),
            pltpu.VMEM((units, width), bf16),
            pltpu.VMEM((vocab_rows, width), bf16),
            pltpu.VMEM((2, 2 * chunks, rows // 2, cw), bf16),
            pltpu.VMEM((2, 2 * chunks, rows // 2, cw), bf16),
            pltpu.VMEM((2 * chunks, rows // 2, cw), bf16),
            pltpu.VMEM((2 * chunks, rows // 2, cw), bf16),
            pltpu.VMEM((rows, width), f32),
            pltpu.VMEM((n, 2 * chunks, rows // 2, cw), bf16),
            pltpu.VMEM((2, rows // 2, 2 * units), f32),
            pltpu.VMEM((rows // 2, units), bf16),
            pltpu.VMEM((n, 2 * chunks, rows // 2, cw), bf16),
            pltpu.VMEM((n, 2 * chunks, rows // 2, cw), bf16),
            pltpu.VMEM((n, 2 * chunks, rows // 2, cw), bf16),
            pltpu.VMEM((8 * chunks, cw), bf16),
            pltpu.VMEM((tok_count, 8 * chunks, cw), bf16),
            pltpu.VMEM((vocab_rows, 128), f32),
            pltpu.VMEM((8, 128), f32),
            pltpu.VMEM((tok_count, 8, 128), f32),
            dma((4,)),
            dma((2, 2 * chunks)),
            dma((2, 2 * chunks)),
            dma((2 * chunks,)),
            dma((2 * chunks,)),
            dma((2, n, 2 * chunks)),
            dma((n, 2 * chunks)),
            dma((n, 2 * chunks)),
            dma((n, 2 * chunks)),
            dma((n, 2 * chunks)),
            dma((tok_count,)),
            dma((tok_count,)),
            dma((tok_count,)),
            dma((tok_count,)),
        ],
        compiler_params=pltpu.CompilerParams(
            collective_id=1, has_side_effects=True, vmem_limit_bytes=VMEM_LIMIT
        ),
        name="back",
    )(
        lengths,
        attended,
        hidden,
        out_weight,
        projects,
        mlp_gain,
        final_gain,
        gate_weight,
        up_weight,
        down_weight,
        head_weight,
    )


def shards(
    hidden_in,
    suffix_len,
    prefix_of,
    prefix_slot,
    prefix_cache,
    attn_gain,
    query_weight,
    keyval_weight,
    out_weight,
    mlp_gain,
    gate_weight,
    up_weight,
    down_weight,
    final_gain,
    head_weight,
):
    tok_count = lax.axis_size("tok")
    owner_count = lax.axis_size("req")
    tok_rows = hidden_in.shape[0]
    own_rows = tok_rows * tok_count
    kv_count = keyval_weight.shape[0]
    members = tok_count // kv_count

    window_block = prefix_cache.shape[2]
    queries, suffix, windows, projects = front(
        suffix_len,
        hidden_in,
        attn_gain,
        query_weight,
        keyval_weight,
        prefix_cache.reshape(kv_count, members, window_block // members, 2 * HD),
        out_weight,
        owner_count,
        kv_count,
        tok_count,
    )
    attended, suffix_cache = attention(
        suffix_len,
        prefix_of,
        prefix_slot,
        queries,
        windows.reshape(owner_count, window_block * tok_count, 2 * HD),
        suffix.reshape(own_rows, 2 * HD),
        tok_rows,
        kv_count,
        tok_count,
    )
    request_count = suffix_len.shape[1]
    final_state, tail = back(
        suffix_len,
        attended,
        hidden_in,
        out_weight,
        projects,
        mlp_gain,
        final_gain,
        gate_weight,
        up_weight,
        down_weight,
        head_weight,
        owner_count,
        kv_count,
        tok_count,
    )
    return (
        final_state,
        suffix_cache.T,
        tail[0:1, :request_count],
        tail[1:2, :request_count],
        tail[2:3, :request_count],
    )


def solution(mesh):
    placed = (
        P(("req", "tok"), None),
        P("req", None),
        P("req", None),
        P(),
        P("req", None, "tok", None),
        P(),
        P(None, "tok"),
        P(),
        P("tok", None),
        P(),
        P(None, "req"),
        P(None, "req"),
        P("req", None),
        P(),
        P("tok", None),
    )
    return jax.shard_map(
        shards,
        mesh=mesh,
        in_specs=placed,
        out_specs=(
            P(("req", "tok"), None),
            P("req", "tok"),
            P("req", None),
            P("req", None),
            P("req", None),
        ),
        check_vma=False,
    )
```

```python
import math

import jax
import jax.numpy as jnp
from jax import lax
from jax.experimental import pallas as pl
from jax.experimental.pallas import tpu as pltpu
from jax.sharding import PartitionSpec as P

HD = 64
PRE_LEN = 16384
VMEM_LIMIT = 60 * 2**20


epsilon = 1e-05
neg_large = -1e30


def attention_kernel(
    most_rows,
    tok_count,
    kv_count,
    lengths_ref,
    chosen_ref,
    slot_ref,
    query_ref,
    windows,
    suffix_ref,
    out_ref,
    cache_ref,
    padded,
    band,
    band_values,
    score_scr,
):
    requests = lengths_ref.shape[1]
    units, unused, narrow = query_ref.shape
    units, lanes = units // 2, 2 * narrow
    rows = out_ref.shape[0] // kv_count
    unit_rows = out_ref.shape[0] // units
    per_tile = rows // unit_rows
    step_rows = unit_rows // 2
    pairs = narrow // 2 // step_rows
    window_len = windows.shape[1]
    own_rows = suffix_ref.shape[0]
    chunk = 256
    span = window_len + chunk
    tail_rows = band.shape[0] - window_len
    members = tok_count // kv_count
    tok = lax.axis_index("tok")
    member = lax.rem(tok, members)

    cache_width = cache_ref.shape[0]
    for first in range(0, own_rows, chunk):
        block = suffix_ref[first : first + chunk, :].astype(jnp.float32).T.astype(jnp.bfloat16)
        for place in range(2 * HD // cache_width):

            @pl.when(lax.rem(tok, 2 * HD // cache_width) == place)
            def _(place=place, first=first, block=block):
                cache_ref[:, first : first + chunk] = block[
                    place * cache_width : (place + 1) * cache_width
                ]

    padded[:own_rows, :] = suffix_ref[...]
    padded[own_rows:, :] = jnp.zeros((padded.shape[0] - own_rows, 2 * HD), jnp.bfloat16)

    def turned(block):
        return block.astype(jnp.float32).T[HD:].astype(jnp.bfloat16)

    def folded(values, fold):
        return fold(values.reshape(values.shape[0] // 8, 8, lanes), axis=0)

    def one_request(request, start):
        end = start + lengths_ref[0, request]
        slot = slot_ref[chosen_ref[0, request]]
        touched = jnp.int32(0)
        for tile in range(kv_count):
            first_row = (tile * members + member) * rows
            touched = touched + ((start < first_row + rows) & (end > first_row)).astype(jnp.int32)

        @pl.when(touched > 0)
        def _():
            for first in range(0, window_len, chunk):
                block = windows[slot, first : first + chunk, :]
                band[first : first + chunk, :] = block
                band_values[:, first : first + chunk] = turned(block)
            base = pl.multiple_of(start // 16 * 16, 16)
            lifted = padded[pl.ds(base, tail_rows + 16), :].astype(jnp.float32)
            lifted = pltpu.roll(lifted, tail_rows + 16 - (start - base), axis=0)
            for first in range(0, tail_rows, 128):
                block = lifted[first : first + 128].astype(jnp.bfloat16)
                at = slice(window_len + first, window_len + first + 128)
                band[at, :] = block
                band_values[:, at] = turned(block)

        def one_unit(unit, carry):
            tile = unit // per_tile
            first_row = (tile * members + member) * rows + lax.rem(unit, per_tile) * unit_rows

            @pl.when((start < first_row + unit_rows) & (end > first_row))
            def _():
                query = jnp.concatenate([query_ref[2 * unit], query_ref[2 * unit + 1]], axis=1)
                lane = lax.broadcasted_iota(jnp.int32, (1, lanes), 1)
                lane_row = first_row + lane // narrow * step_rows + lane % step_rows
                offset = lane_row - start
                low = pl.multiple_of((jnp.maximum(first_row, start) - start) // 128 * 128, 128)
                high = None
                for first in range(0, span, chunk):
                    scores = jnp.dot(
                        band[pl.ds(low + first, chunk), :],
                        query,
                        preferred_element_type=jnp.float32,
                    )
                    place = low + first + lax.broadcasted_iota(jnp.int32, (chunk, 1), 0)
                    if first == 0:
                        scores = jnp.where(place > offset, scores, neg_large)
                    if first == span - chunk:
                        scores = jnp.where(place <= offset + window_len, scores, neg_large)
                    score_scr[first : first + chunk, :] = scores
                    top = folded(scores, jnp.max)
                    high = top if high is None else jnp.maximum(high, top)
                high = jnp.max(high, axis=0, keepdims=True)
                total, acc = None, None
                for first in range(0, span, chunk):
                    weights = jnp.exp2(score_scr[first : first + chunk, :] - high)
                    part = folded(weights, jnp.sum)
                    term = jnp.dot(
                        band_values[:, pl.ds(low + first, chunk)],
                        weights.astype(jnp.bfloat16),
                        preferred_element_type=jnp.float32,
                    )
                    total = part if total is None else total + part
                    acc = term if acc is None else acc + term
                result = acc / jnp.sum(total, axis=0, keepdims=True)
                for odd in range(2):
                    part = result[:, odd * narrow : (odd + 1) * narrow]
                    both = jnp.concatenate(
                        [part[:, : narrow // 2], part[:, narrow // 2 :]], axis=0
                    )
                    flat = both.T
                    at = pl.ds(
                        pl.multiple_of(unit * unit_rows + odd * step_rows, step_rows), step_rows
                    )
                    row = (
                        first_row
                        + odd * step_rows
                        + lax.broadcasted_iota(jnp.int32, (step_rows, 1), 0)
                    )
                    mine = (row >= start) & (row < end)
                    for pair in range(pairs):
                        cols = slice(pair * 2 * HD, (pair + 1) * 2 * HD)
                        new = flat[pair * step_rows : (pair + 1) * step_rows]
                        old = out_ref[at, cols].astype(jnp.float32)
                        out_ref[at, cols] = jnp.where(mine, new, old).astype(jnp.bfloat16)

            return carry

        lax.fori_loop(0, units, one_unit, 0)
        return end

    lax.fori_loop(0, requests, one_request, 0)


def attention(lengths, chosen, prefix_slot, queries, windows, suffix, rows, kv_count, tok_count):
    units, unused, lanes = queries.shape
    heads = units * lanes // (kv_count * rows)
    own_rows = suffix.shape[0]
    window_len = windows.shape[1]
    cache_width = kv_count * 2 * HD // tok_count
    tail_rows = own_rows // 2 + 256
    smem = pl.BlockSpec(memory_space=pltpu.SMEM)
    vmem = pl.BlockSpec(memory_space=pltpu.VMEM)
    return pl.pallas_call(
        lambda *refs: attention_kernel(own_rows // 2, tok_count, kv_count, *refs),
        out_shape=[
            jax.ShapeDtypeStruct((kv_count * rows, heads * HD), jnp.bfloat16),
            jax.ShapeDtypeStruct((cache_width, own_rows), jnp.bfloat16),
        ],
        in_specs=[smem] * 3 + [vmem] * 3,
        out_specs=[vmem] * 2,
        scratch_shapes=[
            pltpu.VMEM((own_rows + tail_rows + 16, 2 * HD), jnp.bfloat16),
            pltpu.VMEM((window_len + tail_rows, 2 * HD), jnp.bfloat16),
            pltpu.VMEM((HD, window_len + tail_rows), jnp.bfloat16),
            pltpu.VMEM((window_len + 256, 2 * lanes), jnp.float32),
        ],
        compiler_params=pltpu.CompilerParams(vmem_limit_bytes=VMEM_LIMIT),
        cost_estimate=pl.CostEstimate(
            flops=10_000_000_000, bytes_accessed=8_000_000, transcendentals=10_000_000
        ),
        name="attention",
    )(lengths, chosen, prefix_slot, queries, windows, suffix)


MESH = pl.DeviceIdType.MESH


def request_ends(lengths_ref, count):
    ends, end = [], 0
    for request in range(count):
        end = end + lengths_ref[0, request]
        ends.append(end)
    return ends


def front_kernel(
    owner_count,
    kv_count,
    tok_count,
    lengths_ref,
    hid_ref,
    gain_ref,
    query_hbm,
    keyval_hbm,
    prefix_hbm,
    project_hbm,
    query_ref,
    suffix_ref,
    windows,
    projects,
    weights,
    tiles,
    suffix,
    local_sem,
    weight_ss,
    weight_rs,
    project_ss,
    project_rs,
    deal_ss,
    deal_rs,
    tile_ss,
    tile_rs,
    hop_ss,
    hop_rs,
    core_ss,
    core_rs,
    suffix_ss,
    suffix_rs,
):
    n = owner_count
    rows, width = hid_ref.shape
    chunks = tiles.shape[1]
    cw = width // chunks
    columns = query_hbm.shape[1]
    tok = lax.axis_index("tok")
    z = lax.axis_index("req")
    members = tok_count // kv_count
    mine, member = tok // members, lax.rem(tok, members)
    across = mine + 1 - 2 * lax.rem(mine, 2)
    along = lax.rem(mine + 2, 4)
    diagonal = 3 - mine
    has_left, has_right = z > 0, z < n - 1
    left, right = lax.rem(z - 1 + n, n), lax.rem(z + 1, n)
    onward = (has_right, has_left)
    half = HD // 2
    heads = members * columns // HD
    run = tok_count // 2

    own_query = pltpu.make_async_copy(query_hbm, weights.at[:, :columns], local_sem.at[0])
    own_keyval = pltpu.make_async_copy(
        keyval_hbm.at[mine], weights.at[:, members * columns :], local_sem.at[1]
    )
    own_window = pltpu.make_async_copy(
        prefix_hbm.at[mine, member], windows.at[z, tok, member], local_sem.at[2]
    )
    own_query.start()
    own_keyval.start()
    own_window.start()

    barrier = pltpu.get_barrier_semaphore()

    def greet(shift, carry):
        pl.semaphore_signal(
            barrier,
            inc=1,
            device_id={"tok": lax.rem(tok + shift, tok_count)},
            device_id_type=MESH,
        )
        return carry

    lax.fori_loop(1, tok_count, greet, 0)

    @pl.when(has_left)
    def _():
        pl.semaphore_signal(barrier, inc=1, device_id={"req": left}, device_id_type=MESH)

    @pl.when(has_right)
    def _():
        pl.semaphore_signal(barrier, inc=1, device_id={"req": right}, device_id_type=MESH)

    squares = jnp.zeros((rows, 1), jnp.float32)
    for c in range(chunks):
        part = hid_ref[:, c * cw : (c + 1) * cw].astype(jnp.float32)
        squares = squares + jnp.sum(part * part, axis=1, keepdims=True)
    scale = lax.rsqrt(squares / width + epsilon)
    for c in range(chunks):
        cols = slice(c * cw, (c + 1) * cw)
        tiles[mine, c] = (
            hid_ref[:, cols].astype(jnp.float32)
            * scale
            * gain_ref[cols].astype(jnp.float32).reshape(1, cw)
        ).astype(jnp.bfloat16)

    def deal_copy(shift):
        peer = lax.rem(tok + shift, tok_count)
        peer_member = lax.rem(peer, members)
        return pltpu.make_async_remote_copy(
            src_ref=prefix_hbm.at[peer // members, peer_member],
            dst_ref=windows.at[z, tok, peer_member],
            send_sem=deal_ss.at[shift],
            recv_sem=deal_rs.at[shift],
            device_id={"tok": peer},
            device_id_type=MESH,
        )

    def dealt(shift):
        return pltpu.make_async_remote_copy(
            src_ref=prefix_hbm.at[0, 0],
            dst_ref=windows.at[z, lax.rem(tok - shift + tok_count, tok_count), member],
            send_sem=deal_ss.at[shift],
            recv_sem=deal_rs.at[shift],
            device_id={"tok": lax.rem(tok + shift, tok_count)},
            device_id_type=MESH,
        )

    def weight_copy(shift):
        peer = lax.rem(member - shift + members, members)
        return pltpu.make_async_remote_copy(
            src_ref=query_hbm,
            dst_ref=weights.at[:, shift * columns : (shift + 1) * columns],
            send_sem=weight_ss.at[shift],
            recv_sem=weight_rs.at[shift],
            device_id={"tok": mine * members + peer},
            device_id_type=MESH,
        )

    def project_copy(shift):
        peer = lax.rem(member - shift + members, members)
        return pltpu.make_async_remote_copy(
            src_ref=project_hbm,
            dst_ref=projects.at[shift - 1],
            send_sem=project_ss.at[shift],
            recv_sem=project_rs.at[shift],
            device_id={"tok": mine * members + peer},
            device_id_type=MESH,
        )

    def tile_copy(tile, c, to_along, relayed):
        return pltpu.make_async_remote_copy(
            src_ref=tiles.at[tile, c],
            dst_ref=tiles.at[tile, c],
            send_sem=tile_ss.at[int(to_along), int(relayed), c],
            recv_sem=tile_rs.at[tile, c],
            device_id={"tok": (along if to_along else across) * members + member},
            device_id_type=MESH,
        )

    def hop_copy(side, slot, part):
        return pltpu.make_async_remote_copy(
            src_ref=windows.at[slot, part * run : (part + 1) * run, member],
            dst_ref=windows.at[slot, part * run : (part + 1) * run, member],
            send_sem=hop_ss.at[side, slot, part],
            recv_sem=hop_rs.at[slot, part],
            device_id={"req": right if side == 0 else left},
            device_id_type=MESH,
        )

    def core_copy(slot, shift, place):
        return pltpu.make_async_remote_copy(
            src_ref=windows.at[slot, :, place],
            dst_ref=windows.at[slot, :, place],
            send_sem=core_ss.at[slot, shift],
            recv_sem=core_rs.at[slot, shift],
            device_id={"tok": mine * members + lax.rem(member + shift, members)},
            device_id_type=MESH,
        )

    def suffix_copy(tile, shift, place):
        return pltpu.make_async_remote_copy(
            src_ref=suffix.at[tile, place],
            dst_ref=suffix.at[tile, place],
            send_sem=suffix_ss.at[tile, shift],
            recv_sem=suffix_rs.at[tile, shift],
            device_id={"tok": mine * members + lax.rem(member + shift, members)},
            device_id_type=MESH,
        )

    pl.semaphore_wait(
        barrier, tok_count - 1 + has_left.astype(jnp.int32) + has_right.astype(jnp.int32)
    )

    def start_deal(shift, carry):
        deal_copy(shift).start()
        return carry

    lax.fori_loop(1, tok_count, start_deal, 0)
    order = [c for pair in zip(range(chunks // 2), range(chunks // 2, chunks)) for c in pair]
    for a, b in zip(range(chunks // 2), range(chunks // 2, chunks)):
        tile_copy(mine, a, False, False).start()
        tile_copy(mine, b, True, False).start()
    for a, b in zip(range(chunks // 2), range(chunks // 2, chunks)):
        tile_copy(mine, b, False, False).start()
        tile_copy(mine, a, True, False).start()
    for shift in range(1, members):
        weight_copy(shift).start()

    ends = request_ends(lengths_ref, lengths_ref.shape[1])

    def turns(row):
        start = jnp.zeros((1, rows), jnp.int32)
        for end in ends[:-1]:
            start = jnp.where(row >= end, end, start)
        positions = (row - start + PRE_LEN).astype(jnp.float32)
        level = lax.broadcasted_iota(jnp.int32, (half, 1), 0).astype(jnp.float32)
        angles = jnp.exp(level * (-2.0 * math.log(10000.0) / HD)) * positions
        return jnp.cos(angles), jnp.sin(angles)

    unit_rows = 2 * rows // heads
    per_tile = rows // unit_rows

    def project(tile):
        result = None
        for c in range(chunks):
            term = jnp.dot(
                tiles[tile, c],
                weights[c * cw : (c + 1) * cw, :],
                preferred_element_type=jnp.float32,
            )
            result = term if result is None else result + term
        first_row = (tile * members + member) * rows
        lane = lax.broadcasted_iota(jnp.int32, (1, rows), 1)
        zeros = jnp.zeros((HD, 2 * rows), jnp.bfloat16)
        for u in range(per_tile):
            cosine, sine = turns(first_row + u * unit_rows + lax.rem(lane, unit_rows))
            block = result[u * unit_rows : (u + 1) * unit_rows]
            turned = jnp.concatenate(
                [block[:, p * 2 * HD : (p + 1) * 2 * HD] for p in range(heads // 2)], axis=0
            ).T
            for odd in range(2):
                low = turned[odd * HD : odd * HD + half]
                high = turned[odd * HD + half : (odd + 1) * HD]
                both = jnp.concatenate(
                    [low * cosine - high * sine, high * cosine + low * sine], axis=0
                )
                query_ref[tile * per_tile + u, :HD, odd * rows : (odd + 1) * rows] = (
                    both * (HD**-0.5 * math.log2(math.e))
                ).astype(jnp.bfloat16)
            query_ref[tile * per_tile + u, HD:, :] = zeros
        cosine, sine = turns(first_row + lane)
        turned = result[:, heads * HD :].T
        low, high = turned[:half], turned[half:HD]
        keyvals = jnp.concatenate(
            [low * cosine - high * sine, high * cosine + low * sine, turned[HD:]], axis=0
        )
        suffix[tile, member] = keyvals.T.astype(jnp.bfloat16)
        for shift in range(1, members):
            suffix_copy(tile, shift, member).start()

    def relay(step):
        sources = ((0, z - step, z >= step), (1, z + step, z + step < n))
        for part in range(2):
            for side, slot, valid in sources:

                @pl.when(valid)
                def _(side=side, slot=slot, part=part):
                    hop_copy(side, slot, part).wait_recv()

                    @pl.when(onward[side])
                    def _():
                        hop_copy(side, slot, part).start()

        for side, slot, valid in sources:

            @pl.when(valid)
            def _(slot=slot):
                for shift in range(1, members):
                    core_copy(slot, shift, member).start()

    own_window.wait()

    def wait_deal(shift, carry):
        dealt(shift).wait_recv()
        return carry

    lax.fori_loop(1, tok_count, wait_deal, 0)
    for side in range(2):

        @pl.when(onward[side])
        def _(side=side):
            for part in range(2):
                hop_copy(side, z, part).start()

    for shift in range(1, members):
        core_copy(z, shift, member).start()

    for a, b in zip(range(chunks // 2), range(chunks // 2, chunks)):
        tile_copy(across, a, False, False).wait_recv()
        tile_copy(across, a, True, True).start()
        tile_copy(along, b, True, False).wait_recv()
        tile_copy(along, b, False, True).start()
    own_query.wait()
    own_keyval.wait()
    for shift in range(1, members):
        weight_copy(shift).wait_recv()
        project_copy(shift).start()
    project(mine)
    for a, b in zip(range(chunks // 2), range(chunks // 2, chunks)):
        tile_copy(across, b, False, False).wait_recv()
        tile_copy(along, a, True, False).wait_recv()
    relay(1)
    project(across)
    project(along)
    relay(2)
    for a, b in zip(range(chunks // 2), range(chunks // 2, chunks)):
        tile_copy(diagonal, a, True, True).wait_recv()
        tile_copy(diagonal, b, False, True).wait_recv()
    project(diagonal)
    for step in range(3, n):
        relay(step)

    for tile in range(kv_count):
        for shift in range(1, members):
            peer = lax.rem(member - shift + members, members)
            suffix_copy(tile, shift, peer).wait_recv()
    suffix_ref[...] = suffix[...]

    def settle(slot, carry):
        for shift in range(1, members):
            peer = lax.rem(member - shift + members, members)
            core_copy(slot, shift, peer).wait_recv()
            core_copy(slot, shift, member).wait_send()

        @pl.when(has_right & (slot <= z))
        def _():
            for part in range(2):
                hop_copy(0, slot, part).wait_send()

        @pl.when(has_left & (slot >= z))
        def _():
            for part in range(2):
                hop_copy(1, slot, part).wait_send()

        return carry

    lax.fori_loop(0, n, settle, 0)
    for c in range(chunks):
        tile_copy(mine, c, False, False).wait_send()
        tile_copy(mine, c, True, False).wait_send()
        if c < chunks // 2:
            tile_copy(across, c, True, True).wait_send()
        else:
            tile_copy(along, c, False, True).wait_send()
    for shift in range(1, members):
        weight_copy(shift).wait_send()
        project_copy(shift).wait()
    for tile in range(kv_count):
        for shift in range(1, members):
            suffix_copy(tile, shift, member).wait_send()

    def deal_sent(shift, carry):
        deal_copy(shift).wait_send()
        return carry

    lax.fori_loop(1, tok_count, deal_sent, 0)


def front(
    lengths,
    hidden,
    gain,
    query_weight,
    keyval_weight,
    prefix,
    out_weight,
    owner_count,
    kv_count,
    tok_count,
):
    rows, width = hidden.shape
    members = tok_count // kv_count
    columns = query_weight.shape[1]
    heads = members * columns // HD
    piece = prefix.shape[2]
    n, chunks = owner_count, 4
    cw = width // chunks
    bf16 = jnp.bfloat16
    dma = pltpu.SemaphoreType.DMA
    vmem = pl.BlockSpec(memory_space=pltpu.VMEM)
    hbm = pl.BlockSpec(memory_space=pltpu.HBM)
    return pl.pallas_call(
        lambda *refs: front_kernel(n, kv_count, tok_count, *refs),
        out_shape=[
            jax.ShapeDtypeStruct((kv_count * heads // 2, 2 * HD, 2 * rows), bf16),
            jax.ShapeDtypeStruct((kv_count, members, rows, 2 * HD), bf16),
            jax.ShapeDtypeStruct((n, tok_count, members, piece, 2 * HD), bf16),
            jax.ShapeDtypeStruct((members - 1,) + out_weight.shape, bf16),
        ],
        in_specs=[pl.BlockSpec(memory_space=pltpu.SMEM), vmem, vmem, hbm, hbm, hbm, hbm],
        out_specs=[vmem, vmem, hbm, hbm],
        scratch_shapes=[
            pltpu.VMEM((width, members * columns + 2 * HD), bf16),
            pltpu.VMEM((kv_count, chunks, rows, cw), bf16),
            pltpu.VMEM((kv_count, members, rows, 2 * HD), bf16),
            dma((3,)),
            dma((members,)),
            dma((members,)),
            dma((members,)),
            dma((members,)),
            dma((tok_count,)),
            dma((tok_count,)),
            dma((2, 2, chunks)),
            dma((kv_count, chunks)),
            dma((2, n, 2)),
            dma((n, 2)),
            dma((n, members)),
            dma((n, members)),
            dma((kv_count, members)),
            dma((kv_count, members)),
        ],
        compiler_params=pltpu.CompilerParams(
            collective_id=0, has_side_effects=True, vmem_limit_bytes=VMEM_LIMIT
        ),
        name="front",
    )(lengths, hidden, gain, query_weight, keyval_weight, prefix, out_weight)


def back_kernel(owner_count, kv_count, tok_count, parts, rows, vocab_step, *refs):
    lengths_ref, att_hbm, hid_hbm, own_hbm, others_hbm = refs[:5]
    (
        gain_ref,
        final_gain_ref,
        gate_hbm,
        up_hbm,
        down_hbm,
        head_hbm,
        out_ref,
        stat_ref,
        att_ref,
        hid_ref,
        outw,
        first_sem,
        w_in,
        w_down,
        w_head,
        part_send,
        part_recv,
        half_send,
        half_recv,
        total,
        tiles,
        acc,
        act,
        shares,
        from_left,
        from_right,
        picked,
        picked_all,
        logits,
        stats,
        stats_all,
        load_sem,
        part_ss,
        part_rs,
        half_ss,
        half_rs,
        tile_ss,
        tile_rs,
        share_ss,
        left_rs,
        right_rs,
        pick_ss,
        pick_rs,
        stat_ss,
        stat_rs,
    ) = refs[5:]
    n = owner_count
    width = hid_ref.shape[1]
    chunks = tiles.shape[1] // 2
    cw = width // chunks
    units = w_down.shape[0]
    tok = lax.axis_index("tok")
    z = lax.axis_index("req")
    members = tok_count // kv_count
    mine, member = tok // members, lax.rem(tok, members)
    across = mine + 1 - 2 * lax.rem(mine, 2)
    along = lax.rem(mine + 2, 4)
    diagonal = 3 - mine
    has_left, has_right = z > 0, z < n - 1
    left, right = lax.rem(z - 1 + n, n), lax.rem(z + 1, n)

    loads = [
        pltpu.make_async_copy(gate_hbm, w_in.at[:, :units], load_sem.at[0]),
        pltpu.make_async_copy(up_hbm, w_in.at[:, units:], load_sem.at[1]),
        pltpu.make_async_copy(down_hbm, w_down, load_sem.at[2]),
        pltpu.make_async_copy(head_hbm, w_head, load_sem.at[3]),
    ]
    early = [
        pltpu.make_async_copy(att_hbm, att_ref, first_sem.at[0]),
        pltpu.make_async_copy(own_hbm, outw.at[0], first_sem.at[1]),
        pltpu.make_async_copy(hid_hbm, hid_ref, first_sem.at[2]),
    ]
    for i in range(parts - 1):
        early.append(
            pltpu.make_async_copy(others_hbm.at[i], outw.at[i + 1], first_sem.at[3 + i])
        )
    for load in early:
        load.start()

    barrier = pltpu.get_barrier_semaphore()

    def greet(shift, carry):
        pl.semaphore_signal(
            barrier,
            inc=1,
            device_id={"tok": lax.rem(tok + shift, tok_count)},
            device_id_type=MESH,
        )
        return carry

    lax.fori_loop(1, tok_count, greet, 0)

    @pl.when(has_left)
    def _():
        pl.semaphore_signal(barrier, inc=1, device_id={"req": left}, device_id_type=MESH)

    @pl.when(has_right)
    def _():
        pl.semaphore_signal(barrier, inc=1, device_id={"req": right}, device_id_type=MESH)

    half = rows // 2
    pieces = 2 * chunks

    def product(tile, h, c):
        at = pl.ds(pl.multiple_of(tile * rows + h * half, half), half)
        depth = att_ref.shape[1] // parts
        result = None
        for i in range(parts):
            term = jnp.dot(
                att_ref[at, i * depth : (i + 1) * depth],
                outw[i, :, c * cw : (c + 1) * cw],
                preferred_element_type=jnp.float32,
            )
            result = term if result is None else result + term
        return result

    def part_copy(kind, h, c):
        peer = across if c < chunks // 2 else along
        j = h * chunks + c
        return pltpu.make_async_remote_copy(
            src_ref=part_send.at[kind, j],
            dst_ref=part_recv.at[kind, j],
            send_sem=part_ss.at[kind, j],
            recv_sem=part_rs.at[kind, j],
            device_id={"tok": peer * members + member},
            device_id_type=MESH,
        )

    def half_copy(h, c):
        peer = along if c < chunks // 2 else across
        j = h * chunks + c
        return pltpu.make_async_remote_copy(
            src_ref=half_send.at[j],
            dst_ref=half_recv.at[j],
            send_sem=half_ss.at[j],
            recv_sem=half_rs.at[j],
            device_id={"tok": peer * members + member},
            device_id_type=MESH,
        )

    order = [c for pair in zip(range(chunks // 2), range(chunks // 2, chunks)) for c in pair]

    def send_diagonal(h):
        for c in order:
            part_send[0, h * chunks + c] = product(diagonal, h, c).astype(jnp.bfloat16)
            if h > 0:
                part_copy(0, h, c).start()

    def send_near(h):
        for c in order:
            near = across if c < chunks // 2 else along
            part_send[1, h * chunks + c] = product(near, h, c).astype(jnp.bfloat16)
            part_copy(1, h, c).start()

    def send_far(h):
        for c in order:
            j = h * chunks + c
            far = along if c < chunks // 2 else across
            here = product(far, h, c)
            part_copy(0, h, c).wait_recv()
            half_send[j] = (here + part_recv[0, j].astype(jnp.float32)).astype(jnp.bfloat16)
            half_copy(h, c).start()

    def keep_own(h):
        at = slice(h * half, (h + 1) * half)
        for c in order:
            cols = slice(c * cw, (c + 1) * cw)
            total[at, cols] = hid_ref[at, cols].astype(jnp.float32) + product(mine, h, c)

    def tile_copy(side, tile, c):
        return pltpu.make_async_remote_copy(
            src_ref=tiles.at[tile, c],
            dst_ref=tiles.at[tile, c],
            send_sem=tile_ss.at[side, tile, c],
            recv_sem=tile_rs.at[tile, c],
            device_id={"req": right if side == 0 else left},
            device_id_type=MESH,
        )

    def share_copy(side, tile, c):
        return pltpu.make_async_remote_copy(
            src_ref=shares.at[tile, c],
            dst_ref=(from_left if side == 0 else from_right).at[tile, c],
            send_sem=share_ss.at[tile, c],
            recv_sem=(left_rs if side == 0 else right_rs).at[tile, c],
            device_id={"req": right if side == 0 else left},
            device_id_type=MESH,
        )

    onward = (has_right, has_left)

    def hand_on(h):
        at = slice(h * half, (h + 1) * half)
        squares = jnp.zeros((half, 1), jnp.float32)
        for c in order:
            j = h * chunks + c
            cols = slice(c * cw, (c + 1) * cw)
            part_copy(1, h, c).wait_recv()
            half_copy(h, c).wait_recv()
            summed = (
                total[at, cols]
                + part_recv[1, j].astype(jnp.float32)
                + half_recv[j].astype(jnp.float32)
            )
            middle = summed.astype(jnp.bfloat16).astype(jnp.float32)
            total[at, cols] = middle
            squares = squares + jnp.sum(middle * middle, axis=1, keepdims=True)
        scale = lax.rsqrt(squares / width + epsilon)
        for c in range(chunks):
            j = h * chunks + c
            cols = slice(c * cw, (c + 1) * cw)
            tiles[z, j] = (
                total[at, cols] * scale * gain_ref[cols].astype(jnp.float32).reshape(1, cw)
            ).astype(jnp.bfloat16)
            for side in range(2):

                @pl.when(onward[side])
                def _(side=side, j=j):
                    tile_copy(side, z, j).start()

    for load in early:
        load.wait()
    for load in loads:
        load.start()
    send_diagonal(0)
    pl.semaphore_wait(
        barrier, tok_count - 1 + has_left.astype(jnp.int32) + has_right.astype(jnp.int32)
    )
    for c in order:
        part_copy(0, 0, c).start()
    send_near(0)
    send_diagonal(1)
    send_far(0)
    send_near(1)
    keep_own(0)
    keep_own(1)
    hand_on(0)
    send_far(1)

    def pass_on(side, source, j):
        tile_copy(side, source, j).wait_recv()

        @pl.when(onward[side])
        def _():
            tile_copy(side, source, j).start()

    for j in range(chunks):
        for side, source, valid in ((0, left, has_left), (1, right, has_right)):

            @pl.when(valid)
            def _(side=side, source=source, j=j):
                pass_on(side, source, j)

    hand_on(1)
    for load in loads[:3]:
        load.wait()
    own_step = jnp.maximum(z, n - 1 - z) + 1

    def step(t, carry):
        s, h = t // 2, lax.rem(t, 2)
        own = s == own_step
        sources = (jnp.where(own, z, z - s), z + s)
        valid = (sources[0] >= 0, sources[1] < n)
        for c in range(chunks):
            j = h * chunks + c
            for side in range(2):

                @pl.when(valid[side] & jnp.logical_not(own) & (t > 2))
                def _(side=side, j=j):
                    pass_on(side, sources[side], j)

            for side in range(2):

                @pl.when(valid[side])
                def _(side=side, c=c, j=j):
                    term = jnp.dot(
                        tiles[sources[side], j],
                        w_in[c * cw : (c + 1) * cw, :],
                        preferred_element_type=jnp.float32,
                    )
                    if c == 0:
                        acc[side] = term
                    else:
                        acc[side] += term

        for side in range(2):

            @pl.when(valid[side])
            def _(side=side):
                gate_proj = acc[side, :, :units]
                lifted = acc[side, :, units:]
                act[...] = (gate_proj / (1.0 + jnp.exp(-gate_proj)) * lifted).astype(
                    jnp.bfloat16
                )
                starts_sum = jnp.logical_not(own) & jnp.logical_not(onward[side])
                for c in range(chunks):
                    j = h * chunks + c
                    shares[sources[side], j] = jnp.dot(
                        act[...],
                        w_down[:, c * cw : (c + 1) * cw],
                        preferred_element_type=jnp.float32,
                    ).astype(jnp.bfloat16)

                    @pl.when(starts_sum)
                    def _(j=j):
                        share_copy(1 - side, sources[side], j).start()

        begun = (t - z, t - (n - 1 - z))
        targets = (begun[0] // 2, n - 1 - begun[1] // 2)
        coming = (
            has_left & (begun[0] >= 0) & (targets[0] > z) & (targets[0] < n),
            has_right & (begun[1] >= 0) & (targets[1] < z) & (targets[1] >= 0),
        )
        for side in range(2):

            @pl.when(coming[side])
            def _(side=side):
                target = targets[side]
                arrived = from_left if side == 0 else from_right
                for c in range(chunks):
                    j = lax.rem(begun[side], 2) * chunks + c
                    share_copy(side, target, j).wait_recv()
                    shares[target, j] = (
                        shares[target, j].astype(jnp.float32)
                        + arrived[target, j].astype(jnp.float32)
                    ).astype(jnp.bfloat16)
                    share_copy(side, target, j).start()

        return carry

    lax.fori_loop(2, max(2 * n + 2, 3 * n - 2), step, 0)

    sublane = lax.broadcasted_iota(jnp.int32, (8 * chunks, rows), 0)
    row = tok * rows + lax.broadcasted_iota(jnp.int32, (8 * chunks, rows), 1)
    picks = jnp.zeros((8 * chunks, rows), jnp.float32)
    for request, end in enumerate(request_ends(lengths_ref, lengths_ref.shape[1])):
        picks = jnp.where((lax.rem(sublane, 8) == request) & (row == end - 1), 1.0, picks)
    chosen = jnp.zeros((8 * chunks, cw), jnp.float32)
    for h in range(2):
        at = slice(h * half, (h + 1) * half)
        for c in range(chunks):
            cols = slice(c * cw, (c + 1) * cw)
            j = h * chunks + c
            total[at, cols] += shares[z, j].astype(jnp.float32)

            @pl.when(has_left)
            def _(at=at, cols=cols, j=j):
                share_copy(0, z, j).wait_recv()
                total[at, cols] += from_left[z, j].astype(jnp.float32)

            @pl.when(has_right)
            def _(at=at, cols=cols, j=j):
                share_copy(1, z, j).wait_recv()
                total[at, cols] += from_right[z, j].astype(jnp.float32)

    for c in range(chunks):
        cols = slice(c * cw, (c + 1) * cw)
        final = total[:, cols].astype(jnp.bfloat16)
        out_ref[:, cols] = final
        picker = jnp.where(sublane // 8 == c, picks, 0.0).astype(jnp.bfloat16)
        chosen = chosen + jnp.dot(picker, final, preferred_element_type=jnp.float32)
    picked[...] = chosen.astype(jnp.bfloat16)

    def spread(source, target, ss, rs):
        def peer_copy(shift):
            return pltpu.make_async_remote_copy(
                src_ref=source,
                dst_ref=target.at[tok],
                send_sem=ss.at[shift],
                recv_sem=rs.at[shift],
                device_id={"tok": lax.rem(tok + shift, tok_count)},
                device_id_type=MESH,
            )

        def begin(shift, carry):
            peer_copy(shift).start()
            return carry

        def end(shift, carry):
            peer_copy(shift).wait()
            return carry

        lax.fori_loop(1, tok_count, begin, 0)
        target[tok] = source[...]
        lax.fori_loop(1, tok_count, end, 0)

    spread(picked, picked_all, pick_ss, pick_rs)
    gathered = picked_all[0].astype(jnp.float32)
    for i in range(1, tok_count):
        gathered = gathered + picked_all[i].astype(jnp.float32)
    last = jnp.concatenate([gathered[8 * c : 8 * c + 8] for c in range(chunks)], axis=1)
    mean_square = jnp.mean(last * last, axis=1, keepdims=True)
    diagonal_mask = lax.broadcasted_iota(jnp.int32, (8, 128), 0) == lax.broadcasted_iota(
        jnp.int32, (8, 128), 1
    )
    spread_row = jnp.sum(
        jnp.where(diagonal_mask, jnp.sqrt(mean_square + epsilon), 0.0), axis=0, keepdims=True
    )
    final_normed = (
        last * lax.rsqrt(mean_square + epsilon) * final_gain_ref[...].astype(jnp.float32).reshape(1, width)
    ).astype(jnp.bfloat16)
    final_normed = jnp.concatenate(
        [final_normed, jnp.zeros((128 - 8, width), jnp.bfloat16)], axis=0
    )
    loads[3].wait()

    def vocab(block, highest):
        at = pl.ds(pl.multiple_of(block * vocab_step, vocab_step), vocab_step)
        values = lax.dot_general(
            w_head[at, :],
            final_normed,
            (((1,), (1,)), ((), ())),
            preferred_element_type=jnp.float32,
        )
        logits[at, :] = values
        return jnp.maximum(highest, jnp.max(values, axis=0, keepdims=True))

    blocks = w_head.shape[0] // vocab_step
    top = lax.fori_loop(0, blocks, vocab, jnp.full((1, 128), -jnp.inf, jnp.float32))

    def exponents(block, amount):
        at = pl.ds(pl.multiple_of(block * vocab_step, vocab_step), vocab_step)
        return amount + jnp.sum(jnp.exp(logits[at, :] - top), axis=0, keepdims=True)

    amount = lax.fori_loop(0, blocks, exponents, jnp.zeros((1, 128), jnp.float32))
    stats[...] = jnp.concatenate([top, amount, jnp.zeros((6, 128), jnp.float32)], axis=0)
    spread(stats, stats_all, stat_ss, stat_rs)
    highest = stats_all[0, 0:1]
    for i in range(1, tok_count):
        highest = jnp.maximum(highest, stats_all[i, 0:1])
    amount = jnp.zeros((1, 128), jnp.float32)
    for i in range(tok_count):
        amount = amount + stats_all[i, 1:2] * jnp.exp(stats_all[i, 0:1] - highest)
    stat_ref[...] = jnp.concatenate(
        [spread_row, highest, highest + jnp.log(amount), jnp.zeros((5, 128), jnp.float32)], axis=0
    )

    for h in range(2):
        for c in order:
            part_copy(0, h, c).wait_send()
            part_copy(1, h, c).wait_send()
            half_copy(h, c).wait_send()

    def settle(tile, carry):
        for c in range(pieces):

            @pl.when(has_right & (tile <= z))
            def _(c=c):
                tile_copy(0, tile, c).wait_send()

            @pl.when(has_left & (tile >= z))
            def _(c=c):
                tile_copy(1, tile, c).wait_send()

            @pl.when(tile > z)
            def _(c=c):
                share_copy(0, tile, c).wait_send()

            @pl.when(tile < z)
            def _(c=c):
                share_copy(1, tile, c).wait_send()

        return carry

    lax.fori_loop(0, n, settle, 0)


def back(
    lengths,
    attended,
    hidden,
    out_weight,
    projects,
    mlp_gain,
    final_gain,
    gate_weight,
    up_weight,
    down_weight,
    head_weight,
    owner_count,
    kv_count,
    tok_count,
):
    rows, width = hidden.shape
    units = down_weight.shape[0]
    vocab_rows = head_weight.shape[0]
    vocab_step = max(b for b in range(16, 4097, 16) if vocab_rows % b == 0)
    n, chunks = owner_count, 4
    cw = width // chunks
    bf16, f32 = jnp.bfloat16, jnp.float32
    dma = pltpu.SemaphoreType.DMA
    vmem = pl.BlockSpec(memory_space=pltpu.VMEM)
    hbm = pl.BlockSpec(memory_space=pltpu.HBM)
    parts = tok_count // kv_count
    return pl.pallas_call(
        lambda *refs: back_kernel(n, kv_count, tok_count, parts, rows, vocab_step, *refs),
        out_shape=[
            jax.ShapeDtypeStruct((rows, width), bf16),
            jax.ShapeDtypeStruct((8, 128), f32),
        ],
        in_specs=[pl.BlockSpec(memory_space=pltpu.SMEM)] + [hbm] * 4 + [vmem] * 2 + [hbm] * 4,
        out_specs=[vmem] * 2,
        scratch_shapes=[
            pltpu.VMEM(attended.shape, bf16),
            pltpu.VMEM(hidden.shape, bf16),
            pltpu.VMEM((parts,) + out_weight.shape, bf16),
            dma((parts + 2,)),
            pltpu.VMEM((width, 2 * units), bf16),
            pltpu.VMEM((units, width), bf16),
            pltpu.VMEM((vocab_rows, width), bf16),
            pltpu.VMEM((2, 2 * chunks, rows // 2, cw), bf16),
            pltpu.VMEM((2, 2 * chunks, rows // 2, cw), bf16),
            pltpu.VMEM((2 * chunks, rows // 2, cw), bf16),
            pltpu.VMEM((2 * chunks, rows // 2, cw), bf16),
            pltpu.VMEM((rows, width), f32),
            pltpu.VMEM((n, 2 * chunks, rows // 2, cw), bf16),
            pltpu.VMEM((2, rows // 2, 2 * units), f32),
            pltpu.VMEM((rows // 2, units), bf16),
            pltpu.VMEM((n, 2 * chunks, rows // 2, cw), bf16),
            pltpu.VMEM((n, 2 * chunks, rows // 2, cw), bf16),
            pltpu.VMEM((n, 2 * chunks, rows // 2, cw), bf16),
            pltpu.VMEM((8 * chunks, cw), bf16),
            pltpu.VMEM((tok_count, 8 * chunks, cw), bf16),
            pltpu.VMEM((vocab_rows, 128), f32),
            pltpu.VMEM((8, 128), f32),
            pltpu.VMEM((tok_count, 8, 128), f32),
            dma((4,)),
            dma((2, 2 * chunks)),
            dma((2, 2 * chunks)),
            dma((2 * chunks,)),
            dma((2 * chunks,)),
            dma((2, n, 2 * chunks)),
            dma((n, 2 * chunks)),
            dma((n, 2 * chunks)),
            dma((n, 2 * chunks)),
            dma((n, 2 * chunks)),
            dma((tok_count,)),
            dma((tok_count,)),
            dma((tok_count,)),
            dma((tok_count,)),
        ],
        compiler_params=pltpu.CompilerParams(
            collective_id=1, has_side_effects=True, vmem_limit_bytes=VMEM_LIMIT
        ),
        name="back",
    )(
        lengths,
        attended,
        hidden,
        out_weight,
        projects,
        mlp_gain,
        final_gain,
        gate_weight,
        up_weight,
        down_weight,
        head_weight,
    )


def shards(
    hidden_in,
    suffix_len,
    prefix_of,
    prefix_slot,
    prefix_cache,
    attn_gain,
    query_weight,
    keyval_weight,
    out_weight,
    mlp_gain,
    gate_weight,
    up_weight,
    down_weight,
    final_gain,
    head_weight,
):
    tok_count = lax.axis_size("tok")
    owner_count = lax.axis_size("req")
    tok_rows = hidden_in.shape[0]
    own_rows = tok_rows * tok_count
    kv_count = keyval_weight.shape[0]
    members = tok_count // kv_count

    window_block = prefix_cache.shape[2]
    queries, suffix, windows, projects = front(
        suffix_len,
        hidden_in,
        attn_gain,
        query_weight,
        keyval_weight,
        prefix_cache.reshape(kv_count, members, window_block // members, 2 * HD),
        out_weight,
        owner_count,
        kv_count,
        tok_count,
    )
    attended, suffix_cache = attention(
        suffix_len,
        prefix_of,
        prefix_slot,
        queries,
        windows.reshape(owner_count, window_block * tok_count, 2 * HD),
        suffix.reshape(own_rows, 2 * HD),
        tok_rows,
        kv_count,
        tok_count,
    )
    request_count = suffix_len.shape[1]
    final_state, tail = back(
        suffix_len,
        attended,
        hidden_in,
        out_weight,
        projects,
        mlp_gain,
        final_gain,
        gate_weight,
        up_weight,
        down_weight,
        head_weight,
        owner_count,
        kv_count,
        tok_count,
    )
    return (
        final_state,
        suffix_cache.T,
        tail[0:1, :request_count],
        tail[1:2, :request_count],
        tail[2:3, :request_count],
    )


def solution(mesh):
    placed = (
        P(("req", "tok"), None),
        P("req", None),
        P("req", None),
        P(),
        P("req", None, "tok", None),
        P(),
        P(None, "tok"),
        P(),
        P("tok", None),
        P(),
        P(None, "req"),
        P(None, "req"),
        P("req", None),
        P(),
        P("tok", None),
    )
    return jax.shard_map(
        shards,
        mesh=mesh,
        in_specs=placed,
        out_specs=(
            P(("req", "tok"), None),
            P("req", "tok"),
            P("req", None),
            P("req", None),
            P("req", None),
        ),
        check_vma=False,
    )
```

```python
import math

import jax
import jax.numpy as jnp
from jax import lax
from jax.experimental import pallas as pl
from jax.experimental.pallas import tpu as pltpu
from jax.sharding import PartitionSpec as P

HD = 64
PRE_LEN = 16384
VMEM_LIMIT = 60 * 2**20


epsilon = 1e-05
neg_large = -1e30


def attention_kernel(
    most_rows,
    tok_count,
    kv_count,
    lengths_ref,
    chosen_ref,
    slot_ref,
    query_ref,
    windows,
    suffix_ref,
    out_ref,
    cache_ref,
    padded,
    band,
    band_values,
    score_scr,
):
    requests = lengths_ref.shape[1]
    units, unused, narrow = query_ref.shape
    units, lanes = units // 2, 2 * narrow
    rows = out_ref.shape[0] // kv_count
    unit_rows = out_ref.shape[0] // units
    per_tile = rows // unit_rows
    step_rows = unit_rows // 2
    pairs = narrow // 2 // step_rows
    window_len = windows.shape[1]
    own_rows = suffix_ref.shape[0]
    chunk = 256
    span = window_len + chunk
    tail_rows = band.shape[0] - window_len
    members = tok_count // kv_count
    tok = lax.axis_index("tok")
    member = lax.rem(tok, members)

    cache_width = cache_ref.shape[0]
    for first in range(0, own_rows, chunk):
        block = suffix_ref[first : first + chunk, :].astype(jnp.float32).T.astype(jnp.bfloat16)
        for place in range(2 * HD // cache_width):

            @pl.when(lax.rem(tok, 2 * HD // cache_width) == place)
            def _(place=place, first=first, block=block):
                cache_ref[:, first : first + chunk] = block[
                    place * cache_width : (place + 1) * cache_width
                ]

    padded[:own_rows, :] = suffix_ref[...]
    padded[own_rows:, :] = jnp.zeros((padded.shape[0] - own_rows, 2 * HD), jnp.bfloat16)

    def turned(block):
        return block.astype(jnp.float32).T[HD:].astype(jnp.bfloat16)

    def folded(values, fold):
        return fold(values.reshape(values.shape[0] // 8, 8, lanes), axis=0)

    def one_request(request, start):
        end = start + lengths_ref[0, request]
        slot = slot_ref[chosen_ref[0, request]]
        touched = jnp.int32(0)
        for tile in range(kv_count):
            first_row = (tile * members + member) * rows
            touched = touched + ((start < first_row + rows) & (end > first_row)).astype(jnp.int32)

        @pl.when(touched > 0)
        def _():
            for first in range(0, window_len, chunk):
                block = windows[slot, first : first + chunk, :]
                band[first : first + chunk, :] = block
                band_values[:, first : first + chunk] = turned(block)
            base = pl.multiple_of(start // 16 * 16, 16)
            lifted = padded[pl.ds(base, tail_rows + 16), :].astype(jnp.float32)
            lifted = pltpu.roll(lifted, tail_rows + 16 - (start - base), axis=0)
            for first in range(0, tail_rows, 128):
                block = lifted[first : first + 128].astype(jnp.bfloat16)
                at = slice(window_len + first, window_len + first + 128)
                band[at, :] = block
                band_values[:, at] = turned(block)

        def one_unit(unit, carry):
            tile = unit // per_tile
            first_row = (tile * members + member) * rows + lax.rem(unit, per_tile) * unit_rows

            @pl.when((start < first_row + unit_rows) & (end > first_row))
            def _():
                query = jnp.concatenate([query_ref[2 * unit], query_ref[2 * unit + 1]], axis=1)
                lane = lax.broadcasted_iota(jnp.int32, (1, lanes), 1)
                lane_row = first_row + lane // narrow * step_rows + lane % step_rows
                offset = lane_row - start
                low = pl.multiple_of((jnp.maximum(first_row, start) - start) // 128 * 128, 128)
                high = None
                for first in range(0, span, chunk):
                    scores = jnp.dot(
                        band[pl.ds(low + first, chunk), :],
                        query,
                        preferred_element_type=jnp.float32,
                    )
                    place = low + first + lax.broadcasted_iota(jnp.int32, (chunk, 1), 0)
                    if first == 0:
                        scores = jnp.where(place > offset, scores, neg_large)
                    if first == span - chunk:
                        scores = jnp.where(place <= offset + window_len, scores, neg_large)
                    score_scr[first : first + chunk, :] = scores
                    top = folded(scores, jnp.max)
                    high = top if high is None else jnp.maximum(high, top)
                high = jnp.max(high, axis=0, keepdims=True)
                total, acc = None, None
                for first in range(0, span, chunk):
                    weights = jnp.exp2(score_scr[first : first + chunk, :] - high)
                    part = folded(weights, jnp.sum)
                    term = jnp.dot(
                        band_values[:, pl.ds(low + first, chunk)],
                        weights.astype(jnp.bfloat16),
                        preferred_element_type=jnp.float32,
                    )
                    total = part if total is None else total + part
                    acc = term if acc is None else acc + term
                result = acc / jnp.sum(total, axis=0, keepdims=True)
                for odd in range(2):
                    part = result[:, odd * narrow : (odd + 1) * narrow]
                    both = jnp.concatenate(
                        [part[:, : narrow // 2], part[:, narrow // 2 :]], axis=0
                    )
                    flat = both.T
                    at = pl.ds(
                        pl.multiple_of(unit * unit_rows + odd * step_rows, step_rows), step_rows
                    )
                    row = (
                        first_row
                        + odd * step_rows
                        + lax.broadcasted_iota(jnp.int32, (step_rows, 1), 0)
                    )
                    mine = (row >= start) & (row < end)
                    for pair in range(pairs):
                        cols = slice(pair * 2 * HD, (pair + 1) * 2 * HD)
                        new = flat[pair * step_rows : (pair + 1) * step_rows]
                        old = out_ref[at, cols].astype(jnp.float32)
                        out_ref[at, cols] = jnp.where(mine, new, old).astype(jnp.bfloat16)

            return carry

        lax.fori_loop(0, units, one_unit, 0)
        return end

    lax.fori_loop(0, requests, one_request, 0)


def attention(lengths, chosen, prefix_slot, queries, windows, suffix, rows, kv_count, tok_count):
    units, unused, lanes = queries.shape
    heads = units * lanes // (kv_count * rows)
    own_rows = suffix.shape[0]
    window_len = windows.shape[1]
    cache_width = kv_count * 2 * HD // tok_count
    tail_rows = own_rows // 2 + 256
    smem = pl.BlockSpec(memory_space=pltpu.SMEM)
    vmem = pl.BlockSpec(memory_space=pltpu.VMEM)
    return pl.pallas_call(
        lambda *refs: attention_kernel(own_rows // 2, tok_count, kv_count, *refs),
        out_shape=[
            jax.ShapeDtypeStruct((kv_count * rows, heads * HD), jnp.bfloat16),
            jax.ShapeDtypeStruct((cache_width, own_rows), jnp.bfloat16),
        ],
        in_specs=[smem] * 3 + [vmem] * 3,
        out_specs=[vmem] * 2,
        scratch_shapes=[
            pltpu.VMEM((own_rows + tail_rows + 16, 2 * HD), jnp.bfloat16),
            pltpu.VMEM((window_len + tail_rows, 2 * HD), jnp.bfloat16),
            pltpu.VMEM((HD, window_len + tail_rows), jnp.bfloat16),
            pltpu.VMEM((window_len + 256, 2 * lanes), jnp.float32),
        ],
        compiler_params=pltpu.CompilerParams(vmem_limit_bytes=VMEM_LIMIT),
        cost_estimate=pl.CostEstimate(
            flops=10_000_000_000, bytes_accessed=8_000_000, transcendentals=10_000_000
        ),
        name="attention",
    )(lengths, chosen, prefix_slot, queries, windows, suffix)


MESH = pl.DeviceIdType.MESH


def request_ends(lengths_ref, count):
    ends, end = [], 0
    for request in range(count):
        end = end + lengths_ref[0, request]
        ends.append(end)
    return ends


def front_kernel(
    owner_count,
    kv_count,
    tok_count,
    lengths_ref,
    hid_ref,
    gain_ref,
    query_hbm,
    keyval_hbm,
    prefix_hbm,
    project_hbm,
    query_ref,
    suffix_ref,
    windows,
    projects,
    weights,
    tiles,
    suffix,
    local_sem,
    weight_ss,
    weight_rs,
    project_ss,
    project_rs,
    deal_ss,
    deal_rs,
    tile_ss,
    tile_rs,
    hop_ss,
    hop_rs,
    core_ss,
    core_rs,
    suffix_ss,
    suffix_rs,
):
    n = owner_count
    rows, width = hid_ref.shape
    chunks = tiles.shape[1]
    cw = width // chunks
    columns = query_hbm.shape[1]
    tok = lax.axis_index("tok")
    z = lax.axis_index("req")
    members = tok_count // kv_count
    mine, member = tok // members, lax.rem(tok, members)
    across = mine + 1 - 2 * lax.rem(mine, 2)
    along = lax.rem(mine + 2, 4)
    diagonal = 3 - mine
    has_left, has_right = z > 0, z < n - 1
    left, right = lax.rem(z - 1 + n, n), lax.rem(z + 1, n)
    onward = (has_right, has_left)
    half = HD // 2
    heads = members * columns // HD
    run = tok_count // 2

    own_query = pltpu.make_async_copy(query_hbm, weights.at[:, :columns], local_sem.at[0])
    own_keyval = pltpu.make_async_copy(
        keyval_hbm.at[mine], weights.at[:, members * columns :], local_sem.at[1]
    )
    own_window = pltpu.make_async_copy(
        prefix_hbm.at[mine, member], windows.at[z, tok, member], local_sem.at[2]
    )
    own_query.start()
    own_keyval.start()
    own_window.start()

    barrier = pltpu.get_barrier_semaphore()

    def greet(shift, carry):
        pl.semaphore_signal(
            barrier,
            inc=1,
            device_id={"tok": lax.rem(tok + shift, tok_count)},
            device_id_type=MESH,
        )
        return carry

    lax.fori_loop(1, tok_count, greet, 0)

    @pl.when(has_left)
    def _():
        pl.semaphore_signal(barrier, inc=1, device_id={"req": left}, device_id_type=MESH)

    @pl.when(has_right)
    def _():
        pl.semaphore_signal(barrier, inc=1, device_id={"req": right}, device_id_type=MESH)

    squares = jnp.zeros((rows, 1), jnp.float32)
    for c in range(chunks):
        part = hid_ref[:, c * cw : (c + 1) * cw].astype(jnp.float32)
        squares = squares + jnp.sum(part * part, axis=1, keepdims=True)
    scale = lax.rsqrt(squares / width + epsilon)
    for c in range(chunks):
        cols = slice(c * cw, (c + 1) * cw)
        tiles[mine, c] = (
            hid_ref[:, cols].astype(jnp.float32)
            * scale
            * gain_ref[cols].astype(jnp.float32).reshape(1, cw)
        ).astype(jnp.bfloat16)

    def deal_copy(shift):
        peer = lax.rem(tok + shift, tok_count)
        peer_member = lax.rem(peer, members)
        return pltpu.make_async_remote_copy(
            src_ref=prefix_hbm.at[peer // members, peer_member],
            dst_ref=windows.at[z, tok, peer_member],
            send_sem=deal_ss.at[shift],
            recv_sem=deal_rs.at[shift],
            device_id={"tok": peer},
            device_id_type=MESH,
        )

    def dealt(shift):
        return pltpu.make_async_remote_copy(
            src_ref=prefix_hbm.at[0, 0],
            dst_ref=windows.at[z, lax.rem(tok - shift + tok_count, tok_count), member],
            send_sem=deal_ss.at[shift],
            recv_sem=deal_rs.at[shift],
            device_id={"tok": lax.rem(tok + shift, tok_count)},
            device_id_type=MESH,
        )

    def weight_copy(shift):
        peer = lax.rem(member - shift + members, members)
        return pltpu.make_async_remote_copy(
            src_ref=query_hbm,
            dst_ref=weights.at[:, shift * columns : (shift + 1) * columns],
            send_sem=weight_ss.at[shift],
            recv_sem=weight_rs.at[shift],
            device_id={"tok": mine * members + peer},
            device_id_type=MESH,
        )

    def project_copy(shift):
        peer = lax.rem(member - shift + members, members)
        return pltpu.make_async_remote_copy(
            src_ref=project_hbm,
            dst_ref=projects.at[shift - 1],
            send_sem=project_ss.at[shift],
            recv_sem=project_rs.at[shift],
            device_id={"tok": mine * members + peer},
            device_id_type=MESH,
        )

    def tile_copy(tile, c, to_along, relayed):
        return pltpu.make_async_remote_copy(
            src_ref=tiles.at[tile, c],
            dst_ref=tiles.at[tile, c],
            send_sem=tile_ss.at[int(to_along), int(relayed), c],
            recv_sem=tile_rs.at[tile, c],
            device_id={"tok": (along if to_along else across) * members + member},
            device_id_type=MESH,
        )

    def hop_copy(side, slot, part):
        return pltpu.make_async_remote_copy(
            src_ref=windows.at[slot, part * run : (part + 1) * run, member],
            dst_ref=windows.at[slot, part * run : (part + 1) * run, member],
            send_sem=hop_ss.at[side, slot, part],
            recv_sem=hop_rs.at[slot, part],
            device_id={"req": right if side == 0 else left},
            device_id_type=MESH,
        )

    def core_copy(slot, shift, place):
        return pltpu.make_async_remote_copy(
            src_ref=windows.at[slot, :, place],
            dst_ref=windows.at[slot, :, place],
            send_sem=core_ss.at[slot, shift],
            recv_sem=core_rs.at[slot, shift],
            device_id={"tok": mine * members + lax.rem(member + shift, members)},
            device_id_type=MESH,
        )

    def suffix_copy(tile, shift, place):
        return pltpu.make_async_remote_copy(
            src_ref=suffix.at[tile, place],
            dst_ref=suffix.at[tile, place],
            send_sem=suffix_ss.at[tile, shift],
            recv_sem=suffix_rs.at[tile, shift],
            device_id={"tok": mine * members + lax.rem(member + shift, members)},
            device_id_type=MESH,
        )

    pl.semaphore_wait(
        barrier, tok_count - 1 + has_left.astype(jnp.int32) + has_right.astype(jnp.int32)
    )

    def start_deal(shift, carry):
        deal_copy(shift).start()
        return carry

    lax.fori_loop(1, tok_count, start_deal, 0)
    order = [c for pair in zip(range(chunks // 2), range(chunks // 2, chunks)) for c in pair]
    for a, b in zip(range(chunks // 2), range(chunks // 2, chunks)):
        tile_copy(mine, a, False, False).start()
        tile_copy(mine, b, True, False).start()
    for a, b in zip(range(chunks // 2), range(chunks // 2, chunks)):
        tile_copy(mine, b, False, False).start()
        tile_copy(mine, a, True, False).start()
    for shift in range(1, members):
        weight_copy(shift).start()

    ends = request_ends(lengths_ref, lengths_ref.shape[1])

    def turns(row):
        start = jnp.zeros((1, rows), jnp.int32)
        for end in ends[:-1]:
            start = jnp.where(row >= end, end, start)
        positions = (row - start + PRE_LEN).astype(jnp.float32)
        level = lax.broadcasted_iota(jnp.int32, (half, 1), 0).astype(jnp.float32)
        angles = jnp.exp(level * (-2.0 * math.log(10000.0) / HD)) * positions
        return jnp.cos(angles), jnp.sin(angles)

    unit_rows = 2 * rows // heads
    per_tile = rows // unit_rows

    def project(tile):
        result = None
        for c in range(chunks):
            term = jnp.dot(
                tiles[tile, c],
                weights[c * cw : (c + 1) * cw, :],
                preferred_element_type=jnp.float32,
            )
            result = term if result is None else result + term
        first_row = (tile * members + member) * rows
        lane = lax.broadcasted_iota(jnp.int32, (1, rows), 1)
        zeros = jnp.zeros((HD, 2 * rows), jnp.bfloat16)
        for u in range(per_tile):
            cosine, sine = turns(first_row + u * unit_rows + lax.rem(lane, unit_rows))
            block = result[u * unit_rows : (u + 1) * unit_rows]
            turned = jnp.concatenate(
                [block[:, p * 2 * HD : (p + 1) * 2 * HD] for p in range(heads // 2)], axis=0
            ).T
            for odd in range(2):
                low = turned[odd * HD : odd * HD + half]
                high = turned[odd * HD + half : (odd + 1) * HD]
                both = jnp.concatenate(
                    [low * cosine - high * sine, high * cosine + low * sine], axis=0
                )
                query_ref[tile * per_tile + u, :HD, odd * rows : (odd + 1) * rows] = (
                    both * (HD**-0.5 * math.log2(math.e))
                ).astype(jnp.bfloat16)
            query_ref[tile * per_tile + u, HD:, :] = zeros
        cosine, sine = turns(first_row + lane)
        turned = result[:, heads * HD :].T
        low, high = turned[:half], turned[half:HD]
        keyvals = jnp.concatenate(
            [low * cosine - high * sine, high * cosine + low * sine, turned[HD:]], axis=0
        )
        suffix[tile, member] = keyvals.T.astype(jnp.bfloat16)
        for shift in range(1, members):
            suffix_copy(tile, shift, member).start()

    def relay(step):
        sources = ((0, z - step, z >= step), (1, z + step, z + step < n))
        for part in range(2):
            for side, slot, valid in sources:

                @pl.when(valid)
                def _(side=side, slot=slot, part=part):
                    hop_copy(side, slot, part).wait_recv()

                    @pl.when(onward[side])
                    def _():
                        hop_copy(side, slot, part).start()

        for side, slot, valid in sources:

            @pl.when(valid)
            def _(slot=slot):
                for shift in range(1, members):
                    core_copy(slot, shift, member).start()

    own_window.wait()

    def wait_deal(shift, carry):
        dealt(shift).wait_recv()
        return carry

    lax.fori_loop(1, tok_count, wait_deal, 0)
    for side in range(2):

        @pl.when(onward[side])
        def _(side=side):
            for part in range(2):
                hop_copy(side, z, part).start()

    for shift in range(1, members):
        core_copy(z, shift, member).start()

    for a, b in zip(range(chunks // 2), range(chunks // 2, chunks)):
        tile_copy(across, a, False, False).wait_recv()
        tile_copy(across, a, True, True).start()
        tile_copy(along, b, True, False).wait_recv()
        tile_copy(along, b, False, True).start()
    own_query.wait()
    own_keyval.wait()
    for shift in range(1, members):
        weight_copy(shift).wait_recv()
        project_copy(shift).start()
    project(mine)
    for a, b in zip(range(chunks // 2), range(chunks // 2, chunks)):
        tile_copy(across, b, False, False).wait_recv()
        tile_copy(along, a, True, False).wait_recv()
    relay(1)
    project(across)
    project(along)
    relay(2)
    for a, b in zip(range(chunks // 2), range(chunks // 2, chunks)):
        tile_copy(diagonal, a, True, True).wait_recv()
        tile_copy(diagonal, b, False, True).wait_recv()
    project(diagonal)
    for step in range(3, n):
        relay(step)

    for tile in range(kv_count):
        for shift in range(1, members):
            peer = lax.rem(member - shift + members, members)
            suffix_copy(tile, shift, peer).wait_recv()
    suffix_ref[...] = suffix[...]

    def settle(slot, carry):
        for shift in range(1, members):
            peer = lax.rem(member - shift + members, members)
            core_copy(slot, shift, peer).wait_recv()
            core_copy(slot, shift, member).wait_send()

        @pl.when(has_right & (slot <= z))
        def _():
            for part in range(2):
                hop_copy(0, slot, part).wait_send()

        @pl.when(has_left & (slot >= z))
        def _():
            for part in range(2):
                hop_copy(1, slot, part).wait_send()

        return carry

    lax.fori_loop(0, n, settle, 0)
    for c in range(chunks):
        tile_copy(mine, c, False, False).wait_send()
        tile_copy(mine, c, True, False).wait_send()
        if c < chunks // 2:
            tile_copy(across, c, True, True).wait_send()
        else:
            tile_copy(along, c, False, True).wait_send()
    for shift in range(1, members):
        weight_copy(shift).wait_send()
        project_copy(shift).wait()
    for tile in range(kv_count):
        for shift in range(1, members):
            suffix_copy(tile, shift, member).wait_send()

    def deal_sent(shift, carry):
        deal_copy(shift).wait_send()
        return carry

    lax.fori_loop(1, tok_count, deal_sent, 0)


def front(
    lengths,
    hidden,
    gain,
    query_weight,
    keyval_weight,
    prefix,
    out_weight,
    owner_count,
    kv_count,
    tok_count,
):
    rows, width = hidden.shape
    members = tok_count // kv_count
    columns = query_weight.shape[1]
    heads = members * columns // HD
    piece = prefix.shape[2]
    n, chunks = owner_count, 4
    cw = width // chunks
    bf16 = jnp.bfloat16
    dma = pltpu.SemaphoreType.DMA
    vmem = pl.BlockSpec(memory_space=pltpu.VMEM)
    hbm = pl.BlockSpec(memory_space=pltpu.HBM)
    return pl.pallas_call(
        lambda *refs: front_kernel(n, kv_count, tok_count, *refs),
        out_shape=[
            jax.ShapeDtypeStruct((kv_count * heads // 2, 2 * HD, 2 * rows), bf16),
            jax.ShapeDtypeStruct((kv_count, members, rows, 2 * HD), bf16),
            jax.ShapeDtypeStruct((n, tok_count, members, piece, 2 * HD), bf16),
            jax.ShapeDtypeStruct((members - 1,) + out_weight.shape, bf16),
        ],
        in_specs=[pl.BlockSpec(memory_space=pltpu.SMEM), vmem, vmem, hbm, hbm, hbm, hbm],
        out_specs=[vmem, vmem, hbm, hbm],
        scratch_shapes=[
            pltpu.VMEM((width, members * columns + 2 * HD), bf16),
            pltpu.VMEM((kv_count, chunks, rows, cw), bf16),
            pltpu.VMEM((kv_count, members, rows, 2 * HD), bf16),
            dma((3,)),
            dma((members,)),
            dma((members,)),
            dma((members,)),
            dma((members,)),
            dma((tok_count,)),
            dma((tok_count,)),
            dma((2, 2, chunks)),
            dma((kv_count, chunks)),
            dma((2, n, 2)),
            dma((n, 2)),
            dma((n, members)),
            dma((n, members)),
            dma((kv_count, members)),
            dma((kv_count, members)),
        ],
        compiler_params=pltpu.CompilerParams(
            collective_id=0, has_side_effects=True, vmem_limit_bytes=VMEM_LIMIT
        ),
        name="front",
    )(lengths, hidden, gain, query_weight, keyval_weight, prefix, out_weight)


def back_kernel(owner_count, kv_count, tok_count, parts, rows, vocab_step, *refs):
    lengths_ref, att_ref, hid_ref = refs[:3]
    outw = (refs[3],) + tuple(refs[4].at[i] for i in range(parts - 1))
    (
        gain_ref,
        final_gain_ref,
        gate_hbm,
        up_hbm,
        down_hbm,
        head_hbm,
        out_ref,
        stat_ref,
        w_in,
        w_down,
        w_head,
        part_send,
        part_recv,
        half_send,
        half_recv,
        total,
        tiles,
        acc,
        act,
        shares,
        from_left,
        from_right,
        picked,
        picked_all,
        logits,
        stats,
        stats_all,
        load_sem,
        part_ss,
        part_rs,
        half_ss,
        half_rs,
        tile_ss,
        tile_rs,
        share_ss,
        left_rs,
        right_rs,
        pick_ss,
        pick_rs,
        stat_ss,
        stat_rs,
    ) = refs[5:]
    n = owner_count
    width = hid_ref.shape[1]
    chunks = tiles.shape[1] // 2
    cw = width // chunks
    units = w_down.shape[0]
    tok = lax.axis_index("tok")
    z = lax.axis_index("req")
    members = tok_count // kv_count
    mine, member = tok // members, lax.rem(tok, members)
    across = mine + 1 - 2 * lax.rem(mine, 2)
    along = lax.rem(mine + 2, 4)
    diagonal = 3 - mine
    has_left, has_right = z > 0, z < n - 1
    left, right = lax.rem(z - 1 + n, n), lax.rem(z + 1, n)

    loads = [
        pltpu.make_async_copy(gate_hbm, w_in.at[:, :units], load_sem.at[0]),
        pltpu.make_async_copy(up_hbm, w_in.at[:, units:], load_sem.at[1]),
        pltpu.make_async_copy(down_hbm, w_down, load_sem.at[2]),
        pltpu.make_async_copy(head_hbm, w_head, load_sem.at[3]),
    ]
    for load in loads:
        load.start()

    barrier = pltpu.get_barrier_semaphore()

    def greet(shift, carry):
        pl.semaphore_signal(
            barrier,
            inc=1,
            device_id={"tok": lax.rem(tok + shift, tok_count)},
            device_id_type=MESH,
        )
        return carry

    lax.fori_loop(1, tok_count, greet, 0)

    @pl.when(has_left)
    def _():
        pl.semaphore_signal(barrier, inc=1, device_id={"req": left}, device_id_type=MESH)

    @pl.when(has_right)
    def _():
        pl.semaphore_signal(barrier, inc=1, device_id={"req": right}, device_id_type=MESH)

    half = rows // 2
    pieces = 2 * chunks

    def product(tile, h, c):
        at = pl.ds(pl.multiple_of(tile * rows + h * half, half), half)
        depth = att_ref.shape[1] // parts
        result = None
        for i in range(parts):
            term = jnp.dot(
                att_ref[at, i * depth : (i + 1) * depth],
                outw[i][:, c * cw : (c + 1) * cw],
                preferred_element_type=jnp.float32,
            )
            result = term if result is None else result + term
        return result

    def part_copy(kind, h, c):
        peer = across if c < chunks // 2 else along
        j = h * chunks + c
        return pltpu.make_async_remote_copy(
            src_ref=part_send.at[kind, j],
            dst_ref=part_recv.at[kind, j],
            send_sem=part_ss.at[kind, j],
            recv_sem=part_rs.at[kind, j],
            device_id={"tok": peer * members + member},
            device_id_type=MESH,
        )

    def half_copy(h, c):
        peer = along if c < chunks // 2 else across
        j = h * chunks + c
        return pltpu.make_async_remote_copy(
            src_ref=half_send.at[j],
            dst_ref=half_recv.at[j],
            send_sem=half_ss.at[j],
            recv_sem=half_rs.at[j],
            device_id={"tok": peer * members + member},
            device_id_type=MESH,
        )

    order = [c for pair in zip(range(chunks // 2), range(chunks // 2, chunks)) for c in pair]

    def send_diagonal(h):
        for c in order:
            part_send[0, h * chunks + c] = product(diagonal, h, c).astype(jnp.bfloat16)
            if h > 0:
                part_copy(0, h, c).start()

    def send_near(h):
        for c in order:
            near = across if c < chunks // 2 else along
            part_send[1, h * chunks + c] = product(near, h, c).astype(jnp.bfloat16)
            part_copy(1, h, c).start()

    def send_far(h):
        for c in order:
            j = h * chunks + c
            far = along if c < chunks // 2 else across
            here = product(far, h, c)
            part_copy(0, h, c).wait_recv()
            half_send[j] = (here + part_recv[0, j].astype(jnp.float32)).astype(jnp.bfloat16)
            half_copy(h, c).start()

    def keep_own(h):
        at = slice(h * half, (h + 1) * half)
        for c in order:
            cols = slice(c * cw, (c + 1) * cw)
            total[at, cols] = hid_ref[at, cols].astype(jnp.float32) + product(mine, h, c)

    def tile_copy(side, tile, c):
        return pltpu.make_async_remote_copy(
            src_ref=tiles.at[tile, c],
            dst_ref=tiles.at[tile, c],
            send_sem=tile_ss.at[side, tile, c],
            recv_sem=tile_rs.at[tile, c],
            device_id={"req": right if side == 0 else left},
            device_id_type=MESH,
        )

    def share_copy(side, tile, c):
        return pltpu.make_async_remote_copy(
            src_ref=shares.at[tile, c],
            dst_ref=(from_left if side == 0 else from_right).at[tile, c],
            send_sem=share_ss.at[tile, c],
            recv_sem=(left_rs if side == 0 else right_rs).at[tile, c],
            device_id={"req": right if side == 0 else left},
            device_id_type=MESH,
        )

    onward = (has_right, has_left)

    def hand_on(h):
        at = slice(h * half, (h + 1) * half)
        squares = jnp.zeros((half, 1), jnp.float32)
        for c in order:
            j = h * chunks + c
            cols = slice(c * cw, (c + 1) * cw)
            part_copy(1, h, c).wait_recv()
            half_copy(h, c).wait_recv()
            summed = (
                total[at, cols]
                + part_recv[1, j].astype(jnp.float32)
                + half_recv[j].astype(jnp.float32)
            )
            middle = summed.astype(jnp.bfloat16).astype(jnp.float32)
            total[at, cols] = middle
            squares = squares + jnp.sum(middle * middle, axis=1, keepdims=True)
        scale = lax.rsqrt(squares / width + epsilon)
        for c in range(chunks):
            j = h * chunks + c
            cols = slice(c * cw, (c + 1) * cw)
            tiles[z, j] = (
                total[at, cols] * scale * gain_ref[cols].astype(jnp.float32).reshape(1, cw)
            ).astype(jnp.bfloat16)
            for side in range(2):

                @pl.when(onward[side])
                def _(side=side, j=j):
                    tile_copy(side, z, j).start()

    send_diagonal(0)
    pl.semaphore_wait(
        barrier, tok_count - 1 + has_left.astype(jnp.int32) + has_right.astype(jnp.int32)
    )
    for c in order:
        part_copy(0, 0, c).start()
    send_near(0)
    send_diagonal(1)
    send_far(0)
    send_near(1)
    keep_own(0)
    hand_on(0)
    send_far(1)
    keep_own(1)

    def pass_on(side, source, j):
        tile_copy(side, source, j).wait_recv()

        @pl.when(onward[side])
        def _():
            tile_copy(side, source, j).start()

    for j in range(chunks):
        for side, source, valid in ((0, left, has_left), (1, right, has_right)):

            @pl.when(valid)
            def _(side=side, source=source, j=j):
                pass_on(side, source, j)

    hand_on(1)
    for load in loads[:3]:
        load.wait()
    own_step = jnp.maximum(z, n - 1 - z) + 1

    def step(t, carry):
        s, h = t // 2, lax.rem(t, 2)
        own = s == own_step
        sources = (jnp.where(own, z, z - s), z + s)
        valid = (sources[0] >= 0, sources[1] < n)
        for c in range(chunks):
            j = h * chunks + c
            for side in range(2):

                @pl.when(valid[side] & jnp.logical_not(own) & (t > 2))
                def _(side=side, j=j):
                    pass_on(side, sources[side], j)

            for side in range(2):

                @pl.when(valid[side])
                def _(side=side, c=c, j=j):
                    term = jnp.dot(
                        tiles[sources[side], j],
                        w_in[c * cw : (c + 1) * cw, :],
                        preferred_element_type=jnp.float32,
                    )
                    if c == 0:
                        acc[side] = term
                    else:
                        acc[side] += term

        for side in range(2):

            @pl.when(valid[side])
            def _(side=side):
                gate_proj = acc[side, :, :units]
                lifted = acc[side, :, units:]
                act[...] = (gate_proj / (1.0 + jnp.exp(-gate_proj)) * lifted).astype(
                    jnp.bfloat16
                )
                starts_sum = jnp.logical_not(own) & jnp.logical_not(onward[side])
                for c in range(chunks):
                    j = h * chunks + c
                    shares[sources[side], j] = jnp.dot(
                        act[...],
                        w_down[:, c * cw : (c + 1) * cw],
                        preferred_element_type=jnp.float32,
                    ).astype(jnp.bfloat16)

                    @pl.when(starts_sum)
                    def _(j=j):
                        share_copy(1 - side, sources[side], j).start()

        begun = (t - z, t - (n - 1 - z))
        targets = (begun[0] // 2, n - 1 - begun[1] // 2)
        coming = (
            has_left & (begun[0] >= 0) & (targets[0] > z) & (targets[0] < n),
            has_right & (begun[1] >= 0) & (targets[1] < z) & (targets[1] >= 0),
        )
        for side in range(2):

            @pl.when(coming[side])
            def _(side=side):
                target = targets[side]
                arrived = from_left if side == 0 else from_right
                for c in range(chunks):
                    j = lax.rem(begun[side], 2) * chunks + c
                    share_copy(side, target, j).wait_recv()
                    shares[target, j] = (
                        shares[target, j].astype(jnp.float32)
                        + arrived[target, j].astype(jnp.float32)
                    ).astype(jnp.bfloat16)
                    share_copy(side, target, j).start()

        return carry

    lax.fori_loop(2, max(2 * n + 2, 3 * n - 2), step, 0)

    sublane = lax.broadcasted_iota(jnp.int32, (8 * chunks, rows), 0)
    row = tok * rows + lax.broadcasted_iota(jnp.int32, (8 * chunks, rows), 1)
    picks = jnp.zeros((8 * chunks, rows), jnp.float32)
    for request, end in enumerate(request_ends(lengths_ref, lengths_ref.shape[1])):
        picks = jnp.where((lax.rem(sublane, 8) == request) & (row == end - 1), 1.0, picks)
    chosen = jnp.zeros((8 * chunks, cw), jnp.float32)
    for h in range(2):
        at = slice(h * half, (h + 1) * half)
        for c in range(chunks):
            cols = slice(c * cw, (c + 1) * cw)
            j = h * chunks + c
            total[at, cols] += shares[z, j].astype(jnp.float32)

            @pl.when(has_left)
            def _(at=at, cols=cols, j=j):
                share_copy(0, z, j).wait_recv()
                total[at, cols] += from_left[z, j].astype(jnp.float32)

            @pl.when(has_right)
            def _(at=at, cols=cols, j=j):
                share_copy(1, z, j).wait_recv()
                total[at, cols] += from_right[z, j].astype(jnp.float32)

    for c in range(chunks):
        cols = slice(c * cw, (c + 1) * cw)
        final = total[:, cols].astype(jnp.bfloat16)
        out_ref[:, cols] = final
        picker = jnp.where(sublane // 8 == c, picks, 0.0).astype(jnp.bfloat16)
        chosen = chosen + jnp.dot(picker, final, preferred_element_type=jnp.float32)
    picked[...] = chosen.astype(jnp.bfloat16)

    def spread(source, target, ss, rs):
        def peer_copy(shift):
            return pltpu.make_async_remote_copy(
                src_ref=source,
                dst_ref=target.at[tok],
                send_sem=ss.at[shift],
                recv_sem=rs.at[shift],
                device_id={"tok": lax.rem(tok + shift, tok_count)},
                device_id_type=MESH,
            )

        def begin(shift, carry):
            peer_copy(shift).start()
            return carry

        def end(shift, carry):
            peer_copy(shift).wait()
            return carry

        lax.fori_loop(1, tok_count, begin, 0)
        target[tok] = source[...]
        lax.fori_loop(1, tok_count, end, 0)

    spread(picked, picked_all, pick_ss, pick_rs)
    gathered = picked_all[0].astype(jnp.float32)
    for i in range(1, tok_count):
        gathered = gathered + picked_all[i].astype(jnp.float32)
    last = jnp.concatenate([gathered[8 * c : 8 * c + 8] for c in range(chunks)], axis=1)
    mean_square = jnp.mean(last * last, axis=1, keepdims=True)
    diagonal_mask = lax.broadcasted_iota(jnp.int32, (8, 128), 0) == lax.broadcasted_iota(
        jnp.int32, (8, 128), 1
    )
    spread_row = jnp.sum(
        jnp.where(diagonal_mask, jnp.sqrt(mean_square + epsilon), 0.0), axis=0, keepdims=True
    )
    final_normed = (
        last * lax.rsqrt(mean_square + epsilon) * final_gain_ref[...].astype(jnp.float32).reshape(1, width)
    ).astype(jnp.bfloat16)
    final_normed = jnp.concatenate(
        [final_normed, jnp.zeros((128 - 8, width), jnp.bfloat16)], axis=0
    )
    loads[3].wait()

    def vocab(block, highest):
        at = pl.ds(pl.multiple_of(block * vocab_step, vocab_step), vocab_step)
        values = lax.dot_general(
            w_head[at, :],
            final_normed,
            (((1,), (1,)), ((), ())),
            preferred_element_type=jnp.float32,
        )
        logits[at, :] = values
        return jnp.maximum(highest, jnp.max(values, axis=0, keepdims=True))

    blocks = w_head.shape[0] // vocab_step
    top = lax.fori_loop(0, blocks, vocab, jnp.full((1, 128), -jnp.inf, jnp.float32))

    def exponents(block, amount):
        at = pl.ds(pl.multiple_of(block * vocab_step, vocab_step), vocab_step)
        return amount + jnp.sum(jnp.exp(logits[at, :] - top), axis=0, keepdims=True)

    amount = lax.fori_loop(0, blocks, exponents, jnp.zeros((1, 128), jnp.float32))
    stats[...] = jnp.concatenate([top, amount, jnp.zeros((6, 128), jnp.float32)], axis=0)
    spread(stats, stats_all, stat_ss, stat_rs)
    highest = stats_all[0, 0:1]
    for i in range(1, tok_count):
        highest = jnp.maximum(highest, stats_all[i, 0:1])
    amount = jnp.zeros((1, 128), jnp.float32)
    for i in range(tok_count):
        amount = amount + stats_all[i, 1:2] * jnp.exp(stats_all[i, 0:1] - highest)
    stat_ref[...] = jnp.concatenate(
        [spread_row, highest, highest + jnp.log(amount), jnp.zeros((5, 128), jnp.float32)], axis=0
    )

    for h in range(2):
        for c in order:
            part_copy(0, h, c).wait_send()
            part_copy(1, h, c).wait_send()
            half_copy(h, c).wait_send()

    def settle(tile, carry):
        for c in range(pieces):

            @pl.when(has_right & (tile <= z))
            def _(c=c):
                tile_copy(0, tile, c).wait_send()

            @pl.when(has_left & (tile >= z))
            def _(c=c):
                tile_copy(1, tile, c).wait_send()

            @pl.when(tile > z)
            def _(c=c):
                share_copy(0, tile, c).wait_send()

            @pl.when(tile < z)
            def _(c=c):
                share_copy(1, tile, c).wait_send()

        return carry

    lax.fori_loop(0, n, settle, 0)


def back(
    lengths,
    attended,
    hidden,
    out_weight,
    projects,
    mlp_gain,
    final_gain,
    gate_weight,
    up_weight,
    down_weight,
    head_weight,
    owner_count,
    kv_count,
    tok_count,
):
    rows, width = hidden.shape
    units = down_weight.shape[0]
    vocab_rows = head_weight.shape[0]
    vocab_step = max(b for b in range(16, 2049, 16) if vocab_rows % b == 0)
    n, chunks = owner_count, 4
    cw = width // chunks
    bf16, f32 = jnp.bfloat16, jnp.float32
    dma = pltpu.SemaphoreType.DMA
    vmem = pl.BlockSpec(memory_space=pltpu.VMEM)
    hbm = pl.BlockSpec(memory_space=pltpu.HBM)
    parts = tok_count // kv_count
    return pl.pallas_call(
        lambda *refs: back_kernel(n, kv_count, tok_count, parts, rows, vocab_step, *refs),
        out_shape=[
            jax.ShapeDtypeStruct((rows, width), bf16),
            jax.ShapeDtypeStruct((8, 128), f32),
        ],
        in_specs=[pl.BlockSpec(memory_space=pltpu.SMEM)] + [vmem] * 6 + [hbm] * 4,
        out_specs=[vmem] * 2,
        scratch_shapes=[
            pltpu.VMEM((width, 2 * units), bf16),
            pltpu.VMEM((units, width), bf16),
            pltpu.VMEM((vocab_rows, width), bf16),
            pltpu.VMEM((2, 2 * chunks, rows // 2, cw), bf16),
            pltpu.VMEM((2, 2 * chunks, rows // 2, cw), bf16),
            pltpu.VMEM((2 * chunks, rows // 2, cw), bf16),
            pltpu.VMEM((2 * chunks, rows // 2, cw), bf16),
            pltpu.VMEM((rows, width), f32),
            pltpu.VMEM((n, 2 * chunks, rows // 2, cw), bf16),
            pltpu.VMEM((2, rows // 2, 2 * units), f32),
            pltpu.VMEM((rows // 2, units), bf16),
            pltpu.VMEM((n, 2 * chunks, rows // 2, cw), bf16),
            pltpu.VMEM((n, 2 * chunks, rows // 2, cw), bf16),
            pltpu.VMEM((n, 2 * chunks, rows // 2, cw), bf16),
            pltpu.VMEM((8 * chunks, cw), bf16),
            pltpu.VMEM((tok_count, 8 * chunks, cw), bf16),
            pltpu.VMEM((vocab_rows, 128), f32),
            pltpu.VMEM((8, 128), f32),
            pltpu.VMEM((tok_count, 8, 128), f32),
            dma((4,)),
            dma((2, 2 * chunks)),
            dma((2, 2 * chunks)),
            dma((2 * chunks,)),
            dma((2 * chunks,)),
            dma((2, n, 2 * chunks)),
            dma((n, 2 * chunks)),
            dma((n, 2 * chunks)),
            dma((n, 2 * chunks)),
            dma((n, 2 * chunks)),
            dma((tok_count,)),
            dma((tok_count,)),
            dma((tok_count,)),
            dma((tok_count,)),
        ],
        compiler_params=pltpu.CompilerParams(
            collective_id=1, has_side_effects=True, vmem_limit_bytes=VMEM_LIMIT
        ),
        name="back",
    )(
        lengths,
        attended,
        hidden,
        out_weight,
        projects,
        mlp_gain,
        final_gain,
        gate_weight,
        up_weight,
        down_weight,
        head_weight,
    )


def shards(
    hidden_in,
    suffix_len,
    prefix_of,
    prefix_slot,
    prefix_cache,
    attn_gain,
    query_weight,
    keyval_weight,
    out_weight,
    mlp_gain,
    gate_weight,
    up_weight,
    down_weight,
    final_gain,
    head_weight,
):
    tok_count = lax.axis_size("tok")
    owner_count = lax.axis_size("req")
    tok_rows = hidden_in.shape[0]
    own_rows = tok_rows * tok_count
    kv_count = keyval_weight.shape[0]
    members = tok_count // kv_count

    window_block = prefix_cache.shape[2]
    queries, suffix, windows, projects = front(
        suffix_len,
        hidden_in,
        attn_gain,
        query_weight,
        keyval_weight,
        prefix_cache.reshape(kv_count, members, window_block // members, 2 * HD),
        out_weight,
        owner_count,
        kv_count,
        tok_count,
    )
    attended, suffix_cache = attention(
        suffix_len,
        prefix_of,
        prefix_slot,
        queries,
        windows.reshape(owner_count, window_block * tok_count, 2 * HD),
        suffix.reshape(own_rows, 2 * HD),
        tok_rows,
        kv_count,
        tok_count,
    )
    request_count = suffix_len.shape[1]
    final_state, tail = back(
        suffix_len,
        attended,
        hidden_in,
        out_weight,
        projects,
        mlp_gain,
        final_gain,
        gate_weight,
        up_weight,
        down_weight,
        head_weight,
        owner_count,
        kv_count,
        tok_count,
    )
    return (
        final_state,
        suffix_cache.T,
        tail[0:1, :request_count],
        tail[1:2, :request_count],
        tail[2:3, :request_count],
    )


def solution(mesh):
    placed = (
        P(("req", "tok"), None),
        P("req", None),
        P("req", None),
        P(),
        P("req", None, "tok", None),
        P(),
        P(None, "tok"),
        P(),
        P("tok", None),
        P(),
        P(None, "req"),
        P(None, "req"),
        P("req", None),
        P(),
        P("tok", None),
    )
    return jax.shard_map(
        shards,
        mesh=mesh,
        in_specs=placed,
        out_specs=(
            P(("req", "tok"), None),
            P("req", "tok"),
            P("req", None),
            P("req", None),
            P("req", None),
        ),
        check_vma=False,
    )
```
